32 devices in a mesh: dp: 16 (over z, y, core), tensor: 2 (over x).
Axes of the slice: x: 2, y: 2, z: 4, core: 2. Of those that a mesh axis runs over, the one named last changes fastest.
Arguments:
- inputs: bfloat16 [32, 1024, 768], P('dp'), may hold values from -6 to 6
- qkv_weight: bfloat16 [768, 3, 768], P('dp', None, 'tensor'), may hold values from -0.3125 to 0.3125
- out_weight: bfloat16 [768, 768], P('dp', 'tensor'), may hold values from -0.875 to 0.875
- norm_gains: bfloat16 [2, 768], P(None, 'dp'), may hold values from 0.25 to 1.75
- norm_shifts: bfloat16 [2, 768], P(None, 'dp'), may hold values from -1 to 1
- expert_in: bfloat16 [16, 768, 3072], P('dp', None, 'tensor'), may hold values from -0.21875 to 0.21875
- expert_out: bfloat16 [16, 3072, 768], P('dp', 'tensor'), may hold values from -0.15625 to 0.15625
- token_ids: int32 [32, 1024], P('dp'), may hold values from 0 to 51199, as said below
- hash_table: int32 [51200], replicated, may hold values from 0 to 15, as said below
- segment_ids: int32 [32, 1024], P('dp'), may hold values from 0 to 3, never falling along the last dimension, each value on 1 to 800 neighbouring positions
- cotangent: bfloat16 [32, 1024, 768], P('dp'), may hold values from -6 to 6
Outputs:
- output: bfloat16 [32, 1024, 768], P('dp')
- grad_inputs: bfloat16 [32, 1024, 768], P('dp')
- grad_qkv_weight: float32 [768, 3, 768], P('dp', None, 'tensor')
- grad_out_weight: float32 [768, 768], P('dp', 'tensor')
- grad_norm_gains: float32 [2, 768], P(None, 'dp')
- grad_norm_shifts: float32 [2, 768], P(None, 'dp')
- grad_expert_in: float32 [16, 768, 3072], P('dp', None, 'tensor')
- grad_expert_out: float32 [16, 3072, 768], P('dp', 'tensor')
The draws below stay inside these ranges and needn't reach their ends.
Inputs may be any that keep to these rules, and one draw needn't show every extreme that they name: `token_ids`: in every sequence at most 128 tokens map to one expert through hash_table, and one expert gets exactly 128; sequences with the same index among one dp index's 2 have the same such expert. `hash_table`: each expert is named by exactly 3200 entries.
All inputs are finite; a program needn't handle non-finite values.
Results may differ from the reference program's by a relative error of at most 0.017.
Values may be sent and summed in bfloat16 or wider, within the bound.
No kernel may reach another device: no remote copies, remote signals or barrier semaphores. Data moves between devices by JAX's collectives and lax.ppermute only.
A program may use at most 384 MiB of HBM per device.

```python
import math
import jax
import jax.numpy as jnp
import numpy as np
from jax import lax

D = 768
HEADS = 12
HEAD_DIM = 64
FF = 3072
VOCAB = 51200
SEQ_LEN = 1024
MICRO = 2
EXPERTS = 16
CAP = 128
SEQS = 32


def expert_order(key):
    return jax.random.permutation(jax.random.fold_in(key, 101), EXPERTS)


def sequence_choices(key):
    favoured = jax.random.permutation(jax.random.fold_in(key, 202), EXPERTS)

    def one_sequence(seq_row):
        row_key = jax.random.fold_in(jax.random.fold_in(key, 303), seq_row)
        full_expert = favoured[seq_row % MICRO % EXPERTS]
        others = jax.random.permutation(row_key, (EXPERTS - 1) * CAP)[:SEQ_LEN - CAP]
        other_experts = ((full_expert + 1 + others // CAP) % EXPERTS).astype(jnp.int32)
        joined = jnp.concatenate([jnp.zeros((CAP,), jnp.int32) + full_expert, other_experts])
        shuffle_order = jax.random.permutation(jax.random.fold_in(row_key, 7), SEQ_LEN)
        return joined[shuffle_order]
    return jax.vmap(one_sequence)(jnp.arange(SEQS, dtype=jnp.int32))


def draw_token_ids(key, part):
    chosen = sequence_choices(key)
    inverse = jnp.argsort(expert_order(key)).astype(jnp.int32)
    offsets = jax.random.randint(jax.random.fold_in(key, 404), (SEQS, SEQ_LEN), 0, VOCAB // EXPERTS)
    return (inverse[chosen] + EXPERTS * offsets).astype(jnp.int32)


def draw_hash_table(key, part):
    plan_order = expert_order(key).astype(jnp.int32)
    return plan_order[jnp.arange(VOCAB, dtype=jnp.int32) % EXPERTS]


def steps_of(key, dims, shards, least, largest):
    def one(position, blocks):
        draws = jax.random.uniform(jax.random.fold_in(jax.random.fold_in(key, 6), position), (blocks,), jnp.float32, least / len(shards), largest / len(shards))
        return jnp.repeat(jnp.exp(draws), dims[position] // blocks).reshape((-1,) + (1,) * (len(dims) - position - 1))

    gain = one(*shards[0])
    for cut in shards[1:]:
        gain = gain * one(*cut)
    return gain


def split_up(number_of, total, limit, lean):
    loads = [(1 << 20) // math.isqrt(grade ** lean) + 1 for grade in range(2, number_of + 1)]
    spare, given = total - limit - (number_of - 1), [1] * (number_of - 1)
    while spare > 0:
        candidates = [i for i in range(number_of - 1) if given[i] < limit]
        pool, budget = sum([loads[i] for i in candidates]), spare
        for i in candidates:
            addition = min(limit - given[i], max(1, budget * loads[i] // pool), spare)
            given[i] = given[i] + addition
            spare = spare - addition
    return np.array([limit] + given)


def uneven_parts(stream_key, amount, total, limit, lean):
    if amount == 2:
        one = jax.random.randint(stream_key, (), max(1, total - limit), min(limit, total - 1) + 1)
        return jnp.stack([one, total - one])
    tallies = jnp.asarray(split_up(amount, total, limit, lean), jnp.int32)
    pairs = (amount - 1) // 2
    giver, taker = tallies[1:1 + 2 * pairs:2], tallies[2:2 + 2 * pairs:2]
    margin = jnp.minimum(giver - 1, limit - taker)
    passed = jax.random.randint(jax.random.fold_in(stream_key, 1), (pairs,), 0, 1 << 20) % (margin + 1)
    tallies = tallies.at[1:1 + 2 * pairs:2].set(giver - passed).at[2:2 + 2 * pairs:2].set(taker + passed)
    return tallies[jax.random.permutation(jax.random.fold_in(stream_key, 2), amount)]


def bell_draw(rng, dims, spread, reach, cuts=(), kind=jnp.bfloat16):
    values = spread * jax.random.normal(rng, dims, jnp.float32)
    if cuts:
        values = values * steps_of(rng, dims, cuts, -0.22, 0.18)
    return jnp.clip(values, -reach, reach).astype(kind)


def setup_inputs(seed: int = 0) -> dict:
    arg_keys = jax.random.split(jax.random.key(seed), 12)
    return {
        "inputs": bell_draw(arg_keys[0], (SEQS, SEQ_LEN, D), 1.0, 6.0, ((0, 16),)),
        "qkv_weight": bell_draw(arg_keys[1], (D, 3, D), (D // 2) ** -0.5, 0.3125, ((0, 16), (2, 2))),
        "out_weight": bell_draw(arg_keys[2], (D, D), (D // 16) ** -0.5, 0.875, ((0, 16), (1, 2))),
        "norm_gains": jnp.clip(1.0 + 0.15 * jax.random.normal(arg_keys[3], (2, D), jnp.float32), 0.25, 1.75).astype(jnp.bfloat16),
        "norm_shifts": bell_draw(arg_keys[4], (2, D), 0.2, 1.0, ((1, 16),)),
        "expert_in": bell_draw(arg_keys[5], (EXPERTS, D, FF), D ** -0.5, 0.21875, ((0, 16), (2, 2))),
        "expert_out": bell_draw(arg_keys[6], (EXPERTS, FF, D), (FF // 2) ** -0.5, 0.15625, ((0, 16), (1, 2))),
        "token_ids": draw_token_ids(jax.random.fold_in(arg_keys[11], 71), 0),
        "hash_table": draw_hash_table(jax.random.fold_in(arg_keys[11], 71), 0),
        "segment_ids": jax.vmap(lambda own: jnp.searchsorted(jnp.cumsum(uneven_parts(own, 4, SEQ_LEN, SEQ_LEN * 25 // 32, 1)), jnp.arange(SEQ_LEN), side="right"))(jax.random.split(arg_keys[9], SEQS)).reshape((SEQS, SEQ_LEN)).astype(jnp.int32),
        "cotangent": bell_draw(arg_keys[10], (SEQS, SEQ_LEN, D), 1.0, 6.0, ((0, 16),)),
    }


@jax.custom_vjp
def low(v):
    return lax.optimization_barrier(v.astype(jnp.bfloat16)).astype(jnp.float32)

@jax.custom_vjp
def low_back(v):
    return v

def low_keep(v):
    return (low(v), None)

def low_pass(kept, grad):
    return (grad,)

def back_keep(v):
    return (v, None)

def back_low(kept, grad):
    return (low(grad),)
low.defvjp(low_keep, low_pass)
low_back.defvjp(back_keep, back_low)

def layer_norm(values, gain_row, shift_row):
    centred = values - lax.optimization_barrier(jnp.mean(values, axis=-1, keepdims=True))
    variance = lax.optimization_barrier(jnp.mean(centred * centred, axis=-1, keepdims=True))
    return centred * lax.rsqrt(variance + 1e-05) * gain_row + shift_row

def attention_part(weights, inputs, segment):
    qkv_weight, out_weight, gains, shifts = weights
    highest = lax.Precision.HIGHEST
    length = inputs.shape[0]
    normed = low(layer_norm(inputs, gains[0], shifts[0]))
    packed = low(low_back(jnp.einsum('sd,dtc->stc', normed, qkv_weight, precision=highest)))
    query_heads = packed[:, 0].reshape(length, HEADS, HEAD_DIM)
    key_heads = packed[:, 1].reshape(length, HEADS, HEAD_DIM)
    value_heads = packed[:, 2].reshape(length, HEADS, HEAD_DIM)
    scores = low_back(jnp.einsum('qhd,khd->hqk', query_heads, key_heads, precision=highest)) * HEAD_DIM ** (-0.5)
    places = jnp.arange(length, dtype=jnp.int32)
    allowed = (places[None, :] <= places[:, None]) & (segment[None, :] == segment[:, None])
    scores = jnp.where(allowed[None], scores, -1e+30)
    row_highest = lax.optimization_barrier(jnp.max(scores, axis=-1, keepdims=True))
    exponent = jnp.exp(scores - row_highest)
    soft_weights = low(exponent / lax.optimization_barrier(jnp.sum(exponent, axis=-1, keepdims=True)))
    context = jnp.einsum('hqk,khd->qhd', soft_weights, value_heads, precision=highest).reshape(length, HEADS * HEAD_DIM)
    context = low(low_back(context))
    branch = low_back(jnp.dot(context, out_weight.T, precision=highest))
    return inputs + branch

def sequence_slots(chosen):
    numbers = jnp.arange(EXPERTS, dtype=jnp.int32)
    onehot = (chosen[:, None] == numbers[None, :]).astype(jnp.int32)
    ranking = (lax.optimization_barrier(jnp.sum(jnp.cumsum(onehot, axis=0) * onehot, axis=1)) - 1).astype(jnp.int32)
    return ranking

def reference(inputs, qkv_weight, out_weight, norm_gains, norm_shifts, expert_in, expert_out, token_ids, hash_table, segment_ids, cotangent):
    chosen_all = jnp.take(hash_table, token_ids, axis=0).astype(jnp.int32)
    ranking_all = jax.vmap(sequence_slots)(chosen_all).astype(jnp.int32)
    seq_numbers = jnp.arange(SEQS, dtype=jnp.int32)[:, None]
    expert_rows = SEQS * CAP
    global_slot = (chosen_all * expert_rows + seq_numbers * CAP + ranking_all).astype(jnp.int32).reshape(-1)
    token_count = SEQS * SEQ_LEN
    slot_table = jnp.full((EXPERTS * expert_rows,), token_count, jnp.int32)
    slot_table = slot_table.at[global_slot].set(jnp.arange(token_count, dtype=jnp.int32)).reshape(EXPERTS, expert_rows)
    weights = tuple((weight_array.astype(jnp.float32) for weight_array in (qkv_weight, out_weight, norm_gains, norm_shifts, expert_in, expert_out)))
    attention_saved = jax.checkpoint(attention_part)

    def forward(inputs_float, weights_float):
        attention_weights = weights_float[:4]
        gains, shifts = (weights_float[2], weights_float[3])

        def advance(scan_carry, pieces):
            return (scan_carry, attention_saved(attention_weights, pieces[0], pieces[1]))
        _, middles = lax.scan(advance, jnp.zeros((), jnp.float32), (inputs_float, segment_ids))
        normed_two = low(low_back(layer_norm(middles, gains[1], shifts[1])))
        flat = normed_two.reshape(token_count, normed_two.shape[2])
        padded = jnp.concatenate([flat, jnp.zeros((1, flat.shape[1]), flat.dtype)], axis=0)
        highest = lax.Precision.HIGHEST

        def one_expert(pieces):
            weight_in, weight_out, rows_index = pieces
            rows = padded[rows_index]
            before = low_back(jnp.dot(rows, weight_in, precision=highest))
            hidden = low(low_back(jax.nn.gelu(before, approximate=True)))
            return jnp.dot(hidden, weight_out, precision=highest)
        products = lax.map(jax.checkpoint(one_expert), (weights_float[4], weights_float[5], slot_table))
        routed = low(low_back(products.reshape(EXPERTS * expert_rows, flat.shape[1])[global_slot]))
        return middles + routed.reshape(middles.shape)
    result, pullback = jax.vjp(forward, inputs.astype(jnp.float32), weights)
    grad_in, grad_weights = pullback(cotangent.astype(jnp.float32))
    return (result.astype(jnp.bfloat16), grad_in.astype(jnp.bfloat16), grad_weights[0], grad_weights[1], grad_weights[2], grad_weights[3], grad_weights[4], grad_weights[5])
```

```python
import functools

import jax
import jax.numpy as jnp
from jax import lax
from jax.experimental import pallas as pl
from jax.experimental.pallas import tpu as pltpu
from jax.sharding import PartitionSpec as P

HEAD_DIM = 64
SEQ_LEN = 1024
WIDTH = 768
PAIR = 128
BLOCK = 256
CHUNKS = 2
EPSILON = 1e-05
MASKED = -1e30
SEGMENTS = 4
VMEM = 60 * 1024 * 1024

f32 = jnp.float32
bf16 = jnp.bfloat16


def dot(a, b):
    return jnp.dot(a, b, preferred_element_type=f32)


def dot_nt(a, b):
    return lax.dot_general(a, b, (((1,), (1,)), ((), ())), preferred_element_type=f32)


def dot_tn(a, b):
    return lax.dot_general(a, b, (((0,), (0,)), ((), ())), preferred_element_type=f32)


def iota(shape, dim):
    return lax.broadcasted_iota(jnp.int32, shape, dim)


def params(axes=1):
    return pltpu.CompilerParams(
        dimension_semantics=("arbitrary",) * axes, vmem_limit_bytes=VMEM
    )


def whole(shape):
    zeros = (0,) * len(shape)
    return pl.BlockSpec(shape, lambda *_: zeros)


def normalize(values):
    centred = values - jnp.mean(values, axis=-1, keepdims=True)
    variance = jnp.mean(centred * centred, axis=-1, keepdims=True)
    inverse = lax.rsqrt(variance + EPSILON)
    return centred * inverse, inverse


def norm_backward(upstream, scaled, inverse, gain):
    weighted = upstream * gain
    inner = jnp.mean(weighted * scaled, axis=-1, keepdims=True)
    centred = weighted - jnp.mean(weighted, axis=-1, keepdims=True)
    return inverse * (centred - scaled * inner)


def norm_rows(norm_ref):
    rows = norm_ref[...].astype(f32).T
    return rows[0:1], rows[1:2], rows[2:3], rows[3:4]


def dispatch(slot_row, values, out_refs):
    for chunk, out_ref in enumerate(out_refs):
        rows = out_ref.shape[0]
        for start in range(0, rows, BLOCK):
            base = chunk * rows + start
            pick = (iota((BLOCK, SEQ_LEN), 0) + base == slot_row).astype(f32).astype(bf16)
            out_ref[start : start + BLOCK] = dot(pick, values).astype(bf16)


def combine(slot_col, back_refs, start, size):
    total = None
    for chunk, back_ref in enumerate(back_refs):
        rows = back_ref.shape[0]
        pick = (iota((size, rows), 1) + chunk * rows == slot_col[start : start + size]).astype(f32)
        part = dot(pick.astype(bf16), back_ref[...])
        total = part if total is None else total + part
    return total


def slots_of(chosen, rank, experts, share):
    chunk = (rank >= share).astype(jnp.int32)
    return chunk * (experts * share - share) + chosen * share + rank


def route_kernel(experts, share, _, row_ref, col_ref, cot_ref, first_ref, second_ref, slot_row_ref, slot_col_ref):
    row = row_ref[...]
    hot = (iota((experts, SEQ_LEN), 0) == row).astype(f32)
    order = (iota((SEQ_LEN, SEQ_LEN), 0) <= iota((SEQ_LEN, SEQ_LEN), 1)).astype(f32).astype(bf16)
    seen = dot(hot.astype(bf16), order)
    rank = jnp.sum(seen * hot, axis=0, keepdims=True).astype(jnp.int32) - 1
    slot_row = slots_of(row, rank, experts, share)
    slot_row_ref[...] = slot_row
    col = col_ref[...]
    hot_col = (iota((SEQ_LEN, experts), 1) == col).astype(f32)
    seen_col = dot_tn(order, hot_col.astype(bf16))
    rank_col = jnp.sum(seen_col * hot_col, axis=1, keepdims=True).astype(jnp.int32) - 1
    slot_col_ref[...] = slots_of(col, rank_col, experts, share)
    dispatch(slot_row, cot_ref[0], (first_ref, second_ref))


def route(tensor_place, chosen, cotangent, experts, share):
    rows = experts * share
    one = lambda i, place: (place[0], 0, 0)
    return pl.pallas_call(
        functools.partial(route_kernel, experts, share),
        grid_spec=pltpu.PrefetchScalarGridSpec(
            num_scalar_prefetch=1,
            grid=(1,),
            in_specs=[
                whole((1, SEQ_LEN)),
                whole((SEQ_LEN, 1)),
                pl.BlockSpec((1, SEQ_LEN, WIDTH), one),
            ],
            out_specs=[
                whole((rows, WIDTH)),
                whole((rows, WIDTH)),
                whole((1, SEQ_LEN)),
                whole((SEQ_LEN, 1)),
            ],
        ),
        out_shape=[
            jax.ShapeDtypeStruct((rows, WIDTH), bf16),
            jax.ShapeDtypeStruct((rows, WIDTH), bf16),
            jax.ShapeDtypeStruct((1, SEQ_LEN), jnp.int32),
            jax.ShapeDtypeStruct((SEQ_LEN, 1), jnp.int32),
        ],
        compiler_params=params(),
        name="route",
    )(tensor_place, chosen.reshape(1, SEQ_LEN), chosen.reshape(SEQ_LEN, 1), cotangent)


def segment_terms(segment_col):
    lane = iota((SEQ_LEN, PAIR), 1)
    query = jnp.where((lane != segment_col) & (lane < SEGMENTS), MASKED, 0.0).astype(bf16)
    key = (lane == segment_col).astype(f32).astype(bf16)
    return query, key


def causal(block):
    return jnp.where(iota(block.shape, 0) <= iota(block.shape, 1), block, MASKED)


def forward_kernel(
    _,
    x_ref,
    weight_ref,
    norm_ref,
    segment_ref,
    slot_ref,
    packed_ref,
    context_ref,
    logsum_ref,
    normed_ref,
    middle_ref,
    first_ref,
    second_ref,
    branch,
    query_seg,
    key_seg,
    context_t,
):
    step = pl.program_id(0)

    @pl.when(step == 0)
    def _():
        gain, _, shift, _ = norm_rows(norm_ref)
        scaled, _ = normalize(x_ref[0].astype(f32))
        normed_ref[...] = (scaled * gain + shift).astype(bf16)
        branch[...] = x_ref[0].astype(f32)
        query_seg[...], key_seg[...] = segment_terms(segment_ref[...])

    mixed = dot(normed_ref[...], weight_ref[:, : 3 * PAIR])
    packed_ref[...] = mixed.astype(bf16)
    query = mixed[:, :PAIR].astype(bf16) * jnp.asarray(HEAD_DIM**-0.5, bf16)
    keys = jnp.concatenate([mixed[:, PAIR : 2 * PAIR].astype(bf16), key_seg[...]], axis=1)
    values_t = mixed[:, 2 * PAIR :].T.astype(bf16)
    lane = iota((SEQ_LEN, PAIR), 1)
    for head in range(2):
        low, high = head * HEAD_DIM, (head + 1) * HEAD_DIM
        own = jnp.where((lane >= low) & (lane < high), query, jnp.zeros_like(query))
        own = jnp.concatenate([own, query_seg[...]], axis=1)
        for start in range(0, SEQ_LEN, BLOCK):
            stop = start + BLOCK
            block = own[start:stop]
            near = causal(dot_nt(keys[start:stop], block))
            highest = jnp.max(near, axis=0, keepdims=True)
            if start:
                far = dot_nt(keys[:start], block)
                highest = jnp.maximum(highest, jnp.max(far, axis=0, keepdims=True))
            near = jnp.exp(near - highest)
            total = jnp.sum(near, axis=0, keepdims=True)
            result = dot(values_t[low:high, start:stop], near.astype(bf16))
            if start:
                far = jnp.exp(far - highest)
                total = total + jnp.sum(far, axis=0, keepdims=True)
                result = result + dot(values_t[low:high, :start], far.astype(bf16))
            context_t[low:high, start:stop] = result * (1.0 / total)
            logsum_ref[0, head : head + 1, start:stop] = highest + jnp.log(total)
    context = context_t[...].T.astype(bf16)
    context_ref[...] = context
    branch[...] += dot_nt(context, weight_ref[:, 3 * PAIR :])

    @pl.when(step == pl.num_programs(0) - 1)
    def _():
        _, gain, _, shift = norm_rows(norm_ref)
        middle = branch[...]
        middle_ref[...] = middle
        scaled, _ = normalize(middle)
        normed_two = (scaled * gain + shift).astype(bf16)
        dispatch(slot_ref[...], normed_two, (first_ref, second_ref))


def forward(tensor_place, inputs, weights, segment_col, slot_row, rows):
    pairs = WIDTH // PAIR
    one = lambda i, place: (place[0], 0, 0)
    return pl.pallas_call(
        forward_kernel,
        grid_spec=pltpu.PrefetchScalarGridSpec(
            num_scalar_prefetch=1,
            grid=(pairs,),
            in_specs=[
                pl.BlockSpec((1, SEQ_LEN, WIDTH), one),
                pl.BlockSpec((WIDTH, 4 * PAIR), lambda i, _: (0, i)),
                pl.BlockSpec((WIDTH, PAIR), lambda i, _: (0, 4 * pairs)),
                whole((SEQ_LEN, 1)),
                whole((1, SEQ_LEN)),
            ],
            out_specs=[
                pl.BlockSpec((SEQ_LEN, 3 * PAIR), lambda i, _: (0, i)),
                pl.BlockSpec((SEQ_LEN, PAIR), lambda i, _: (0, i)),
                pl.BlockSpec((1, 2, SEQ_LEN), lambda i, _: (i, 0, 0)),
                whole((SEQ_LEN, WIDTH)),
                whole((SEQ_LEN, WIDTH)),
                whole((rows, WIDTH)),
                whole((rows, WIDTH)),
            ],
            scratch_shapes=[
                pltpu.VMEM((SEQ_LEN, WIDTH), f32),
                pltpu.VMEM((SEQ_LEN, PAIR), bf16),
                pltpu.VMEM((SEQ_LEN, PAIR), bf16),
                pltpu.VMEM((PAIR, SEQ_LEN), f32),
            ],
        ),
        out_shape=[
            jax.ShapeDtypeStruct((SEQ_LEN, 3 * WIDTH), bf16),
            jax.ShapeDtypeStruct((SEQ_LEN, WIDTH), bf16),
            jax.ShapeDtypeStruct((pairs, 2, SEQ_LEN), f32),
            jax.ShapeDtypeStruct((SEQ_LEN, WIDTH), bf16),
            jax.ShapeDtypeStruct((SEQ_LEN, WIDTH), f32),
            jax.ShapeDtypeStruct((rows, WIDTH), bf16),
            jax.ShapeDtypeStruct((rows, WIDTH), bf16),
        ],
        compiler_params=params(),
        name="attention_forward",
    )(tensor_place, inputs, weights, weights, segment_col, slot_row)


def halves(step, own_ref, other_ref, own_steps):
    return jnp.where(step < own_steps, own_ref[...], other_ref[...])


def half_specs(shape, dim, own_steps):
    def at(block):
        return tuple(block if d == dim else 0 for d in range(len(shape)))

    return [
        pl.BlockSpec(shape, lambda i: at(jnp.minimum(i, own_steps - 1))),
        pl.BlockSpec(shape, lambda i: at(jnp.maximum(i - own_steps, 0))),
    ]


UNITS = 512


def grad_hidden_kernel(own_steps, grad_ref, own_ref, other_ref, out_ref):
    weight = halves(pl.program_id(0), own_ref, other_ref, own_steps)
    out_ref[...] = dot_nt(grad_ref[...], weight).astype(bf16)


def grad_hidden(arrived, out_own, out_other):
    rows = arrived.shape[0]
    own_steps = out_own.shape[0] // UNITS
    return pl.pallas_call(
        functools.partial(grad_hidden_kernel, own_steps),
        grid=(2 * own_steps,),
        in_specs=[whole((rows, WIDTH))] + half_specs((UNITS, WIDTH), 0, own_steps),
        out_specs=pl.BlockSpec((rows, UNITS), lambda i: (0, i)),
        out_shape=jax.ShapeDtypeStruct((rows, 2 * own_steps * UNITS), bf16),
        compiler_params=params(),
        name="grad_hidden",
    )(arrived, out_own, out_other)


def expert_kernel(own_steps, rows_ref, grad_ref, own_ref, other_ref, hidden_ref, pre_ref, back_ref, total):
    step = pl.program_id(0)
    weight = halves(step, own_ref, other_ref, own_steps)
    before = dot(rows_ref[...], weight)
    root = 0.7978845608028654
    cube = 0.044715
    square = before * before
    tanh = jnp.tanh(before * (root + (root * cube) * square))
    half_up = 0.5 + 0.5 * tanh
    hidden_ref[...] = (before * half_up).astype(bf16)
    slope = half_up + (0.5 * before) * (1.0 - tanh * tanh) * (root + (3.0 * root * cube) * square)
    grad_pre = (grad_ref[...].astype(f32) * slope).astype(bf16)
    pre_ref[...] = grad_pre
    part = dot_nt(grad_pre, weight)

    @pl.when(step == 0)
    def _():
        total[...] = part

    @pl.when(step > 0)
    def _():
        total[...] += part

    @pl.when(step == pl.num_programs(0) - 1)
    def _():
        back_ref[...] = total[...].astype(bf16)


def expert(arrived, grads, in_own, in_other):
    rows = arrived.shape[0]
    own_steps = in_own.shape[1] // UNITS
    wide = pl.BlockSpec((rows, UNITS), lambda i: (0, i))
    units = 2 * own_steps * UNITS
    return pl.pallas_call(
        functools.partial(expert_kernel, own_steps),
        grid=(2 * own_steps,),
        in_specs=[whole((rows, WIDTH)), wide] + half_specs((WIDTH, UNITS), 1, own_steps),
        out_specs=[wide, wide, whole((rows, WIDTH))],
        out_shape=[
            jax.ShapeDtypeStruct((rows, units), bf16),
            jax.ShapeDtypeStruct((rows, units), bf16),
            jax.ShapeDtypeStruct((rows, WIDTH), bf16),
        ],
        scratch_shapes=[pltpu.VMEM((rows, WIDTH), f32)],
        compiler_params=params(),
        name="expert",
    )(arrived, grads, in_own, in_other)


def expert_out_kernel(hidden_ref, own_ref, other_ref, out_ref):
    units = own_ref.shape[0]
    hidden = hidden_ref[...]
    total = dot(hidden[:, :units], own_ref[...]) + dot(hidden[:, units:], other_ref[...])
    out_ref[...] = total.astype(bf16)


def expert_result(hidden, out_own, out_other):
    rows, units = hidden.shape
    return pl.pallas_call(
        expert_out_kernel,
        grid=(rows // BLOCK,),
        in_specs=[
            pl.BlockSpec((BLOCK, units), lambda i: (i, 0)),
            whole(out_own.shape),
            whole(out_other.shape),
        ],
        out_specs=pl.BlockSpec((BLOCK, WIDTH), lambda i: (i, 0)),
        out_shape=jax.ShapeDtypeStruct((rows, WIDTH), bf16),
        compiler_params=params(),
        name="expert_result",
    )(hidden, out_own, out_other)


def expert_grads_kernel(count, *refs):
    arrived = refs[:count]
    grads = refs[count : 2 * count]
    hidden = refs[2 * count : 3 * count]
    pre = refs[3 * count : 4 * count]
    in_ref, out_ref, arrived_t = refs[4 * count :]
    rows = arrived[0].shape[0]

    @pl.when(pl.program_id(0) == 0)
    def _():
        for chunk in range(count):
            arrived_t[:, chunk * rows : (chunk + 1) * rows] = arrived[chunk][...].T

    total_in, total_out = None, None
    for chunk in range(count):
        part_in = dot(arrived_t[:, chunk * rows : (chunk + 1) * rows], pre[chunk][...])
        part_out = dot_tn(hidden[chunk][...], grads[chunk][...])
        total_in = part_in if total_in is None else total_in + part_in
        total_out = part_out if total_out is None else total_out + part_out
    in_ref[...] = total_in.astype(in_ref.dtype)
    out_ref[...] = total_out.astype(out_ref.dtype)


def expert_grads(arrived, grads, hidden, pre, half, dtype):
    count = len(arrived)
    rows = arrived[0].shape[0]
    steps = hidden[0].shape[1] // (2 * UNITS)
    wide = pl.BlockSpec((rows, UNITS), lambda i: (0, i + half * steps))
    full = whole((rows, WIDTH))
    return pl.pallas_call(
        functools.partial(expert_grads_kernel, count),
        grid=(steps,),
        in_specs=[full] * (2 * count) + [wide] * (2 * count),
        out_specs=[
            pl.BlockSpec((WIDTH, UNITS), lambda i: (0, i)),
            pl.BlockSpec((UNITS, WIDTH), lambda i: (i, 0)),
        ],
        out_shape=[
            jax.ShapeDtypeStruct((WIDTH, steps * UNITS), dtype),
            jax.ShapeDtypeStruct((steps * UNITS, WIDTH), dtype),
        ],
        scratch_shapes=[pltpu.VMEM((WIDTH, count * rows), bf16)],
        compiler_params=params(),
        name="expert_grads",
    )(*arrived, *grads, *hidden, *pre)


def backward_kernel(
    _,
    x_ref,
    cot_ref,
    middle_ref,
    first_ref,
    second_ref,
    slot_ref,
    segment_ref,
    normed_ref,
    norm_ref,
    weight_ref,
    packed_ref,
    context_ref,
    logsum_ref,
    grad_weight_ref,
    grad_norm_ref,
    grad_input_ref,
    grad_middle,
    grad_branch,
    grad_branch_t,
    normed_t,
    grad_normed,
    query_seg,
    key_seg,
    sums,
    grad_keys,
    grad_values,
    grad_queries_t,
):
    step = pl.program_id(0)

    @pl.when(step == 0)
    def _():
        _, gain, _, _ = norm_rows(norm_ref)
        query_seg[...], key_seg[...] = segment_terms(segment_ref[...])
        gain_sum = jnp.zeros((1, WIDTH), f32)
        shift_sum = jnp.zeros((1, WIDTH), f32)
        for start in range(0, SEQ_LEN, BLOCK):
            stop = start + BLOCK
            upstream = combine(slot_ref[...], (first_ref, second_ref), start, BLOCK)
            scaled, inverse = normalize(middle_ref[start:stop])
            result = cot_ref[0, start:stop].astype(f32) + norm_backward(upstream, scaled, inverse, gain)
            grad_middle[start:stop] = result
            grad_branch[start:stop] = result.astype(bf16)
            grad_branch_t[:, start:stop] = result.T.astype(bf16)
            normed_t[:, start:stop] = normed_ref[start:stop].T
            gain_sum += jnp.sum(upstream * scaled, axis=0, keepdims=True)
            shift_sum += jnp.sum(upstream, axis=0, keepdims=True)
        sums[1:2] = gain_sum
        sums[3:4] = shift_sum

    grad_context = dot(grad_branch[...], weight_ref[:, 3 * PAIR :]).astype(bf16)
    grad_weight_ref[:, 3 * PAIR :] = dot(grad_branch_t[...], context_ref[...]).astype(bf16)
    inner = (grad_context.astype(f32) * context_ref[...].astype(f32)).T
    query = packed_ref[:, :PAIR] * jnp.asarray(HEAD_DIM**-0.5, bf16)
    keys = packed_ref[:, PAIR : 2 * PAIR]
    keys_t = keys.T
    keys = jnp.concatenate([keys, key_seg[...]], axis=1)
    values = packed_ref[:, 2 * PAIR :]
    lane = iota((SEQ_LEN, PAIR), 1)
    grad_keys[...] = jnp.zeros_like(grad_keys)
    grad_values[...] = jnp.zeros_like(grad_values)
    for head in range(2):
        low, high = head * HEAD_DIM, (head + 1) * HEAD_DIM
        mine = (lane >= low) & (lane < high)
        own = jnp.where(mine, query, jnp.zeros_like(query))
        own_wide = jnp.concatenate([own, query_seg[...]], axis=1)
        upstream = jnp.where(mine, grad_context, jnp.zeros_like(grad_context))
        delta = jnp.sum(inner[low:high], axis=0, keepdims=True)
        for start in range(0, SEQ_LEN, BLOCK):
            stop = start + BLOCK
            logs = logsum_ref[0, head : head + 1, start:stop]
            ranges = [(start, stop)] + ([(0, start)] if start else [])
            grad_query = None
            for first, last in ranges:
                scores = dot_nt(keys[first:last], own_wide[start:stop])
                if first == start:
                    scores = causal(scores)
                probs = jnp.exp(scores - logs)
                grad_probs = dot_nt(values[first:last], upstream[start:stop])
                grad_scores = (probs * (grad_probs - delta[:, start:stop])).astype(bf16)
                grad_values[first:last] += dot(probs.astype(bf16), upstream[start:stop])
                grad_keys[first:last] += dot(grad_scores, own[start:stop])
                part = dot(keys_t[low:high, first:last], grad_scores)
                grad_query = part if grad_query is None else grad_query + part
            grad_queries_t[low:high, start:stop] = grad_query * (HEAD_DIM**-0.5)
    grad_packed = jnp.concatenate(
        [grad_queries_t[...].T.astype(bf16), grad_keys[...].astype(bf16), grad_values[...].astype(bf16)],
        axis=1,
    )
    grad_weight_ref[:, : 3 * PAIR] = dot(normed_t[...], grad_packed).astype(bf16)
    part = dot_nt(grad_packed, weight_ref[:, : 3 * PAIR])

    @pl.when(step == 0)
    def _():
        grad_normed[...] = part

    @pl.when(step > 0)
    def _():
        grad_normed[...] += part

    @pl.when(step == pl.num_programs(0) - 1)
    def _():
        gain, _, _, _ = norm_rows(norm_ref)
        upstream = grad_normed[...]
        scaled, inverse = normalize(x_ref[0].astype(f32))
        result = grad_middle[...] + norm_backward(upstream, scaled, inverse, gain)
        grad_input_ref[...] = result.astype(bf16)
        sums[0:1] = jnp.sum(upstream * scaled, axis=0, keepdims=True)
        sums[2:3] = jnp.sum(upstream, axis=0, keepdims=True)
        sums[4:8] = jnp.zeros((4, WIDTH), f32)
        tall = jnp.concatenate([sums[...], jnp.zeros((PAIR - 8, WIDTH), f32)], axis=0)
        grad_norm_ref[...] = tall.T.astype(bf16)


def backward(tensor_place, inputs, cotangent, middle, back, slot_col, segment_col, normed, weights, packed, context, logsums):
    pairs = WIDTH // PAIR
    rows = back[0].shape[0]
    one = lambda i, place: (place[0], 0, 0)
    once = dict(pipeline_mode=pl.Buffered(1))
    full = whole((SEQ_LEN, WIDTH))
    return pl.pallas_call(
        backward_kernel,
        grid_spec=pltpu.PrefetchScalarGridSpec(
            num_scalar_prefetch=1,
            grid=(pairs,),
            in_specs=[
                pl.BlockSpec((1, SEQ_LEN, WIDTH), one, **once),
                pl.BlockSpec((1, SEQ_LEN, WIDTH), one, **once),
                pl.BlockSpec((SEQ_LEN, WIDTH), lambda i, _: (0, 0), **once),
                pl.BlockSpec((rows, WIDTH), lambda i, _: (0, 0), **once),
                pl.BlockSpec((rows, WIDTH), lambda i, _: (0, 0), **once),
                whole((SEQ_LEN, 1)),
                whole((SEQ_LEN, 1)),
                pl.BlockSpec((SEQ_LEN, WIDTH), lambda i, _: (0, 0), **once),
                pl.BlockSpec((WIDTH, PAIR), lambda i, _: (0, 4 * pairs)),
                pl.BlockSpec((WIDTH, 4 * PAIR), lambda i, _: (0, i)),
                pl.BlockSpec((SEQ_LEN, 3 * PAIR), lambda i, _: (0, i)),
                pl.BlockSpec((SEQ_LEN, PAIR), lambda i, _: (0, i)),
                pl.BlockSpec((1, 2, SEQ_LEN), lambda i, _: (i, 0, 0)),
            ],
            out_specs=[
                pl.BlockSpec((WIDTH, 4 * PAIR), lambda i, _: (0, i)),
                whole((WIDTH, PAIR)),
                full,
            ],
            scratch_shapes=[
                pltpu.VMEM((SEQ_LEN, WIDTH), f32),
                pltpu.VMEM((SEQ_LEN, WIDTH), bf16),
                pltpu.VMEM((WIDTH, SEQ_LEN), bf16),
                pltpu.VMEM((WIDTH, SEQ_LEN), bf16),
                pltpu.VMEM((SEQ_LEN, WIDTH), f32),
                pltpu.VMEM((SEQ_LEN, PAIR), bf16),
                pltpu.VMEM((SEQ_LEN, PAIR), bf16),
                pltpu.VMEM((8, WIDTH), f32),
                pltpu.VMEM((SEQ_LEN, PAIR), f32),
                pltpu.VMEM((SEQ_LEN, PAIR), f32),
                pltpu.VMEM((PAIR, SEQ_LEN), f32),
            ],
        ),
        out_shape=[
            jax.ShapeDtypeStruct((WIDTH, 4 * WIDTH), bf16),
            jax.ShapeDtypeStruct((WIDTH, PAIR), bf16),
            jax.ShapeDtypeStruct((SEQ_LEN, WIDTH), bf16),
        ],
        compiler_params=params(),
        name="attention_backward",
    )(
        tensor_place,
        inputs,
        cotangent,
        middle,
        *back,
        slot_col,
        segment_col,
        normed,
        weights,
        weights,
        packed,
        context,
        logsums,
    )


def result_kernel(middle_ref, slot_ref, first_ref, second_ref, out_ref):
    routed = combine(slot_ref[...], (first_ref, second_ref), 0, BLOCK)
    out_ref[...] = (middle_ref[...] + routed).astype(bf16)


def result(middle, slot_col, back):
    rows = back[0].shape[0]
    tile = pl.BlockSpec((BLOCK, WIDTH), lambda i: (i, 0))
    return pl.pallas_call(
        result_kernel,
        grid=(SEQ_LEN // BLOCK,),
        in_specs=[
            tile,
            pl.BlockSpec((BLOCK, 1), lambda i: (i, 0)),
            whole((rows, WIDTH)),
            whole((rows, WIDTH)),
        ],
        out_specs=tile,
        out_shape=jax.ShapeDtypeStruct((SEQ_LEN, WIDTH), bf16),
        compiler_params=params(),
        name="result",
    )(middle, slot_col, *back)


def swap(values):
    return lax.ppermute(values, "tensor", [(0, 1), (1, 0)])


def exchange(values, experts):
    shape = values.shape
    parts = values.reshape(experts, shape[0] // experts, shape[1])
    return lax.all_to_all(parts, "dp", split_axis=0, concat_axis=0, tiled=True).reshape(shape)


def both(place, values):
    other = swap(values)
    first = place == 0
    return jnp.stack([jnp.where(first, values, other), jnp.where(first, other, values)])


def body(
    inputs,
    qkv_weight,
    out_weight,
    norm_gains,
    norm_shifts,
    expert_in,
    expert_out,
    token_ids,
    hash_table,
    segment_ids,
    cotangent,
):
    place = lax.axis_index("tensor")
    places = place.astype(jnp.int32).reshape(1)
    experts = lax.axis_size("dp")
    share = 2 * SEQ_LEN // experts // CHUNKS
    rows = experts * share
    depth = qkv_weight.shape[0]
    half = qkv_weight.shape[2]
    pairs = half // PAIR

    own = jnp.concatenate(
        [
            qkv_weight.reshape(depth, 3, pairs, PAIR).transpose(0, 2, 1, 3),
            out_weight.reshape(depth, pairs, 1, PAIR),
        ],
        axis=2,
    ).reshape(depth, 4 * half)
    norms = jnp.concatenate([norm_gains, norm_shifts], axis=0).T
    norms = jnp.pad(norms, ((0, 0), (0, PAIR - norms.shape[1])))
    shard = jnp.concatenate([own, swap(own), norms], axis=1)
    weights = lax.all_gather(shard, "dp", axis=0, tiled=True)

    in_own, out_own = expert_in[0], expert_out[0]
    out_other = swap(out_own)
    in_other = swap(in_own)

    ids = lax.dynamic_index_in_dim(token_ids, place, 0, keepdims=False)
    chosen = jnp.take(hash_table, ids, axis=0)
    segment_col = lax.dynamic_index_in_dim(segment_ids, place, 0, keepdims=False).reshape(SEQ_LEN, 1)
    grad_first, grad_second, slot_row, slot_col = route(places, chosen, cotangent, experts, share)
    grads = [exchange(grad_first, experts), exchange(grad_second, experts)]

    packed, context, logsums, normed, middle, first, second = forward(
        places, inputs, weights, segment_col, slot_row, rows
    )
    arrived = [exchange(first, experts), exchange(second, experts)]
    upstream = [grad_hidden(g, out_own, out_other) for g in grads]
    done = [expert(a, u, in_own, in_other) for a, u in zip(arrived, upstream)]
    hidden = [d[0] for d in done]
    pre = [d[1] for d in done]
    back = [exchange(d[2], experts) for d in done]

    in_send, out_send = expert_grads(arrived, grads, hidden, pre, 1, bf16)
    in_keep, out_keep = expert_grads(arrived, grads, hidden, pre, 0, f32)
    grad_expert_out = out_keep + swap(out_send).astype(f32)
    grad_expert_in = in_keep + swap(in_send).astype(f32)
    routed = [exchange(expert_result(h, out_own, out_other), experts) for h in hidden]

    grad_weights, grad_norms, grad_own = backward(
        places, inputs, cotangent, middle, back, slot_col, segment_col, normed, weights, packed, context, logsums
    )
    kept = jnp.concatenate([grad_weights[:, : 4 * half], grad_norms], axis=1)
    sent = jnp.concatenate([grad_weights[:, 4 * half :], grad_norms], axis=1)
    pooled = (kept.astype(f32) + swap(sent).astype(f32)).astype(bf16)
    owned = lax.psum_scatter(pooled, "dp", scatter_dimension=0, tiled=True).astype(f32)
    grid = owned[:, : 4 * half].reshape(depth, pairs, 4, PAIR)
    grad_qkv = grid[:, :, :3].transpose(0, 2, 1, 3).reshape(depth, 3, half)
    grad_out = grid[:, :, 3].reshape(depth, half)
    grad_norm = owned[:, 4 * half : 4 * half + 4].T

    output = result(middle, slot_col, routed)
    return (
        both(place, output),
        both(place, grad_own),
        grad_qkv,
        grad_out,
        grad_norm[:2],
        grad_norm[2:],
        grad_expert_in[None],
        grad_expert_out[None],
    )


def solution(mesh):
    return jax.shard_map(
        body,
        mesh=mesh,
        in_specs=(
            P("dp", None, None),
            P("dp", None, "tensor"),
            P("dp", "tensor"),
            P(None, "dp"),
            P(None, "dp"),
            P("dp", None, "tensor"),
            P("dp", "tensor", None),
            P("dp", None),
            P(),
            P("dp", None),
            P("dp", None, None),
        ),
        out_specs=(
            P("dp", None, None),
            P("dp", None, None),
            P("dp", None, "tensor"),
            P("dp", "tensor"),
            P(None, "dp"),
            P(None, "dp"),
            P("dp", None, "tensor"),
            P("dp", "tensor", None),
        ),
        check_vma=False,
    )
```

```python
import functools

import jax
import jax.numpy as jnp
from jax import lax
from jax.experimental import pallas as pl
from jax.experimental.pallas import tpu as pltpu
from jax.sharding import PartitionSpec as P

HEAD_DIM = 64
SEQ_LEN = 1024
WIDTH = 768
PAIR = 128
BLOCK = 256
CHUNKS = 2
EPSILON = 1e-05
MASKED = -1e30
SEGMENTS = 4
SLAB = 48
OFFSETS = (0, 8, 2, 10, 4, 12, 6, 14)
VMEM = 60 * 1024 * 1024

f32 = jnp.float32
bf16 = jnp.bfloat16


def dot(a, b):
    return jnp.dot(a, b, preferred_element_type=f32)


def dot_nt(a, b):
    return lax.dot_general(a, b, (((1,), (1,)), ((), ())), preferred_element_type=f32)


def dot_tn(a, b):
    return lax.dot_general(a, b, (((0,), (0,)), ((), ())), preferred_element_type=f32)


def iota(shape, dim):
    return lax.broadcasted_iota(jnp.int32, shape, dim)


def params(axes=1):
    return pltpu.CompilerParams(
        dimension_semantics=("arbitrary",) * axes, vmem_limit_bytes=VMEM
    )


def cost(microseconds):
    return pl.CostEstimate(flops=int(microseconds * 1.1e9), bytes_accessed=1 << 20, transcendentals=0)


def whole(shape):
    zeros = (0,) * len(shape)
    return pl.BlockSpec(shape, lambda *_: zeros)


def normalize(values):
    centred = values - jnp.mean(values, axis=-1, keepdims=True)
    variance = jnp.mean(centred * centred, axis=-1, keepdims=True)
    inverse = lax.rsqrt(variance + EPSILON)
    return centred * inverse, inverse


def norm_backward(upstream, scaled, inverse, gain):
    weighted = upstream * gain
    inner = jnp.mean(weighted * scaled, axis=-1, keepdims=True)
    centred = weighted - jnp.mean(weighted, axis=-1, keepdims=True)
    return inverse * (centred - scaled * inner)


def slab(number):
    return pl.ds(pl.multiple_of(number * SLAB, SLAB), SLAB)


def assemble(base, near_ref, far_ref, out_ref):
    for ref, flip in ((near_ref, 0), (far_ref, 1)):
        for j, offset in enumerate(OFFSETS):
            out_ref[slab(base ^ offset ^ flip), :] = ref[j * SLAB : (j + 1) * SLAB, :]


def load_weights(base, step, own_steps, refs, out_ref):
    own, own_far, other, other_far = refs

    @pl.when(step < own_steps)
    def _():
        assemble(base, own, own_far, out_ref)

    @pl.when(step >= own_steps)
    def _():
        assemble(base, other, other_far, out_ref)


def load_norms(base, refs, tall_ref, out_ref):
    assemble(base, *refs, tall_ref)
    out_ref[...] = tall_ref[...].astype(f32).T[:8]


def weight_specs(own_steps):
    half = WIDTH // 2
    own = pl.BlockSpec((half, 4 * PAIR), lambda i, *_: (0, jnp.minimum(i, own_steps - 1)))
    other = pl.BlockSpec((half, 4 * PAIR), lambda i, *_: (0, jnp.maximum(i - own_steps, 0)))
    norm = pl.BlockSpec((half, PAIR), lambda i, *_: (0, 4 * own_steps))
    return [own, own, other, other, norm, norm]


def weight_arrays(parts):
    return [*parts, parts[0], parts[1]]


def dispatch(slot_row, values, out_refs):
    for chunk, out_ref in enumerate(out_refs):
        rows = out_ref.shape[0]
        for start in range(0, rows, BLOCK):
            base = chunk * rows + start
            pick = (iota((BLOCK, SEQ_LEN), 0) + base == slot_row).astype(f32).astype(bf16)
            out_ref[start : start + BLOCK] = dot(pick, values).astype(bf16)


def chunked(slot, capacity, rows):
    share = capacity // CHUNKS
    expert = slot // capacity
    rank = slot - expert * capacity
    chunk = rank // share
    return chunk * rows + expert * share + rank - chunk * share


def combine(slot_col, back_refs, start, size):
    total = None
    for chunk, back_ref in enumerate(back_refs):
        rows = back_ref.shape[0]
        pick = (iota((size, rows), 1) + chunk * rows == slot_col[start : start + size]).astype(f32)
        part = dot(pick.astype(bf16), back_ref[...])
        total = part if total is None else total + part
    return total


def route_kernel(experts, capacity, _, row_ref, col_ref, cot_ref, out_ref, slot_row_ref, slot_col_ref):
    row = row_ref[...]
    hot = (iota((experts, SEQ_LEN), 0) == row).astype(f32)
    order = (iota((SEQ_LEN, SEQ_LEN), 0) <= iota((SEQ_LEN, SEQ_LEN), 1)).astype(f32).astype(bf16)
    seen = dot(hot.astype(bf16), order)
    rank = jnp.sum(seen * hot, axis=0, keepdims=True).astype(jnp.int32) - 1
    slot_row = row * capacity + rank
    slot_row_ref[...] = slot_row
    col = col_ref[...]
    hot_col = (iota((SEQ_LEN, experts), 1) == col).astype(f32)
    seen_col = dot_tn(order, hot_col.astype(bf16))
    rank_col = jnp.sum(seen_col * hot_col, axis=1, keepdims=True).astype(jnp.int32) - 1
    slot_col_ref[...] = col * capacity + rank_col
    dispatch(slot_row, cot_ref[0], (out_ref,))


def route(tensor_place, chosen, cotangent, experts, capacity):
    rows = experts * capacity
    one = lambda i, place: (place[0], 0, 0)
    return pl.pallas_call(
        functools.partial(route_kernel, experts, capacity),
        grid_spec=pltpu.PrefetchScalarGridSpec(
            num_scalar_prefetch=1,
            grid=(1,),
            in_specs=[
                whole((1, SEQ_LEN)),
                whole((SEQ_LEN, 1)),
                pl.BlockSpec((1, SEQ_LEN, WIDTH), one),
            ],
            out_specs=[
                whole((rows, WIDTH)),
                whole((1, SEQ_LEN)),
                whole((SEQ_LEN, 1)),
            ],
        ),
        out_shape=[
            jax.ShapeDtypeStruct((rows, WIDTH), bf16),
            jax.ShapeDtypeStruct((1, SEQ_LEN), jnp.int32),
            jax.ShapeDtypeStruct((SEQ_LEN, 1), jnp.int32),
        ],
        compiler_params=params(),
        cost_estimate=cost(7),
        name="route",
    )(tensor_place, chosen.reshape(1, SEQ_LEN), chosen.reshape(SEQ_LEN, 1), cotangent)


def segment_terms(segment_col):
    lane = iota((SEQ_LEN, PAIR), 1)
    query = jnp.where((lane != segment_col) & (lane < SEGMENTS), MASKED, 0.0).astype(bf16)
    key = (lane == segment_col).astype(f32).astype(bf16)
    return query, key


def causal(block):
    return jnp.where(iota(block.shape, 0) <= iota(block.shape, 1), block, MASKED)


def forward_kernel(
    capacity,
    scalars,
    x_ref,
    own_ref,
    own_far_ref,
    other_ref,
    other_far_ref,
    norm_ref,
    norm_far_ref,
    segment_ref,
    slot_ref,
    _after,
    packed_ref,
    context_ref,
    logsum_ref,
    normed_ref,
    middle_ref,
    first_ref,
    second_ref,
    branch,
    query_seg,
    key_seg,
    context_t,
    weight_ref,
    norm_tall,
    norms,
):
    step = pl.program_id(0)
    base = scalars[1]
    load_weights(base, step, pl.num_programs(0) // 2, (own_ref, own_far_ref, other_ref, other_far_ref), weight_ref)

    @pl.when(step == 0)
    def _():
        load_norms(base, (norm_ref, norm_far_ref), norm_tall, norms)
        scaled, _ = normalize(x_ref[0].astype(f32))
        normed_ref[...] = (scaled * norms[0:1] + norms[2:3]).astype(bf16)
        branch[...] = x_ref[0].astype(f32)
        query_seg[...], key_seg[...] = segment_terms(segment_ref[...])

    mixed = dot(normed_ref[...], weight_ref[:, : 3 * PAIR])
    packed_ref[...] = mixed.astype(bf16)
    query = mixed[:, :PAIR].astype(bf16) * jnp.asarray(HEAD_DIM**-0.5, bf16)
    keys = jnp.concatenate([mixed[:, PAIR : 2 * PAIR].astype(bf16), key_seg[...]], axis=1)
    values_t = mixed[:, 2 * PAIR :].T.astype(bf16)
    lane = iota((SEQ_LEN, PAIR), 1)
    for head in range(2):
        low, high = head * HEAD_DIM, (head + 1) * HEAD_DIM
        own = jnp.where((lane >= low) & (lane < high), query, jnp.zeros_like(query))
        own = jnp.concatenate([own, query_seg[...]], axis=1)
        for start in range(0, SEQ_LEN, BLOCK):
            stop = start + BLOCK
            block = own[start:stop]
            near = causal(dot_nt(keys[start:stop], block))
            highest = jnp.max(near, axis=0, keepdims=True)
            if start:
                far = dot_nt(keys[:start], block)
                highest = jnp.maximum(highest, jnp.max(far, axis=0, keepdims=True))
            near = jnp.exp(near - highest)
            total = jnp.sum(near, axis=0, keepdims=True)
            result = dot(values_t[low:high, start:stop], near.astype(bf16))
            if start:
                far = jnp.exp(far - highest)
                total = total + jnp.sum(far, axis=0, keepdims=True)
                result = result + dot(values_t[low:high, :start], far.astype(bf16))
            context_t[low:high, start:stop] = result * (1.0 / total)
            logsum_ref[0, head : head + 1, start:stop] = highest + jnp.log(total)
    context = context_t[...].T.astype(bf16)
    context_ref[...] = context
    branch[...] += dot_nt(context, weight_ref[:, 3 * PAIR :])

    @pl.when(step == pl.num_programs(0) - 1)
    def _():
        middle = branch[...]
        middle_ref[...] = middle
        scaled, _ = normalize(middle)
        normed_two = (scaled * norms[1:2] + norms[3:4]).astype(bf16)
        slots = chunked(slot_ref[...], capacity, first_ref.shape[0])
        dispatch(slots, normed_two, (first_ref, second_ref))


def forward(scalars, inputs, weights, segment_col, slot_row, after, experts, capacity):
    rows = experts * capacity // CHUNKS
    pairs = WIDTH // PAIR
    one = lambda i, place: (place[0], 0, 0)
    return pl.pallas_call(
        functools.partial(forward_kernel, capacity),
        grid_spec=pltpu.PrefetchScalarGridSpec(
            num_scalar_prefetch=1,
            grid=(pairs,),
            in_specs=[
                pl.BlockSpec((1, SEQ_LEN, WIDTH), one),
                *weight_specs(pairs // 2),
                whole((SEQ_LEN, 1)),
                whole((1, SEQ_LEN)),
                pl.BlockSpec(memory_space=pl.ANY),
            ],
            out_specs=[
                pl.BlockSpec((SEQ_LEN, 3 * PAIR), lambda i, _: (0, i)),
                pl.BlockSpec((SEQ_LEN, PAIR), lambda i, _: (0, i)),
                pl.BlockSpec((1, 2, SEQ_LEN), lambda i, _: (i, 0, 0)),
                whole((SEQ_LEN, WIDTH)),
                whole((SEQ_LEN, WIDTH)),
                whole((rows, WIDTH)),
                whole((rows, WIDTH)),
            ],
            scratch_shapes=[
                pltpu.VMEM((SEQ_LEN, WIDTH), f32),
                pltpu.VMEM((SEQ_LEN, PAIR), bf16),
                pltpu.VMEM((SEQ_LEN, PAIR), bf16),
                pltpu.VMEM((PAIR, SEQ_LEN), f32),
                pltpu.VMEM((WIDTH, 4 * PAIR), bf16),
                pltpu.VMEM((WIDTH, PAIR), bf16),
                pltpu.VMEM((8, WIDTH), f32),
            ],
        ),
        out_shape=[
            jax.ShapeDtypeStruct((SEQ_LEN, 3 * WIDTH), bf16),
            jax.ShapeDtypeStruct((SEQ_LEN, WIDTH), bf16),
            jax.ShapeDtypeStruct((pairs, 2, SEQ_LEN), f32),
            jax.ShapeDtypeStruct((SEQ_LEN, WIDTH), bf16),
            jax.ShapeDtypeStruct((SEQ_LEN, WIDTH), f32),
            jax.ShapeDtypeStruct((rows, WIDTH), bf16),
            jax.ShapeDtypeStruct((rows, WIDTH), bf16),
        ],
        compiler_params=params(),
        cost_estimate=cost(35),
        name="attention_forward",
    )(scalars, inputs, *weight_arrays(weights), segment_col, slot_row, after)


def halves(step, own_ref, other_ref, own_steps):
    return jnp.where(step < own_steps, own_ref[...], other_ref[...])


def half_specs(shape, dim, own_steps):
    def at(block):
        return tuple(block if d == dim else 0 for d in range(len(shape)))

    return [
        pl.BlockSpec(shape, lambda i: at(jnp.minimum(i, own_steps - 1))),
        pl.BlockSpec(shape, lambda i: at(jnp.maximum(i - own_steps, 0))),
    ]


UNITS = 512


ANY = pl.BlockSpec(memory_space=pl.ANY)


def grad_hidden_kernel(own_steps, grad_ref, own_ref, other_ref, _, out_ref):
    weight = halves(pl.program_id(0), own_ref, other_ref, own_steps)
    out_ref[...] = dot_nt(grad_ref[...], weight).astype(bf16)


def grad_hidden(arrived, out_own, out_other, after):
    rows = arrived.shape[0]
    own_steps = out_own.shape[0] // UNITS
    return pl.pallas_call(
        functools.partial(grad_hidden_kernel, own_steps),
        grid=(2 * own_steps,),
        in_specs=[whole((rows, WIDTH))] + half_specs((UNITS, WIDTH), 0, own_steps) + [ANY],
        out_specs=pl.BlockSpec((rows, UNITS), lambda i: (0, i)),
        out_shape=jax.ShapeDtypeStruct((rows, 2 * own_steps * UNITS), bf16),
        compiler_params=params(),
        cost_estimate=cost(15),
        name="grad_hidden",
    )(arrived, out_own, out_other, after)


def expert_kernel(own_steps, rows_ref, grad_ref, own_ref, other_ref, hidden_ref, pre_ref, back_ref, total):
    step = pl.program_id(0)
    weight = halves(step, own_ref, other_ref, own_steps)
    before = dot(rows_ref[...], weight)
    root = 0.7978845608028654
    cube = 0.044715
    square = before * before
    tanh = jnp.tanh(before * (root + (root * cube) * square))
    half_up = 0.5 + 0.5 * tanh
    hidden_ref[...] = (before * half_up).astype(bf16)
    slope = half_up + (0.5 * before) * (1.0 - tanh * tanh) * (root + (3.0 * root * cube) * square)
    grad_hidden = grad_ref[...].reshape(before.shape)
    grad_pre = (grad_hidden.astype(f32) * slope).astype(bf16)
    pre_ref[...] = grad_pre
    part = dot_nt(grad_pre, weight)

    @pl.when(step == 0)
    def _():
        total[...] = part

    @pl.when(step > 0)
    def _():
        total[...] += part

    @pl.when(step == pl.num_programs(0) - 1)
    def _():
        back_ref[...] = total[...].astype(bf16)


def expert(arrived, grads, in_own, in_other, chunk):
    rows = arrived.shape[0]
    experts = grads.shape[0]
    share = grads.shape[1] // CHUNKS
    own_steps = in_own.shape[1] // UNITS
    wide = pl.BlockSpec((rows, UNITS), lambda i: (0, i))
    units = 2 * own_steps * UNITS
    return pl.pallas_call(
        functools.partial(expert_kernel, own_steps),
        grid=(2 * own_steps,),
        in_specs=[
            whole((rows, WIDTH)),
            pl.BlockSpec((experts, share, UNITS), lambda i: (0, chunk, i)),
        ]
        + half_specs((WIDTH, UNITS), 1, own_steps),
        out_specs=[wide, wide, whole((rows, WIDTH))],
        out_shape=[
            jax.ShapeDtypeStruct((rows, units), bf16),
            jax.ShapeDtypeStruct((rows, units), bf16),
            jax.ShapeDtypeStruct((rows, WIDTH), bf16),
        ],
        scratch_shapes=[pltpu.VMEM((rows, WIDTH), f32)],
        compiler_params=params(),
        cost_estimate=cost(22),
        name="expert",
    )(arrived, grads, in_own, in_other)


def expert_out_kernel(first_ref, second_ref, own_ref, other_ref, _, out_ref):
    units = own_ref.shape[0]
    share = out_ref.shape[1] // CHUNKS
    for chunk, hidden_ref in enumerate((first_ref, second_ref)):
        hidden = hidden_ref[...]
        total = dot(hidden[:, :units], own_ref[...]) + dot(hidden[:, units:], other_ref[...])
        part = total.astype(bf16).reshape(out_ref.shape[0], share, WIDTH)
        out_ref[:, chunk * share : (chunk + 1) * share] = part


def expert_result(hidden, out_own, out_other, after, experts):
    rows, units = hidden[0].shape
    share = rows // experts
    count = BLOCK // share
    tile = pl.BlockSpec((BLOCK, units), lambda i: (i, 0))
    return pl.pallas_call(
        expert_out_kernel,
        grid=(rows // BLOCK,),
        in_specs=[tile, tile, whole(out_own.shape), whole(out_other.shape), ANY],
        out_specs=pl.BlockSpec((count, CHUNKS * share, WIDTH), lambda i: (i, 0, 0)),
        out_shape=jax.ShapeDtypeStruct((experts, CHUNKS * share, WIDTH), bf16),
        compiler_params=params(),
        cost_estimate=cost(15),
        name="expert_result",
    )(*hidden, out_own, out_other, after)


def expert_grads_kernel(count, keep, *refs):
    arrived = refs[:count]
    grads = refs[count : 2 * count]
    hidden = refs[2 * count : 3 * count]
    pre = refs[3 * count : 4 * count]
    rows = arrived[0].shape[0]
    arrived_t = refs[-1]

    @pl.when(pl.program_id(0) == 0)
    def _():
        for chunk in range(count):
            arrived_t[:, chunk * rows : (chunk + 1) * rows] = arrived[chunk][...].T

    total_in, total_out = None, None
    for chunk in range(count):
        part_in = dot(arrived_t[:, chunk * rows : (chunk + 1) * rows], pre[chunk][...])
        part_out = dot_tn(hidden[chunk][...], grads[chunk][...].reshape(rows, WIDTH))
        total_in = part_in if total_in is None else total_in + part_in
        total_out = part_out if total_out is None else total_out + part_out
    if keep:
        peer_ref, in_ref, out_ref = refs[4 * count : -1]
        in_ref[...] = total_in + peer_ref[0, 0].astype(f32)
        out_ref[...] = total_out + peer_ref[0, 1].astype(f32)
    else:
        out_ref = refs[4 * count]
        out_ref[0, 0] = total_in.astype(bf16)
        out_ref[0, 1] = total_out.astype(bf16)


def expert_grads(arrived, grads, hidden, pre, peer=None):
    count = len(arrived)
    rows = arrived[0].shape[0]
    experts = grads.shape[0]
    share = rows // experts
    keep = peer is not None
    once = dict(pipeline_mode=pl.Buffered(1))
    parts = [pl.BlockSpec((experts, share, WIDTH), lambda i, c=c: (0, c, 0), **once) for c in range(count)]
    units = hidden[0].shape[1] // 2
    steps = units // WIDTH
    shift = 0 if keep else steps
    wide = pl.BlockSpec((rows, WIDTH), lambda i: (0, i + shift))
    full = pl.BlockSpec((rows, WIDTH), lambda i: (0, 0), **once)
    square = pl.BlockSpec((1, 2, WIDTH, WIDTH), lambda i: (i, 0, 0, 0))
    if keep:
        out_specs = [
            pl.BlockSpec((WIDTH, WIDTH), lambda i: (0, i)),
            pl.BlockSpec((WIDTH, WIDTH), lambda i: (i, 0)),
        ]
        out_shape = [
            jax.ShapeDtypeStruct((WIDTH, units), f32),
            jax.ShapeDtypeStruct((units, WIDTH), f32),
        ]
    else:
        out_specs = square
        out_shape = jax.ShapeDtypeStruct((steps, 2, WIDTH, WIDTH), bf16)
    return pl.pallas_call(
        functools.partial(expert_grads_kernel, count, keep),
        grid=(steps,),
        in_specs=[full] * count + parts + [wide] * (2 * count) + ([square] if keep else []),
        out_specs=out_specs,
        out_shape=out_shape,
        scratch_shapes=[pltpu.VMEM((WIDTH, count * rows), bf16)],
        compiler_params=params(),
        cost_estimate=cost(17),
        name="expert_grads_kept" if keep else "expert_grads_sent",
    )(*arrived, *[grads] * count, *hidden, *pre, *([peer] if keep else []))


def spread(base, from_ref, out_ref):
    for low in range(2):
        for next_low in range(2):
            for high in range(4):
                number = (high << 2) | ((base ^ (next_low << 1) ^ low) & 3)
                place = high * SLAB
                out_ref[2 * low + next_low, place : place + SLAB] = from_ref[slab(number), :].astype(bf16)


def backward_kernel(
    capacity,
    scalars,
    x_ref,
    cot_ref,
    middle_ref,
    first_ref,
    second_ref,
    slot_ref,
    segment_ref,
    normed_ref,
    own_ref,
    own_far_ref,
    other_ref,
    other_far_ref,
    norm_ref,
    norm_far_ref,
    packed_ref,
    context_ref,
    logsum_ref,
    _after,
    grad_own_ref,
    grad_other_ref,
    grad_norm_ref,
    grad_input_ref,
    grad_middle,
    grad_branch,
    grad_branch_t,
    normed_t,
    grad_normed,
    query_seg,
    key_seg,
    sums,
    grad_keys,
    grad_values,
    grad_queries_t,
    weight_ref,
    norm_tall,
    norms,
    grad_weight,
):
    step = pl.program_id(0)
    base = scalars[1]
    own_steps = pl.num_programs(0) // 2
    load_weights(base, step, own_steps, (own_ref, own_far_ref, other_ref, other_far_ref), weight_ref)

    @pl.when(step == 0)
    def _():
        load_norms(base, (norm_ref, norm_far_ref), norm_tall, norms)
        query_seg[...], key_seg[...] = segment_terms(segment_ref[...])
        slots = chunked(slot_ref[...], capacity, first_ref.shape[0])
        gain_sum = jnp.zeros((1, WIDTH), f32)
        shift_sum = jnp.zeros((1, WIDTH), f32)
        for start in range(0, SEQ_LEN, BLOCK):
            stop = start + BLOCK
            upstream = combine(slots, (first_ref, second_ref), start, BLOCK)
            scaled, inverse = normalize(middle_ref[start:stop])
            result = cot_ref[0, start:stop].astype(f32) + norm_backward(upstream, scaled, inverse, norms[1:2])
            grad_middle[start:stop] = result
            grad_branch[start:stop] = result.astype(bf16)
            grad_branch_t[:, start:stop] = result.T.astype(bf16)
            normed_t[:, start:stop] = normed_ref[start:stop].T
            gain_sum += jnp.sum(upstream * scaled, axis=0, keepdims=True)
            shift_sum += jnp.sum(upstream, axis=0, keepdims=True)
        sums[1:2] = gain_sum
        sums[3:4] = shift_sum

    grad_context = dot(grad_branch[...], weight_ref[:, 3 * PAIR :]).astype(bf16)
    grad_weight[:, 3 * PAIR :] = dot(grad_branch_t[...], context_ref[...])
    inner = (grad_context.astype(f32) * context_ref[...].astype(f32)).T
    query = packed_ref[:, :PAIR] * jnp.asarray(HEAD_DIM**-0.5, bf16)
    keys = packed_ref[:, PAIR : 2 * PAIR]
    keys_t = keys.T
    keys = jnp.concatenate([keys, key_seg[...]], axis=1)
    values = packed_ref[:, 2 * PAIR :]
    lane = iota((SEQ_LEN, PAIR), 1)
    grad_keys[...] = jnp.zeros_like(grad_keys)
    grad_values[...] = jnp.zeros_like(grad_values)
    for head in range(2):
        low, high = head * HEAD_DIM, (head + 1) * HEAD_DIM
        mine = (lane >= low) & (lane < high)
        own = jnp.where(mine, query, jnp.zeros_like(query))
        own_wide = jnp.concatenate([own, query_seg[...]], axis=1)
        upstream = jnp.where(mine, grad_context, jnp.zeros_like(grad_context))
        delta = jnp.sum(inner[low:high], axis=0, keepdims=True)
        for start in range(0, SEQ_LEN, BLOCK):
            stop = start + BLOCK
            logs = logsum_ref[0, head : head + 1, start:stop]
            ranges = [(start, stop)] + ([(0, start)] if start else [])
            grad_query = None
            for first, last in ranges:
                scores = dot_nt(keys[first:last], own_wide[start:stop])
                if first == start:
                    scores = causal(scores)
                probs = jnp.exp(scores - logs)
                grad_probs = dot_nt(values[first:last], upstream[start:stop])
                grad_scores = (probs * (grad_probs - delta[:, start:stop])).astype(bf16)
                grad_values[first:last] += dot(probs.astype(bf16), upstream[start:stop])
                grad_keys[first:last] += dot(grad_scores, own[start:stop])
                part = dot(keys_t[low:high, first:last], grad_scores)
                grad_query = part if grad_query is None else grad_query + part
            grad_queries_t[low:high, start:stop] = grad_query * (HEAD_DIM**-0.5)
    grad_packed = jnp.concatenate(
        [grad_queries_t[...].T.astype(bf16), grad_keys[...].astype(bf16), grad_values[...].astype(bf16)],
        axis=1,
    )
    grad_weight[:, : 3 * PAIR] = dot(normed_t[...], grad_packed)

    @pl.when(step < own_steps)
    def _():
        spread(base, grad_weight, grad_own_ref)

    @pl.when(step >= own_steps)
    def _():
        spread(base, grad_weight, grad_other_ref)

    part = dot_nt(grad_packed, weight_ref[:, : 3 * PAIR])

    @pl.when(step == 0)
    def _():
        grad_normed[...] = part

    @pl.when(step > 0)
    def _():
        grad_normed[...] += part

    @pl.when(step == pl.num_programs(0) - 1)
    def _():
        gain = norms[0:1]
        upstream = grad_normed[...]
        scaled, inverse = normalize(x_ref[0].astype(f32))
        result = grad_middle[...] + norm_backward(upstream, scaled, inverse, gain)
        grad_input_ref[...] = result.astype(bf16)
        sums[0:1] = jnp.sum(upstream * scaled, axis=0, keepdims=True)
        sums[2:3] = jnp.sum(upstream, axis=0, keepdims=True)
        sums[4:8] = jnp.zeros((4, WIDTH), f32)
        tall = jnp.concatenate([sums[...], jnp.zeros((PAIR - 8, WIDTH), f32)], axis=0)
        grad_weight[:, :PAIR] = tall.T
        spread(base, grad_weight.at[:, :PAIR], grad_norm_ref)


def backward(scalars, inputs, cotangent, middle, back, slot_col, segment_col, normed, weights, packed, context, logsums, after, capacity):
    pairs = WIDTH // PAIR
    rows = back[0].shape[0]
    one = lambda i, place: (place[0], 0, 0)
    once = dict(pipeline_mode=pl.Buffered(1))
    full = whole((SEQ_LEN, WIDTH))
    return pl.pallas_call(
        functools.partial(backward_kernel, capacity),
        grid_spec=pltpu.PrefetchScalarGridSpec(
            num_scalar_prefetch=1,
            grid=(pairs,),
            in_specs=[
                pl.BlockSpec((1, SEQ_LEN, WIDTH), one, **once),
                pl.BlockSpec((1, SEQ_LEN, WIDTH), one, **once),
                pl.BlockSpec((SEQ_LEN, WIDTH), lambda i, _: (0, 0), **once),
                pl.BlockSpec((rows, WIDTH), lambda i, _: (0, 0), **once),
                pl.BlockSpec((rows, WIDTH), lambda i, _: (0, 0), **once),
                whole((SEQ_LEN, 1)),
                whole((SEQ_LEN, 1)),
                pl.BlockSpec((SEQ_LEN, WIDTH), lambda i, _: (0, 0), **once),
                *weight_specs(pairs // 2),
                pl.BlockSpec((SEQ_LEN, 3 * PAIR), lambda i, _: (0, i)),
                pl.BlockSpec((SEQ_LEN, PAIR), lambda i, _: (0, i)),
                pl.BlockSpec((1, 2, SEQ_LEN), lambda i, _: (i, 0, 0)),
                ANY,
            ],
            out_specs=[
                pl.BlockSpec((4, WIDTH // 4, 4 * PAIR), lambda i, _: (0, 0, jnp.minimum(i, pairs // 2 - 1))),
                pl.BlockSpec((4, WIDTH // 4, 4 * PAIR), lambda i, _: (0, 0, jnp.maximum(i - pairs // 2, 0))),
                whole((4, WIDTH // 4, PAIR)),
                full,
            ],
            scratch_shapes=[
                pltpu.VMEM((SEQ_LEN, WIDTH), f32),
                pltpu.VMEM((SEQ_LEN, WIDTH), bf16),
                pltpu.VMEM((WIDTH, SEQ_LEN), bf16),
                pltpu.VMEM((WIDTH, SEQ_LEN), bf16),
                pltpu.VMEM((SEQ_LEN, WIDTH), f32),
                pltpu.VMEM((SEQ_LEN, PAIR), bf16),
                pltpu.VMEM((SEQ_LEN, PAIR), bf16),
                pltpu.VMEM((8, WIDTH), f32),
                pltpu.VMEM((SEQ_LEN, PAIR), f32),
                pltpu.VMEM((SEQ_LEN, PAIR), f32),
                pltpu.VMEM((PAIR, SEQ_LEN), f32),
                pltpu.VMEM((WIDTH, 4 * PAIR), bf16),
                pltpu.VMEM((WIDTH, PAIR), bf16),
                pltpu.VMEM((8, WIDTH), f32),
                pltpu.VMEM((WIDTH, 4 * PAIR), f32),
            ],
        ),
        out_shape=[
            jax.ShapeDtypeStruct((4, WIDTH // 4, 2 * WIDTH), bf16),
            jax.ShapeDtypeStruct((4, WIDTH // 4, 2 * WIDTH), bf16),
            jax.ShapeDtypeStruct((4, WIDTH // 4, PAIR), bf16),
            jax.ShapeDtypeStruct((SEQ_LEN, WIDTH), bf16),
        ],
        compiler_params=params(),
        cost_estimate=cost(56),
        name="attention_backward",
    )(
        scalars,
        inputs,
        cotangent,
        middle,
        *back,
        slot_col,
        segment_col,
        normed,
        *weight_arrays(weights),
        packed,
        context,
        logsums,
        after,
    )


def result_kernel(middle_ref, slot_ref, back_ref, out_ref):
    routed = combine(slot_ref[...], (back_ref,), 0, BLOCK)
    out_ref[...] = (middle_ref[...] + routed).astype(bf16)


def result(middle, slot_col, back):
    rows = back.shape[0]
    tile = pl.BlockSpec((BLOCK, WIDTH), lambda i: (i, 0))
    return pl.pallas_call(
        result_kernel,
        grid=(SEQ_LEN // BLOCK,),
        in_specs=[
            tile,
            pl.BlockSpec((BLOCK, 1), lambda i: (i, 0)),
            whole((rows, WIDTH)),
        ],
        out_specs=tile,
        out_shape=jax.ShapeDtypeStruct((SEQ_LEN, WIDTH), bf16),
        compiler_params=params(),
        cost_estimate=cost(8),
        name="result",
    )(middle, slot_col, back)


def swap(values):
    return lax.ppermute(values, "tensor", [(0, 1), (1, 0)])


def exchange(values, experts):
    shape = values.shape
    parts = values.reshape(experts, shape[0] // experts, shape[1])
    return lax.all_to_all(parts, "dp", split_axis=0, concat_axis=0, tiled=True).reshape(shape)


def both(place, values, *others):
    other = after(swap(values), *others)
    first = place == 0
    return jnp.stack([jnp.where(first, values, other), jnp.where(first, other, values)])


def flip(values, bit):
    size = lax.axis_size("dp")
    return lax.ppermute(values, "dp", [(i, i ^ bit) for i in range(size)])


def after(values, *others):
    return lax.optimization_barrier((values, *others))[0]


def rows_of(parts):
    return jnp.concatenate(parts, axis=0)


def fetch_by_halves(shard):
    own = shard
    for bit in (8, 4):
        own = rows_of([own, flip(own, bit)])
    middle = own.shape[0] // 2
    first, second = own[:middle], own[middle:]
    first_peer, second_next = swap(first), flip(second, 2)
    first_next = flip(rows_of([first, first_peer]), 2)
    second_peer = swap(rows_of([second, second_next]))
    near = rows_of([first, first_next[:middle], second, second_next])
    near_peer = rows_of([first_peer, first_next[middle:], second_peer])
    return near, flip(near, 1), near_peer, flip(near_peer, 1)


def fetch_whole(shard):
    own = lax.all_gather(rows_of([shard, swap(shard)]), "dp", axis=0, tiled=True)
    own = own.reshape(-1, 2, shard.shape[0], shard.shape[1]).transpose(1, 0, 2, 3).reshape(2, -1, SLAB, shard.shape[1])
    return tuple(rows_of([own[side, o ^ far] for o in OFFSETS]) for side in (0, 1) for far in (0, 1))


def pool_by_halves(grads, peer):
    size = lax.axis_size("dp")
    kept = (grads[:2].astype(f32) + after(flip(grads[2:], 1), peer).astype(f32)).astype(bf16)
    kept = (kept[0].astype(f32) + flip(kept[1], 2).astype(f32)).astype(bf16)
    groups = [[high * 4 + low for high in range(size // 4)] for low in range(4)]
    parts = kept.reshape(size // 4, SLAB, -1)
    parts = lax.all_to_all(parts, "dp", split_axis=0, concat_axis=0, tiled=True, axis_index_groups=groups)
    return jnp.sum(parts.astype(f32), axis=0)


def pool_whole(grads):
    full = grads.reshape(2, 2, 4, SLAB, -1).transpose(2, 1, 0, 3, 4).reshape(WIDTH, -1)
    return lax.psum_scatter(full, "dp", scatter_dimension=0, tiled=True).astype(f32)


def body(
    inputs,
    qkv_weight,
    out_weight,
    norm_gains,
    norm_shifts,
    expert_in,
    expert_out,
    token_ids,
    hash_table,
    segment_ids,
    cotangent,
):
    place = lax.axis_index("tensor")
    experts = lax.axis_size("dp")
    by_halves = experts * SLAB == WIDTH
    base = lax.axis_index("dp") if by_halves else jnp.zeros((), jnp.int32)
    places = jnp.stack([place, base]).astype(jnp.int32)
    capacity = 2 * SEQ_LEN // experts
    depth = qkv_weight.shape[0]
    half = qkv_weight.shape[2]
    pairs = half // PAIR

    own = jnp.concatenate(
        [
            qkv_weight.reshape(depth, 3, pairs, PAIR).transpose(0, 2, 1, 3),
            out_weight.reshape(depth, pairs, 1, PAIR),
        ],
        axis=2,
    ).reshape(depth, 4 * half)
    norms = jnp.concatenate([norm_gains, norm_shifts], axis=0).T
    norms = jnp.pad(norms, ((0, 0), (0, PAIR - norms.shape[1])))
    shard = jnp.concatenate([own, norms], axis=1)
    weights = fetch_by_halves(shard) if by_halves else fetch_whole(shard)

    in_own, out_own = expert_in[0], expert_out[0]
    out_other = swap(after(out_own, weights[2]))
    in_other = swap(after(in_own, weights[2]))

    ids = lax.dynamic_index_in_dim(token_ids, place, 0, keepdims=False)
    chosen = jnp.take(hash_table, ids, axis=0)
    segment_col = lax.dynamic_index_in_dim(segment_ids, place, 0, keepdims=False).reshape(SEQ_LEN, 1)
    sent, slot_row, slot_col = route(places, chosen, cotangent, experts, capacity)
    grads = exchange(sent, experts)

    packed, context, logsums, normed, middle, first, second = forward(
        places, inputs, weights, segment_col, slot_row, slot_col, experts, capacity
    )
    upstream = grad_hidden(grads, out_own, out_other, first)
    second, upstream = lax.optimization_barrier((second, upstream))
    arrived = [exchange(first, experts), exchange(second, experts)]
    upstream = upstream.reshape(experts, capacity, -1)
    grads = grads.reshape(experts, capacity, WIDTH)
    done = [expert(a, upstream, in_own, in_other, c) for c, a in enumerate(arrived)]
    hidden = [d[0] for d in done]
    pre = [d[1] for d in done]
    sent = expert_grads(arrived, grads, hidden, pre)
    back = [exchange(done[0][2], experts), exchange(after(done[1][2], sent), experts)]
    peer = swap(sent)
    routed_send = expert_result(hidden, out_own, out_other, sent, experts)
    routed = exchange(routed_send.reshape(experts * capacity, WIDTH), experts)

    grad_own_weights, grad_other_weights, grad_norms, grad_own = backward(
        places, inputs, cotangent, middle, back, slot_col, segment_col, normed, weights, packed, context, logsums,
        routed_send, capacity
    )
    pooled = jnp.concatenate([grad_own_weights, grad_other_weights, grad_norms], axis=2)
    pooled = pool_by_halves(pooled, peer) if by_halves else pool_whole(pooled)
    sent_share = pooled[:, 4 * half :].astype(bf16)
    kept = jnp.concatenate([pooled[:, : 4 * half], pooled[:, 8 * half :]], axis=1)
    owned = kept + swap(sent_share).astype(f32)
    grid = owned[:, : 4 * half].reshape(depth, pairs, 4, PAIR)
    grad_qkv = grid[:, :, :3].transpose(0, 2, 1, 3).reshape(depth, 3, half)
    grad_out = grid[:, :, 3].reshape(depth, half)
    grad_norm = owned[:, 4 * half : 4 * half + 4].T
    grad_expert_in, grad_expert_out = expert_grads(arrived, grads, hidden, pre, peer)

    output = result(middle, slot_col, routed)
    return (
        both(place, output),
        both(place, grad_own, output),
        grad_qkv,
        grad_out,
        grad_norm[:2],
        grad_norm[2:],
        grad_expert_in[None],
        grad_expert_out[None],
    )


def solution(mesh):
    return jax.shard_map(
        body,
        mesh=mesh,
        in_specs=(
            P("dp", None, None),
            P("dp", None, "tensor"),
            P("dp", "tensor"),
            P(None, "dp"),
            P(None, "dp"),
            P("dp", None, "tensor"),
            P("dp", "tensor", None),
            P("dp", None),
            P(),
            P("dp", None),
            P("dp", None, None),
        ),
        out_specs=(
            P("dp", None, None),
            P("dp", None, None),
            P("dp", None, "tensor"),
            P("dp", "tensor"),
            P(None, "dp"),
            P(None, "dp"),
            P("dp", None, "tensor"),
            P("dp", "tensor", None),
        ),
        check_vma=False,
    )
```

```python
import functools

import jax
import jax.numpy as jnp
from jax import lax
from jax.experimental import pallas as pl
from jax.experimental.pallas import tpu as pltpu
from jax.sharding import PartitionSpec as P

HEAD_DIM = 64
SEQ_LEN = 1024
WIDTH = 768
PAIR = 128
BLOCK = 256
EPSILON = 1e-05
MASKED = -1e30
SEGMENTS = 4
SLAB = 48
OFFSETS = (0, 8, 2, 10, 4, 12, 6, 14)
VMEM = 60 * 1024 * 1024

f32 = jnp.float32
bf16 = jnp.bfloat16


def dot(a, b):
    return jnp.dot(a, b, preferred_element_type=f32)


def dot_nt(a, b):
    return lax.dot_general(a, b, (((1,), (1,)), ((), ())), preferred_element_type=f32)


def dot_tn(a, b):
    return lax.dot_general(a, b, (((0,), (0,)), ((), ())), preferred_element_type=f32)


def iota(shape, dim):
    return lax.broadcasted_iota(jnp.int32, shape, dim)


def params(axes=1):
    return pltpu.CompilerParams(
        dimension_semantics=("arbitrary",) * axes, vmem_limit_bytes=VMEM
    )


def cost(microseconds):
    return pl.CostEstimate(flops=int(microseconds * 1.1e9), bytes_accessed=1 << 20, transcendentals=0)


def whole(shape):
    zeros = (0,) * len(shape)
    return pl.BlockSpec(shape, lambda *_: zeros)


def normalize(values):
    centred = values - jnp.mean(values, axis=-1, keepdims=True)
    variance = jnp.mean(centred * centred, axis=-1, keepdims=True)
    inverse = lax.rsqrt(variance + EPSILON)
    return centred * inverse, inverse


def norm_backward(upstream, scaled, inverse, gain):
    weighted = upstream * gain
    inner = jnp.mean(weighted * scaled, axis=-1, keepdims=True)
    centred = weighted - jnp.mean(weighted, axis=-1, keepdims=True)
    return inverse * (centred - scaled * inner)


def slab(number):
    return pl.ds(pl.multiple_of(number * SLAB, SLAB), SLAB)


def assemble(base, near_ref, far_ref, out_ref):
    for ref, flip in ((near_ref, 0), (far_ref, 1)):
        for j, offset in enumerate(OFFSETS):
            out_ref[slab(base ^ offset ^ flip), :] = ref[j * SLAB : (j + 1) * SLAB, :]


def load_pairs(base, refs, out_ref):
    width = out_ref.shape[1] // 2
    for side in range(2):
        assemble(base, refs[2 * side], refs[2 * side + 1], out_ref.at[:, side * width : (side + 1) * width])


def load_norms(base, refs, tall_ref, out_ref):
    assemble(base, *refs, tall_ref)
    out_ref[...] = tall_ref[...].astype(f32).T[:8]


ONCE = dict(pipeline_mode=pl.Buffered(1))
HALF = WIDTH // 2
TRIPLE = 3 * HALF


def weight_specs():
    mixing = pl.BlockSpec((HALF, TRIPLE), lambda *_: (0, 0), **ONCE)
    output = pl.BlockSpec((HALF, HALF), lambda *_: (0, 3), **ONCE)
    norm = pl.BlockSpec((HALF, PAIR), lambda *_: (0, 4 * HALF // PAIR), **ONCE)
    return [mixing] * 4 + [output] * 4 + [norm] * 2


def weight_arrays(parts):
    return [*parts, *parts, parts[0], parts[1]]


def pair_columns(step, kind):
    pairs = HALF // PAIR
    return pl.ds(pl.multiple_of((step // pairs) * TRIPLE + kind * HALF + (step % pairs) * PAIR, PAIR), PAIR)


def rearrange(base, from_ref, out_ref):
    place = 0
    for low in range(2):
        for next_low in range(2):
            for high in range(4):
                number = (high << 2) | ((base ^ (next_low << 1) ^ low) & 3)
                out_ref[place : place + SLAB] = from_ref[slab(number), :]
                place += SLAB


def dispatch(slot_row, values, out_refs):
    base = 0
    for out_ref in out_refs:
        rows = out_ref.shape[0]
        for start in range(0, rows, BLOCK):
            pick = (iota((BLOCK, SEQ_LEN), 0) + (base + start) == slot_row).astype(f32).astype(bf16)
            out_ref[start : start + BLOCK] = dot(pick, values).astype(bf16)
        base += rows


def shares_of(capacity):
    return capacity // 2, capacity // 2


def chunked(slot, capacity, experts):
    first, second = shares_of(capacity)
    expert = slot // capacity
    rank = slot - expert * capacity
    late = experts * first + expert * second + rank - first
    return jnp.where(rank < first, expert * first + rank, late)


def combine(slot_col, back_refs, start, size):
    total, base = None, 0
    for back_ref in back_refs:
        rows = back_ref.shape[0]
        pick = (iota((size, rows), 1) + base == slot_col[start : start + size]).astype(f32)
        part = dot(pick.astype(bf16), back_ref[...])
        total = part if total is None else total + part
        base += rows
    return total


def route_kernel(experts, capacity, _, row_ref, col_ref, cot_ref, out_ref, slot_row_ref, slot_col_ref):
    row = row_ref[...]
    hot = (iota((experts, SEQ_LEN), 0) == row).astype(f32)
    order = (iota((SEQ_LEN, SEQ_LEN), 0) <= iota((SEQ_LEN, SEQ_LEN), 1)).astype(f32).astype(bf16)
    seen = dot(hot.astype(bf16), order)
    rank = jnp.sum(seen * hot, axis=0, keepdims=True).astype(jnp.int32) - 1
    slot_row = row * capacity + rank
    slot_row_ref[...] = slot_row
    col = col_ref[...]
    hot_col = (iota((SEQ_LEN, experts), 1) == col).astype(f32)
    seen_col = dot_tn(order, hot_col.astype(bf16))
    rank_col = jnp.sum(seen_col * hot_col, axis=1, keepdims=True).astype(jnp.int32) - 1
    slot_col_ref[...] = col * capacity + rank_col
    dispatch(slot_row, cot_ref[0], (out_ref,))


def route(tensor_place, chosen, cotangent, experts, capacity):
    rows = experts * capacity
    one = lambda i, place: (place[0], 0, 0)
    return pl.pallas_call(
        functools.partial(route_kernel, experts, capacity),
        grid_spec=pltpu.PrefetchScalarGridSpec(
            num_scalar_prefetch=1,
            grid=(1,),
            in_specs=[
                whole((1, SEQ_LEN)),
                whole((SEQ_LEN, 1)),
                pl.BlockSpec((1, SEQ_LEN, WIDTH), one),
            ],
            out_specs=[
                whole((rows, WIDTH)),
                whole((1, SEQ_LEN)),
                whole((SEQ_LEN, 1)),
            ],
        ),
        out_shape=[
            jax.ShapeDtypeStruct((rows, WIDTH), bf16),
            jax.ShapeDtypeStruct((1, SEQ_LEN), jnp.int32),
            jax.ShapeDtypeStruct((SEQ_LEN, 1), jnp.int32),
        ],
        compiler_params=params(),
        cost_estimate=cost(7),
        name="route",
    )(tensor_place, chosen.reshape(1, SEQ_LEN), chosen.reshape(SEQ_LEN, 1), cotangent)


def segment_terms(segment_col):
    lane = iota((SEQ_LEN, PAIR), 1)
    query = jnp.where((lane != segment_col) & (lane < SEGMENTS), MASKED, 0.0).astype(bf16)
    key = (lane == segment_col) | ((lane >= SEGMENTS) & (lane < SEGMENTS + 3))
    return query, key.astype(f32).astype(bf16)


def minus(lane, column, others):
    result = others.astype(f32)
    for place in range(SEGMENTS, SEGMENTS + 3):
        part = column.astype(bf16).astype(f32)
        result = jnp.where(lane == place, -part, result)
        column = column - part
    return result.astype(bf16)


def causal(block):
    return jnp.where(iota(block.shape, 0) <= iota(block.shape, 1), block, MASKED)


def head_mask(head):
    lane = iota((1, PAIR), 1)
    mine = (lane >= head * HEAD_DIM) & (lane < (head + 1) * HEAD_DIM)
    return mine.astype(f32)


def forward_kernel(
    experts,
    capacity,
    scalars,
    x_ref,
    *refs,
):
    weight_refs = refs[:10]
    segment_ref, slot_ref, _, packed_ref, context_ref, logsum_ref, middle_ref, first_ref, second_ref = refs[10:19]
    normed, all_packed, all_context, query_seg, key_seg, context_t, mixing, output, norm_tall, norms = refs[19:]
    step = pl.program_id(0)
    base = scalars[1]

    @pl.when(step == 0)
    def _():
        load_norms(base, weight_refs[8:], norm_tall, norms)
        load_pairs(base, weight_refs[:4], mixing)
        for start in range(0, SEQ_LEN, BLOCK):
            scaled, _ = normalize(x_ref[0, start : start + BLOCK].astype(f32))
            normed[start : start + BLOCK] = (scaled * norms[0:1] + norms[2:3]).astype(bf16)
        for side in range(2):
            columns = slice(side * TRIPLE, (side + 1) * TRIPLE)
            all_packed[:, columns] = dot(normed[...], mixing[:, columns]).astype(bf16)
        query_seg[...], key_seg[...] = segment_terms(segment_ref[...])

    query, key, value = [all_packed[:, pair_columns(step, kind)] for kind in range(3)]
    packed_ref[:, :PAIR] = query
    packed_ref[:, PAIR : 2 * PAIR] = key
    packed_ref[:, 2 * PAIR :] = value
    keys = jnp.concatenate([key, key_seg[...]], axis=1)
    values_t = value.T
    for head in range(2):
        low, high = head * HEAD_DIM, (head + 1) * HEAD_DIM
        own = query * (head_mask(head) * HEAD_DIM**-0.5).astype(bf16)
        own = jnp.concatenate([own, query_seg[...]], axis=1)
        for start in range(0, SEQ_LEN, BLOCK):
            stop = start + BLOCK
            block = own[start:stop]
            near = causal(dot_nt(keys[start:stop], block))
            highest = jnp.max(near, axis=0, keepdims=True)
            if start:
                far = dot_nt(keys[:start], block)
                highest = jnp.maximum(highest, jnp.max(far, axis=0, keepdims=True))
            near = jnp.exp(near - highest)
            total = jnp.sum(near, axis=0, keepdims=True)
            result = dot(values_t[low:high, start:stop], near.astype(bf16))
            if start:
                far = jnp.exp(far - highest)
                total = total + jnp.sum(far, axis=0, keepdims=True)
                result = result + dot(values_t[low:high, :start], far.astype(bf16))
            context_t[low:high, start:stop] = result * (1.0 / total)
            logsum_ref[0, head : head + 1, start:stop] = highest + jnp.log(total)
    context = context_t[...].T.astype(bf16)
    context_ref[...] = context
    all_context[:, pl.ds(pl.multiple_of(step * PAIR, PAIR), PAIR)] = context

    @pl.when(step == pl.num_programs(0) - 1)
    def _():
        load_pairs(base, weight_refs[4:8], output)
        slots = chunked(slot_ref[...], capacity, experts)
        for start in range(0, SEQ_LEN, BLOCK):
            stop = start + BLOCK
            middle = x_ref[0, start:stop].astype(f32) + dot_nt(all_context[start:stop], output[...])
            middle_ref[start:stop] = middle
            scaled, _ = normalize(middle)
            normed[start:stop] = (scaled * norms[1:2] + norms[3:4]).astype(bf16)
        dispatch(slots, normed[...], (first_ref, second_ref))


def forward(scalars, inputs, weights, segment_col, slot_row, after, experts, capacity):
    first, second = [experts * share for share in shares_of(capacity)]
    pairs = WIDTH // PAIR
    one = lambda i, place: (place[0], 0, 0)
    return pl.pallas_call(
        functools.partial(forward_kernel, experts, capacity),
        grid_spec=pltpu.PrefetchScalarGridSpec(
            num_scalar_prefetch=1,
            grid=(pairs,),
            in_specs=[
                pl.BlockSpec((1, SEQ_LEN, WIDTH), one, **ONCE),
                *weight_specs(),
                whole((SEQ_LEN, 1)),
                whole((1, SEQ_LEN)),
                pl.BlockSpec(memory_space=pl.ANY),
            ],
            out_specs=[
                pl.BlockSpec((SEQ_LEN, 3 * PAIR), lambda i, _: (0, i)),
                pl.BlockSpec((SEQ_LEN, PAIR), lambda i, _: (0, i)),
                pl.BlockSpec((1, 2, SEQ_LEN), lambda i, _: (i, 0, 0)),
                whole((SEQ_LEN, WIDTH)),
                whole((first, WIDTH)),
                whole((second, WIDTH)),
            ],
            scratch_shapes=[
                pltpu.VMEM((SEQ_LEN, WIDTH), bf16),
                pltpu.VMEM((SEQ_LEN, 3 * WIDTH), bf16),
                pltpu.VMEM((SEQ_LEN, WIDTH), bf16),
                pltpu.VMEM((SEQ_LEN, PAIR), bf16),
                pltpu.VMEM((SEQ_LEN, PAIR), bf16),
                pltpu.VMEM((PAIR, SEQ_LEN), f32),
                pltpu.VMEM((WIDTH, 3 * WIDTH), bf16),
                pltpu.VMEM((WIDTH, WIDTH), bf16),
                pltpu.VMEM((WIDTH, PAIR), bf16),
                pltpu.VMEM((8, WIDTH), f32),
            ],
        ),
        out_shape=[
            jax.ShapeDtypeStruct((SEQ_LEN, 3 * WIDTH), bf16),
            jax.ShapeDtypeStruct((SEQ_LEN, WIDTH), bf16),
            jax.ShapeDtypeStruct((pairs, 2, SEQ_LEN), f32),
            jax.ShapeDtypeStruct((SEQ_LEN, WIDTH), f32),
            jax.ShapeDtypeStruct((first, WIDTH), bf16),
            jax.ShapeDtypeStruct((second, WIDTH), bf16),
        ],
        compiler_params=params(),
        cost_estimate=cost(30),
        name="attention_forward",
    )(scalars, inputs, *weight_arrays(weights), segment_col, slot_row, after)


def pick_piece(step, refs, counts):
    ends = starts_of(counts)[1:]
    weight = refs[-1][...]
    for ref, end in reversed(list(zip(refs[:-1], ends[:-1]))):
        weight = jnp.where(step < end, ref[...], weight)
    return weight


def starts_of(counts):
    starts = [0]
    for count in counts:
        starts.append(starts[-1] + count)
    return starts


def piece_specs(shape, dim, counts):
    def at(block):
        return tuple(block if d == dim else 0 for d in range(len(shape)))

    def spec(start, count):
        return pl.BlockSpec(shape, lambda i: at(jnp.clip(i - start, 0, count - 1)))

    return [spec(start, count) for start, count in zip(starts_of(counts), counts)]


UNITS = 512


ANY = pl.BlockSpec(memory_space=pl.ANY)


def grad_hidden_kernel(counts, grad_ref, *refs):
    weight = pick_piece(pl.program_id(0), refs[:-2], counts)
    refs[-1][...] = dot_nt(grad_ref[...], weight).astype(bf16)


def grad_hidden(arrived, pieces, after):
    rows = arrived.shape[0]
    counts = [piece.shape[0] // UNITS for piece in pieces]
    return pl.pallas_call(
        functools.partial(grad_hidden_kernel, counts),
        grid=(sum(counts),),
        in_specs=[whole((rows, WIDTH))] + piece_specs((UNITS, WIDTH), 0, counts) + [ANY],
        out_specs=pl.BlockSpec((rows, UNITS), lambda i: (0, i)),
        out_shape=jax.ShapeDtypeStruct((rows, sum(counts) * UNITS), bf16),
        compiler_params=params(),
        cost_estimate=cost(15),
        name="grad_hidden",
    )(arrived, *pieces, after)


def expert_kernel(resumed, counts, rows_ref, grad_ref, *refs):
    weight_refs, refs = refs[: len(counts)], refs[len(counts) :]
    hidden_ref, pre_ref, back_ref, total = refs[1:] if resumed else refs
    step = pl.program_id(0)
    weight = pick_piece(step, weight_refs, counts)
    root = 0.7978845608028654
    cube = 0.044715

    @pl.when(step == 0)
    def _():
        total[...] = refs[0][...] if resumed else jnp.zeros_like(total)

    rows = rows_ref.shape[0]
    before = dot(rows_ref[...], weight)
    upstream = grad_ref[...].reshape(rows, EXPERT_UNITS).astype(f32)
    square = before * before
    inner = root + (root * cube) * square
    tanh = jnp.tanh(before * inner)
    hidden = before * (0.5 + 0.5 * tanh)
    hidden_ref[...] = hidden.astype(bf16)
    slope = 0.5 + 0.5 * tanh + (hidden - hidden * tanh) * (3.0 * inner - 2.0 * root)
    grad_pre = (upstream * slope).astype(bf16)
    pre_ref[...] = grad_pre
    total[...] += dot_nt(grad_pre, weight)

    @pl.when(step == pl.num_programs(0) - 1)
    def _():
        back_ref[...] = total[...].astype(back_ref.dtype)


EXPERT_UNITS = 768


def expert_part(arrived, grads, pieces, chunk, side, partial=None, last=True):
    rows = arrived.shape[0]
    experts, capacity, _ = grads.shape
    shares = shares_of(capacity)
    share = shares[chunk]
    place = sum(shares[:chunk]) // share
    counts = [piece.shape[1] // EXPERT_UNITS for piece in pieces]
    units = sum(piece.shape[1] for piece in pieces)
    start = side * counts[0]
    wide = pl.BlockSpec((rows, EXPERT_UNITS), lambda i: (0, i))
    resumed = partial is not None
    full = pl.BlockSpec((rows, WIDTH), lambda i: (0, 0), **ONCE)
    return pl.pallas_call(
        functools.partial(expert_kernel, resumed, counts),
        grid=(sum(counts),),
        in_specs=[
            full,
            pl.BlockSpec((experts, share, EXPERT_UNITS), lambda i: (0, place, i + start)),
        ]
        + piece_specs((WIDTH, EXPERT_UNITS), 1, counts)
        + ([full] if resumed else []),
        out_specs=[wide, wide, full],
        out_shape=[
            jax.ShapeDtypeStruct((rows, units), bf16),
            jax.ShapeDtypeStruct((rows, units), bf16),
            jax.ShapeDtypeStruct((rows, WIDTH), bf16 if last else f32),
        ],
        scratch_shapes=[pltpu.VMEM((rows, WIDTH), f32)],
        compiler_params=params(),
        cost_estimate=cost(10 * len(pieces)),
        name="expert",
    )(arrived, grads, *pieces, *([partial] if resumed else []))


def expert(arrived, grads, own, other, chunk):
    if chunk:
        hidden, pre, back = expert_part(arrived, grads, [own, other], chunk, 0)
        return ((hidden, 0), (hidden, 1)), ((pre, 0), (pre, 1)), back
    hidden_own, pre_own, partial = expert_part(arrived, grads, [own], chunk, 0, None, False)
    hidden_other, pre_other, back = expert_part(arrived, grads, [other], chunk, 1, partial)
    return ((hidden_own, 0), (hidden_other, 0)), ((pre_own, 0), (pre_other, 0)), back


def expert_out_kernel(first_ref, first_other_ref, second_ref, second_other_ref, own_ref, other_ref, _, out_ref):
    experts = out_ref.shape[0]
    place = 0
    for hidden_ref, other in ((first_ref, first_other_ref), (second_ref, second_other_ref)):
        share = hidden_ref.shape[0] // experts
        total = dot(hidden_ref[...], own_ref[...]) + dot(other[...], other_ref[...])
        out_ref[:, place : place + share] = total.astype(bf16).reshape(experts, share, WIDTH)
        place += share


def expert_result(hidden, own, other, after, experts):
    steps = 4
    units = own.shape[0]
    parts = [part for chunk in hidden for part in chunk]
    tiles = [pl.BlockSpec((a.shape[0] // steps, units), lambda i, column=column: (i, column)) for a, column in parts]
    capacity = sum(chunk[0][0].shape[0] for chunk in hidden) // experts
    weight = pl.BlockSpec(own.shape, lambda i: (0, 0), **ONCE)
    return pl.pallas_call(
        expert_out_kernel,
        grid=(steps,),
        in_specs=[*tiles, weight, weight, ANY],
        out_specs=pl.BlockSpec((experts // steps, capacity, WIDTH), lambda i: (i, 0, 0)),
        out_shape=jax.ShapeDtypeStruct((experts, capacity, WIDTH), bf16),
        compiler_params=params(),
        cost_estimate=cost(15),
        name="expert_result",
    )(*[a for a, _ in parts], own, other, after)


def expert_grads_kernel(count, keep, *refs):
    arrived = refs[:count]
    grads = refs[count : 2 * count]
    hidden = refs[2 * count : 3 * count]
    pre = refs[3 * count : 4 * count]
    arrived_t = refs[-1]
    starts = starts_of([ref.shape[0] for ref in arrived])

    @pl.when(pl.program_id(0) == 0)
    def _():
        for chunk in range(count):
            arrived_t[:, starts[chunk] : starts[chunk + 1]] = arrived[chunk][...].T

    total_in, total_out = None, None
    for chunk in range(count):
        part_in = dot(arrived_t[:, starts[chunk] : starts[chunk + 1]], pre[chunk][...])
        part_out = dot_tn(hidden[chunk][...], grads[chunk][...].reshape(-1, WIDTH))
        total_in = part_in if total_in is None else total_in + part_in
        total_out = part_out if total_out is None else total_out + part_out
    if keep:
        peer_ref, in_ref, out_ref = refs[4 * count : -1]
        in_ref[...] = total_in + peer_ref[0, 0].astype(f32)
        out_ref[...] = total_out + peer_ref[0, 1].astype(f32)
    else:
        out_ref = refs[4 * count]
        out_ref[0, 0] = total_in.astype(bf16)
        out_ref[0, 1] = total_out.astype(bf16)


def expert_grads(arrived, grads, hidden, pre, units, peer=None):
    count = len(arrived)
    experts, capacity, _ = grads.shape
    shares = shares_of(capacity)
    keep = peer is not None

    def part(chunk):
        place = sum(shares[:chunk]) // shares[chunk]
        return pl.BlockSpec((experts, shares[chunk], WIDTH), lambda i: (0, place, 0), **ONCE)

    steps = units // WIDTH
    wide = [
        pl.BlockSpec((a.shape[0], WIDTH), lambda i, shift=column * steps: (0, i + shift)) for a, column in hidden
    ]
    full = [pl.BlockSpec(a.shape, lambda i: (0, 0), **ONCE) for a in arrived]
    square = pl.BlockSpec((1, 2, WIDTH, WIDTH), lambda i: (i, 0, 0, 0))
    if keep:
        out_specs = [
            pl.BlockSpec((WIDTH, WIDTH), lambda i: (0, i)),
            pl.BlockSpec((WIDTH, WIDTH), lambda i: (i, 0)),
        ]
        out_shape = [
            jax.ShapeDtypeStruct((WIDTH, units), f32),
            jax.ShapeDtypeStruct((units, WIDTH), f32),
        ]
    else:
        out_specs = square
        out_shape = jax.ShapeDtypeStruct((steps, 2, WIDTH, WIDTH), bf16)
    return pl.pallas_call(
        functools.partial(expert_grads_kernel, count, keep),
        grid=(steps,),
        in_specs=[*full, *[part(c) for c in range(count)], *wide, *wide] + ([square] if keep else []),
        out_specs=out_specs,
        out_shape=out_shape,
        scratch_shapes=[pltpu.VMEM((WIDTH, experts * capacity), bf16)],
        compiler_params=params(),
        cost_estimate=cost(17),
        name="expert_grads_kept" if keep else "expert_grads_sent",
    )(*arrived, *[grads] * count, *[a for a, _ in hidden], *[a for a, _ in pre], *([peer] if keep else []))


def backward_kernel(
    experts,
    capacity,
    scalars,
    x_ref,
    cot_ref,
    middle_ref,
    first_ref,
    second_ref,
    slot_ref,
    segment_ref,
    *refs,
):
    weight_refs = refs[:10]
    packed_ref, context_ref, logsum_ref, _, kept_ref, sent_ref, grad_input_ref = refs[10:17]
    (
        grad_middle,
        grad_branch,
        turned,
        arranged,
        grad_context,
        query_seg,
        key_seg,
        sums,
        all_probs,
        all_scores,
        queries_pair,
        keys_pair,
        upstream_pair,
        grad_packed,
        mixing,
        output,
        norm_tall,
        norms,
    ) = refs[17:]
    step = pl.program_id(0)
    base = scalars[1]
    kept_rows = kept_ref.shape[0]

    @pl.when(step == 0)
    def _():
        load_norms(base, weight_refs[8:], norm_tall, norms)
        load_pairs(base, weight_refs[4:8], output)
        query_seg[...], key_seg[...] = segment_terms(segment_ref[...])
        slots = chunked(slot_ref[...], capacity, experts)
        gain_sum = jnp.zeros((1, WIDTH), f32)
        shift_sum = jnp.zeros((1, WIDTH), f32)
        for start in range(0, SEQ_LEN, BLOCK):
            stop = start + BLOCK
            upstream = combine(slots, (first_ref, second_ref), start, BLOCK)
            scaled, inverse = normalize(middle_ref[start:stop])
            result = cot_ref[0, start:stop].astype(f32) + norm_backward(upstream, scaled, inverse, norms[1:2])
            grad_middle[start:stop] = result
            grad_branch[start:stop] = result.astype(bf16)
            turned[:, start:stop] = result.T.astype(bf16)
            gain_sum += jnp.sum(upstream * scaled, axis=0, keepdims=True)
            shift_sum += jnp.sum(upstream, axis=0, keepdims=True)
        sums[1:2] = gain_sum
        sums[3:4] = shift_sum
        grad_context[...] = dot(grad_branch[...], output[...]).astype(bf16)
        rearrange(base, turned, arranged)
        grads = dot(arranged[...], context_ref[...]).astype(bf16)
        for side in range(2):
            place = side * 4 * HALF + TRIPLE
            part = grads[:, side * HALF : (side + 1) * HALF]
            kept_ref[:, place : place + HALF] = part[:kept_rows]
            sent_ref[:, place : place + HALF] = part[kept_rows:]

    columns = pl.ds(pl.multiple_of(step * PAIR, PAIR), PAIR)
    pair_grad = grad_context[:, columns]
    inner = pair_grad.astype(f32) * context_ref[:, columns].astype(f32)
    query = packed_ref[:, :PAIR]
    keys = packed_ref[:, PAIR : 2 * PAIR]
    keys_wide = jnp.concatenate([keys, key_seg[...]], axis=1)
    lane = iota((SEQ_LEN, PAIR), 1)
    ones = ((lane >= SEGMENTS) & (lane < SEGMENTS + 3)).astype(f32).astype(bf16)
    values_wide = jnp.concatenate([packed_ref[:, 2 * PAIR :], ones], axis=1)
    logs = jnp.concatenate([logsum_ref[0], jnp.zeros((6, SEQ_LEN), f32)], axis=0).T
    for head in range(2):
        first_row = head * SEQ_LEN
        mask = head_mask(head)
        own = query * (mask * HEAD_DIM**-0.5).astype(bf16)
        upstream = pair_grad * mask.astype(bf16)
        queries_pair[first_row : first_row + SEQ_LEN] = own
        upstream_pair[first_row : first_row + SEQ_LEN] = upstream
        keys_pair[first_row : first_row + SEQ_LEN] = keys * mask.astype(bf16)
        delta = jnp.sum(inner * mask, axis=1, keepdims=True)
        own_wide = jnp.concatenate([own, minus(lane, logs[:, head : head + 1], query_seg[...])], axis=1)
        upstream_wide = jnp.concatenate([upstream, minus(lane, delta, jnp.zeros((SEQ_LEN, PAIR), f32))], axis=1)
        for start in range(0, SEQ_LEN, BLOCK):
            stop = start + BLOCK
            column = first_row + start
            for first, last in [(start, stop)] + ([(0, start)] if start else []):
                probs = jnp.exp(dot_nt(keys_wide[first:last], own_wide[start:stop]))
                if first == start:
                    probs = jnp.where(iota(probs.shape, 0) <= iota(probs.shape, 1), probs, 0.0)
                grad_probs = dot_nt(values_wide[first:last], upstream_wide[start:stop])
                all_probs[first:last, column : column + BLOCK] = probs.astype(bf16)
                all_scores[first:last, column : column + BLOCK] = (probs * grad_probs).astype(bf16)
    for start in range(0, SEQ_LEN, BLOCK):
        stop = start + BLOCK
        grad_query, grad_key, grad_value = None, None, None
        for head in range(2):
            first_row = head * SEQ_LEN
            later = slice(first_row + start, first_row + SEQ_LEN)
            column = first_row + start
            part_value = dot(all_probs[start:stop, later], upstream_pair[later])
            part_key = dot(all_scores[start:stop, later], queries_pair[later])
            part_query = dot_tn(all_scores[:stop, column : column + BLOCK], keys_pair[first_row : first_row + stop])
            grad_value = part_value if grad_value is None else grad_value + part_value
            grad_key = part_key if grad_key is None else grad_key + part_key
            grad_query = part_query if grad_query is None else grad_query + part_query
        grad_packed[start:stop, pair_columns(step, 0)] = (grad_query * (HEAD_DIM**-0.5)).astype(bf16)
        grad_packed[start:stop, pair_columns(step, 1)] = grad_key.astype(bf16)
        grad_packed[start:stop, pair_columns(step, 2)] = grad_value.astype(bf16)

    @pl.when(step == pl.num_programs(0) - 1)
    def _():
        load_pairs(base, weight_refs[:4], mixing)
        gain_sum = jnp.zeros((1, WIDTH), f32)
        shift_sum = jnp.zeros((1, WIDTH), f32)
        for start in range(0, SEQ_LEN, BLOCK):
            stop = start + BLOCK
            upstream = dot_nt(grad_packed[start:stop], mixing[...])
            scaled, inverse = normalize(x_ref[0, start:stop].astype(f32))
            result = grad_middle[start:stop] + norm_backward(upstream, scaled, inverse, norms[0:1])
            grad_input_ref[start:stop] = result.astype(bf16)
            normed = scaled * norms[0:1] + norms[2:3]
            turned[:, start:stop] = normed.T.astype(bf16)
            gain_sum += jnp.sum(upstream * scaled, axis=0, keepdims=True)
            shift_sum += jnp.sum(upstream, axis=0, keepdims=True)
        rearrange(base, turned, arranged)
        for side in range(2):
            place = side * 4 * HALF
            part = dot(arranged[...], grad_packed[:, side * TRIPLE : (side + 1) * TRIPLE]).astype(bf16)
            kept_ref[:, place : place + TRIPLE] = part[:kept_rows]
            sent_ref[:, place : place + TRIPLE] = part[kept_rows:]
        sums[0:1] = gain_sum
        sums[2:3] = shift_sum
        sums[4:8] = jnp.zeros((4, WIDTH), f32)
        tall = jnp.concatenate([sums[...], jnp.zeros((PAIR - 8, WIDTH), f32)], axis=0)
        turned[:, :PAIR] = tall.T.astype(bf16)
        rearrange(base, turned.at[:, :PAIR], arranged.at[:, :PAIR])
        place = 8 * HALF
        kept_ref[:, place : place + PAIR] = arranged[:kept_rows, :PAIR]
        sent_ref[:, place : place + PAIR] = arranged[kept_rows:, :PAIR]


def backward(scalars, inputs, cotangent, middle, back, slot_col, segment_col, weights, packed, context, logsums, after, experts, capacity):
    pairs = WIDTH // PAIR
    rows = back[0].shape[0]
    one = lambda i, place: (place[0], 0, 0)
    full = whole((SEQ_LEN, WIDTH))
    once = pl.BlockSpec((SEQ_LEN, WIDTH), lambda i, _: (0, 0), **ONCE)
    columns = 8 * HALF + PAIR
    return pl.pallas_call(
        functools.partial(backward_kernel, experts, capacity),
        grid_spec=pltpu.PrefetchScalarGridSpec(
            num_scalar_prefetch=1,
            grid=(pairs,),
            in_specs=[
                pl.BlockSpec((1, SEQ_LEN, WIDTH), one, **ONCE),
                pl.BlockSpec((1, SEQ_LEN, WIDTH), one, **ONCE),
                once,
                *[pl.BlockSpec(b.shape, lambda i, _: (0, 0), **ONCE) for b in back],
                whole((SEQ_LEN, 1)),
                whole((SEQ_LEN, 1)),
                *weight_specs(),
                pl.BlockSpec((SEQ_LEN, 3 * PAIR), lambda i, _: (0, i)),
                once,
                pl.BlockSpec((1, 2, SEQ_LEN), lambda i, _: (i, 0, 0)),
                ANY,
            ],
            out_specs=[
                pl.BlockSpec((HALF, columns), lambda i, _: (0, 0), **ONCE),
                pl.BlockSpec((HALF, columns), lambda i, _: (0, 0), **ONCE),
                pl.BlockSpec((SEQ_LEN, WIDTH), lambda i, _: (0, 0), **ONCE),
            ],
            scratch_shapes=[
                pltpu.VMEM((SEQ_LEN, WIDTH), f32),
                pltpu.VMEM((SEQ_LEN, WIDTH), bf16),
                pltpu.VMEM((WIDTH, SEQ_LEN), bf16),
                pltpu.VMEM((WIDTH, SEQ_LEN), bf16),
                pltpu.VMEM((SEQ_LEN, WIDTH), bf16),
                pltpu.VMEM((SEQ_LEN, PAIR), bf16),
                pltpu.VMEM((SEQ_LEN, PAIR), bf16),
                pltpu.VMEM((8, WIDTH), f32),
                pltpu.VMEM((SEQ_LEN, 2 * SEQ_LEN), bf16),
                pltpu.VMEM((SEQ_LEN, 2 * SEQ_LEN), bf16),
                pltpu.VMEM((2 * SEQ_LEN, PAIR), bf16),
                pltpu.VMEM((2 * SEQ_LEN, PAIR), bf16),
                pltpu.VMEM((2 * SEQ_LEN, PAIR), bf16),
                pltpu.VMEM((SEQ_LEN, 3 * WIDTH), bf16),
                pltpu.VMEM((WIDTH, 3 * WIDTH), bf16),
                pltpu.VMEM((WIDTH, WIDTH), bf16),
                pltpu.VMEM((WIDTH, PAIR), bf16),
                pltpu.VMEM((8, WIDTH), f32),
            ],
        ),
        out_shape=[
            jax.ShapeDtypeStruct((HALF, columns), bf16),
            jax.ShapeDtypeStruct((HALF, columns), bf16),
            jax.ShapeDtypeStruct((SEQ_LEN, WIDTH), bf16),
        ],
        compiler_params=params(),
        cost_estimate=cost(50),
        name="attention_backward",
    )(
        scalars,
        inputs,
        cotangent,
        middle,
        *back,
        slot_col,
        segment_col,
        *weight_arrays(weights),
        packed,
        context,
        logsums,
        after,
    )


def result_kernel(middle_ref, slot_ref, back_ref, out_ref):
    routed = combine(slot_ref[...], (back_ref,), 0, BLOCK)
    out_ref[...] = (middle_ref[...] + routed).astype(bf16)


def result(middle, slot_col, back):
    rows = back.shape[0]
    tile = pl.BlockSpec((BLOCK, WIDTH), lambda i: (i, 0))
    return pl.pallas_call(
        result_kernel,
        grid=(SEQ_LEN // BLOCK,),
        in_specs=[
            tile,
            pl.BlockSpec((BLOCK, 1), lambda i: (i, 0)),
            whole((rows, WIDTH)),
        ],
        out_specs=tile,
        out_shape=jax.ShapeDtypeStruct((SEQ_LEN, WIDTH), bf16),
        compiler_params=params(),
        cost_estimate=cost(8),
        name="result",
    )(middle, slot_col, back)


def swap(values):
    return lax.ppermute(values, "tensor", [(0, 1), (1, 0)])


def exchange(values, experts):
    shape = values.shape
    parts = values.reshape(experts, shape[0] // experts, shape[1])
    return lax.all_to_all(parts, "dp", split_axis=0, concat_axis=0, tiled=True).reshape(shape)


def both(place, values, *others):
    other = after(swap(values), *others)
    first = place == 0
    return jnp.stack([jnp.where(first, values, other), jnp.where(first, other, values)])


def flip(values, bit):
    size = lax.axis_size("dp")
    return lax.ppermute(values, "dp", [(i, i ^ bit) for i in range(size)])


def after(values, *others):
    return lax.optimization_barrier((values, *others))[0]


def rows_of(parts):
    return jnp.concatenate(parts, axis=0)


def fetch_by_halves(shard):
    own = shard
    for bit in (8, 4):
        own = rows_of([own, flip(own, bit)])
    middle = own.shape[0] // 2
    first, second = own[:middle], own[middle:]
    first_peer, second_next = swap(first), flip(second, 2)
    first_next = flip(rows_of([first, first_peer]), 2)
    second_peer = swap(rows_of([second, second_next]))
    near = rows_of([first, first_next[:middle], second, second_next])
    near_peer = rows_of([first_peer, first_next[middle:], second_peer])
    return near, flip(near, 1), near_peer, flip(near_peer, 1)


def fetch_whole(shard):
    own = lax.all_gather(rows_of([shard, swap(shard)]), "dp", axis=0, tiled=True)
    own = own.reshape(-1, 2, shard.shape[0], shard.shape[1]).transpose(1, 0, 2, 3).reshape(2, -1, SLAB, shard.shape[1])
    return tuple(rows_of([own[side, o ^ far] for o in OFFSETS]) for side in (0, 1) for far in (0, 1))


def pool_by_halves(kept, sent, peer):
    size = lax.axis_size("dp")
    kept = (kept.astype(f32) + after(flip(sent, 1), peer).astype(f32)).astype(bf16)
    middle = kept.shape[0] // 2
    kept = (kept[:middle].astype(f32) + flip(kept[middle:], 2).astype(f32)).astype(bf16)
    groups = [[high * 4 + low for high in range(size // 4)] for low in range(4)]
    parts = kept.reshape(size // 4, SLAB, -1)
    parts = lax.all_to_all(parts, "dp", split_axis=0, concat_axis=0, tiled=True, axis_index_groups=groups)
    return jnp.sum(parts.astype(f32), axis=0)


def pool_whole(kept, sent):
    full = jnp.concatenate([kept, sent], axis=0)
    full = full.reshape(2, 2, 4, SLAB, -1).transpose(2, 1, 0, 3, 4).reshape(WIDTH, -1)
    return lax.psum_scatter(full, "dp", scatter_dimension=0, tiled=True).astype(f32)


def body(
    inputs,
    qkv_weight,
    out_weight,
    norm_gains,
    norm_shifts,
    expert_in,
    expert_out,
    token_ids,
    hash_table,
    segment_ids,
    cotangent,
):
    place = lax.axis_index("tensor")
    experts = lax.axis_size("dp")
    by_halves = experts * SLAB == WIDTH
    base = lax.axis_index("dp") if by_halves else jnp.zeros((), jnp.int32)
    places = jnp.stack([place, base]).astype(jnp.int32)
    capacity = 2 * SEQ_LEN // experts
    depth = qkv_weight.shape[0]
    half = qkv_weight.shape[2]

    norms = jnp.concatenate([norm_gains, norm_shifts], axis=0).T
    norms = jnp.pad(norms, ((0, 0), (0, PAIR - norms.shape[1])))
    shard = jnp.concatenate([qkv_weight.reshape(depth, 3 * half), out_weight, norms], axis=1)
    weights = fetch_by_halves(shard) if by_halves else fetch_whole(shard)

    in_own, out_own = expert_in[0], expert_out[0]
    out_other = swap(after(out_own, weights[2]))
    in_other = swap(after(in_own, weights[2]))

    ids = lax.dynamic_index_in_dim(token_ids, place, 0, keepdims=False)
    chosen = jnp.take(hash_table, ids, axis=0)
    segment_col = lax.dynamic_index_in_dim(segment_ids, place, 0, keepdims=False).reshape(SEQ_LEN, 1)
    sent, slot_row, slot_col = route(places, chosen, cotangent, experts, capacity)
    grads = exchange(sent, experts)

    packed, context, logsums, middle, first, second = forward(
        places, inputs, weights, segment_col, slot_row, slot_col, experts, capacity
    )
    upstream = grad_hidden(grads, [out_own, out_other], first)
    second, upstream = lax.optimization_barrier((second, upstream))
    arrived = [exchange(first, experts), exchange(second, experts)]
    upstream = upstream.reshape(experts, capacity, -1)
    grads = grads.reshape(experts, capacity, WIDTH)
    done = [expert(a, upstream, in_own, in_other, c) for c, a in enumerate(arrived)]
    hidden = [d[0] for d in done]
    pre = [d[1] for d in done]
    sent = expert_grads(arrived, grads, [h[1] for h in hidden], [p[1] for p in pre], in_own.shape[1])
    back = [exchange(done[0][2], experts), exchange(after(done[1][2], sent), experts)]
    peer = swap(sent)
    routed_send = expert_result(hidden, out_own, out_other, sent, experts)
    routed = exchange(routed_send.reshape(experts * capacity, WIDTH), experts)

    kept, sent_rows, grad_own = backward(
        places, inputs, cotangent, middle, back, slot_col, segment_col, weights, packed, context, logsums,
        routed_send, experts, capacity
    )
    pooled = pool_by_halves(kept, sent_rows, peer) if by_halves else pool_whole(kept, sent_rows)
    sent_share = pooled[:, 4 * half :].astype(bf16)
    kept = jnp.concatenate([pooled[:, : 4 * half], pooled[:, 8 * half :]], axis=1)
    owned = kept + swap(sent_share).astype(f32)
    grad_qkv = owned[:, : 3 * half].reshape(depth, 3, half)
    grad_out = owned[:, 3 * half : 4 * half]
    grad_norm = owned[:, 4 * half : 4 * half + 4].T
    grad_expert_in, grad_expert_out = expert_grads(
        arrived, grads, [h[0] for h in hidden], [p[0] for p in pre], in_own.shape[1], peer
    )

    output = result(middle, slot_col, routed)
    return (
        both(place, output, owned),
        both(place, grad_own, output),
        grad_qkv,
        grad_out,
        grad_norm[:2],
        grad_norm[2:],
        grad_expert_in[None],
        grad_expert_out[None],
    )


def solution(mesh):
    return jax.shard_map(
        body,
        mesh=mesh,
        in_specs=(
            P("dp", None, None),
            P("dp", None, "tensor"),
            P("dp", "tensor"),
            P(None, "dp"),
            P(None, "dp"),
            P("dp", None, "tensor"),
            P("dp", "tensor", None),
            P("dp", None),
            P(),
            P("dp", None),
            P("dp", None, None),
        ),
        out_specs=(
            P("dp", None, None),
            P("dp", None, None),
            P("dp", None, "tensor"),
            P("dp", "tensor"),
            P(None, "dp"),
            P(None, "dp"),
            P("dp", None, "tensor"),
            P("dp", "tensor", None),
        ),
        check_vma=False,
    )
```

```python
import functools

import jax
import jax.numpy as jnp
from jax import lax
from jax.experimental import pallas as pl
from jax.experimental.pallas import tpu as pltpu
from jax.sharding import PartitionSpec as P

HEAD_DIM = 64
SEQ_LEN = 1024
WIDTH = 768
PAIR = 128
BLOCK = 256
EPSILON = 1e-05
MASKED = -1e30
SEGMENTS = 4
SLAB = 48
OFFSETS = (0, 8, 2, 10, 4, 12, 6, 14)
VMEM = 60 * 1024 * 1024

f32 = jnp.float32
bf16 = jnp.bfloat16


def dot(a, b):
    return jnp.dot(a, b, preferred_element_type=f32)


def dot_nt(a, b):
    return lax.dot_general(a, b, (((1,), (1,)), ((), ())), preferred_element_type=f32)


def dot_tn(a, b):
    return lax.dot_general(a, b, (((0,), (0,)), ((), ())), preferred_element_type=f32)


def iota(shape, dim):
    return lax.broadcasted_iota(jnp.int32, shape, dim)


def params(axes=1):
    return pltpu.CompilerParams(
        dimension_semantics=("arbitrary",) * axes, vmem_limit_bytes=VMEM
    )


def cost(microseconds):
    return pl.CostEstimate(flops=int(microseconds * 1.1e9), bytes_accessed=1 << 20, transcendentals=0)


def whole(shape):
    zeros = (0,) * len(shape)
    return pl.BlockSpec(shape, lambda *_: zeros)


def normalize(values):
    centred = values - jnp.mean(values, axis=-1, keepdims=True)
    variance = jnp.mean(centred * centred, axis=-1, keepdims=True)
    inverse = lax.rsqrt(variance + EPSILON)
    return centred * inverse, inverse


def norm_backward(upstream, scaled, inverse, gain):
    weighted = upstream * gain
    inner = jnp.mean(weighted * scaled, axis=-1, keepdims=True)
    centred = weighted - jnp.mean(weighted, axis=-1, keepdims=True)
    return inverse * (centred - scaled * inner)


def slab(number):
    return pl.ds(pl.multiple_of(number * SLAB, SLAB), SLAB)


def assemble(base, near_ref, far_ref, out_ref):
    for ref, flip in ((near_ref, 0), (far_ref, 1)):
        for j, offset in enumerate(OFFSETS):
            out_ref[slab(base ^ offset ^ flip), :] = ref[j * SLAB : (j + 1) * SLAB, :]


def load_pairs(base, refs, out_ref):
    width = out_ref.shape[1] // 2
    for side in range(2):
        assemble(base, refs[2 * side], refs[2 * side + 1], out_ref.at[:, side * width : (side + 1) * width])


def load_norms(base, refs, tall_ref, out_ref):
    assemble(base, *refs, tall_ref)
    out_ref[...] = tall_ref[...].astype(f32).T[:8]


ONCE = dict(pipeline_mode=pl.Buffered(1))
HALF = WIDTH // 2
TRIPLE = 3 * HALF


def weight_specs():
    mixing = pl.BlockSpec((HALF, TRIPLE), lambda *_: (0, 0), **ONCE)
    output = pl.BlockSpec((HALF, HALF), lambda *_: (0, 3), **ONCE)
    norm = pl.BlockSpec((HALF, PAIR), lambda *_: (0, 4 * HALF // PAIR), **ONCE)
    return [mixing] * 4 + [output] * 4 + [norm] * 2


def weight_arrays(parts):
    return [*parts, *parts, parts[0], parts[1]]


def pair_columns(step, kind):
    pairs = HALF // PAIR
    return pl.ds(pl.multiple_of((step // pairs) * TRIPLE + kind * HALF + (step % pairs) * PAIR, PAIR), PAIR)


def rearrange(base, from_ref, out_ref):
    place = 0
    for low in range(2):
        for next_low in range(2):
            for high in range(4):
                number = (high << 2) | ((base ^ (next_low << 1) ^ low) & 3)
                out_ref[place : place + SLAB] = from_ref[slab(number), :]
                place += SLAB


def dispatch(slot_row, values, out_refs):
    base = 0
    for out_ref in out_refs:
        rows = out_ref.shape[0]
        for start in range(0, rows, BLOCK):
            pick = (iota((BLOCK, SEQ_LEN), 0) + (base + start) == slot_row).astype(f32).astype(bf16)
            out_ref[start : start + BLOCK] = dot(pick, values).astype(bf16)
        base += rows


def shares_of(capacity):
    return capacity // 2, capacity // 2


def chunked(slot, capacity, experts):
    first, second = shares_of(capacity)
    expert = slot // capacity
    rank = slot - expert * capacity
    late = experts * first + expert * second + rank - first
    return jnp.where(rank < first, expert * first + rank, late)


def combine(slot_col, back_refs, start, size):
    total, base = None, 0
    for back_ref in back_refs:
        rows = back_ref.shape[0]
        pick = (iota((size, rows), 1) + base == slot_col[start : start + size]).astype(f32)
        part = dot(pick.astype(bf16), back_ref[...])
        total = part if total is None else total + part
        base += rows
    return total


def route_kernel(experts, capacity, _, row_ref, col_ref, cot_ref, out_ref, slot_row_ref, slot_col_ref):
    row = row_ref[...]
    hot = (iota((experts, SEQ_LEN), 0) == row).astype(f32)
    order = (iota((SEQ_LEN, SEQ_LEN), 0) <= iota((SEQ_LEN, SEQ_LEN), 1)).astype(f32).astype(bf16)
    seen = dot(hot.astype(bf16), order)
    rank = jnp.sum(seen * hot, axis=0, keepdims=True).astype(jnp.int32) - 1
    slot_row = row * capacity + rank
    slot_row_ref[...] = slot_row
    col = col_ref[...]
    hot_col = (iota((SEQ_LEN, experts), 1) == col).astype(f32)
    seen_col = dot_tn(order, hot_col.astype(bf16))
    rank_col = jnp.sum(seen_col * hot_col, axis=1, keepdims=True).astype(jnp.int32) - 1
    slot_col_ref[...] = col * capacity + rank_col
    dispatch(slot_row, cot_ref[0], (out_ref,))


def route(tensor_place, chosen, cotangent, experts, capacity):
    rows = experts * capacity
    one = lambda i, place: (place[0], 0, 0)
    return pl.pallas_call(
        functools.partial(route_kernel, experts, capacity),
        grid_spec=pltpu.PrefetchScalarGridSpec(
            num_scalar_prefetch=1,
            grid=(1,),
            in_specs=[
                whole((1, SEQ_LEN)),
                whole((SEQ_LEN, 1)),
                pl.BlockSpec((1, SEQ_LEN, WIDTH), one),
            ],
            out_specs=[
                whole((rows, WIDTH)),
                whole((1, SEQ_LEN)),
                whole((SEQ_LEN, 1)),
            ],
        ),
        out_shape=[
            jax.ShapeDtypeStruct((rows, WIDTH), bf16),
            jax.ShapeDtypeStruct((1, SEQ_LEN), jnp.int32),
            jax.ShapeDtypeStruct((SEQ_LEN, 1), jnp.int32),
        ],
        compiler_params=params(),
        cost_estimate=cost(7),
        name="route",
    )(tensor_place, chosen.reshape(1, SEQ_LEN), chosen.reshape(SEQ_LEN, 1), cotangent)


def segment_terms(segment_col):
    lane = iota((SEQ_LEN, PAIR), 1)
    query = jnp.where((lane != segment_col) & (lane < SEGMENTS), MASKED, 0.0).astype(bf16)
    key = (lane == segment_col) | ((lane >= SEGMENTS) & (lane < SEGMENTS + 3))
    return query, key.astype(f32).astype(bf16)


def minus(lane, column, others):
    result = others.astype(f32)
    for place in range(SEGMENTS, SEGMENTS + 3):
        part = column.astype(bf16).astype(f32)
        result = jnp.where(lane == place, -part, result)
        column = column - part
    return result.astype(bf16)


def causal(block):
    return jnp.where(iota(block.shape, 0) <= iota(block.shape, 1), block, MASKED)


def head_mask(head):
    lane = iota((1, PAIR), 1)
    mine = (lane >= head * HEAD_DIM) & (lane < (head + 1) * HEAD_DIM)
    return mine.astype(f32)


def forward_kernel(
    experts,
    capacity,
    scalars,
    x_ref,
    *refs,
):
    weight_refs = refs[:10]
    segment_ref, slot_ref, _, packed_ref, context_ref, logsum_ref, middle_ref, first_ref, second_ref = refs[10:19]
    normed, all_packed, all_context, query_seg, key_seg, context_t, mixing, output, norm_tall, norms = refs[19:]
    step = pl.program_id(0)
    base = scalars[1]

    @pl.when(step == 0)
    def _():
        load_norms(base, weight_refs[8:], norm_tall, norms)
        load_pairs(base, weight_refs[:4], mixing)
        for start in range(0, SEQ_LEN, BLOCK):
            scaled, _ = normalize(x_ref[0, start : start + BLOCK].astype(f32))
            normed[start : start + BLOCK] = (scaled * norms[0:1] + norms[2:3]).astype(bf16)
        for side in range(2):
            columns = slice(side * TRIPLE, (side + 1) * TRIPLE)
            all_packed[:, columns] = dot(normed[...], mixing[:, columns]).astype(bf16)
        query_seg[...], key_seg[...] = segment_terms(segment_ref[...])

    query, key, value = [all_packed[:, pair_columns(step, kind)] for kind in range(3)]
    packed_ref[:, :PAIR] = query
    packed_ref[:, PAIR : 2 * PAIR] = key
    packed_ref[:, 2 * PAIR :] = value
    keys = jnp.concatenate([key, key_seg[...]], axis=1)
    values_t = value.T
    for head in range(2):
        low, high = head * HEAD_DIM, (head + 1) * HEAD_DIM
        own = query * (head_mask(head) * HEAD_DIM**-0.5).astype(bf16)
        own = jnp.concatenate([own, query_seg[...]], axis=1)
        for start in range(0, SEQ_LEN, BLOCK):
            stop = start + BLOCK
            block = own[start:stop]
            near = causal(dot_nt(keys[start:stop], block))
            highest = jnp.max(near, axis=0, keepdims=True)
            if start:
                far = dot_nt(keys[:start], block)
                highest = jnp.maximum(highest, jnp.max(far, axis=0, keepdims=True))
            near = jnp.exp(near - highest)
            total = jnp.sum(near, axis=0, keepdims=True)
            result = dot(values_t[low:high, start:stop], near.astype(bf16))
            if start:
                far = jnp.exp(far - highest)
                total = total + jnp.sum(far, axis=0, keepdims=True)
                result = result + dot(values_t[low:high, :start], far.astype(bf16))
            context_t[low:high, start:stop] = result * (1.0 / total)
            logsum_ref[0, head : head + 1, start:stop] = highest + jnp.log(total)
    context = context_t[...].T.astype(bf16)
    context_ref[...] = context
    all_context[:, pl.ds(pl.multiple_of(step * PAIR, PAIR), PAIR)] = context

    @pl.when(step == pl.num_programs(0) - 1)
    def _():
        load_pairs(base, weight_refs[4:8], output)
        slots = chunked(slot_ref[...], capacity, experts)
        for start in range(0, SEQ_LEN, BLOCK):
            stop = start + BLOCK
            middle = x_ref[0, start:stop].astype(f32) + dot_nt(all_context[start:stop], output[...])
            middle_ref[start:stop] = middle
            scaled, _ = normalize(middle)
            normed[start:stop] = (scaled * norms[1:2] + norms[3:4]).astype(bf16)
        dispatch(slots, normed[...], (first_ref, second_ref))


def forward(scalars, inputs, weights, segment_col, slot_row, after, experts, capacity):
    first, second = [experts * share for share in shares_of(capacity)]
    pairs = WIDTH // PAIR
    one = lambda i, place: (place[0], 0, 0)
    return pl.pallas_call(
        functools.partial(forward_kernel, experts, capacity),
        grid_spec=pltpu.PrefetchScalarGridSpec(
            num_scalar_prefetch=1,
            grid=(pairs,),
            in_specs=[
                pl.BlockSpec((1, SEQ_LEN, WIDTH), one, **ONCE),
                *weight_specs(),
                whole((SEQ_LEN, 1)),
                whole((1, SEQ_LEN)),
                pl.BlockSpec(memory_space=pl.ANY),
            ],
            out_specs=[
                pl.BlockSpec((SEQ_LEN, 3 * PAIR), lambda i, _: (0, i)),
                pl.BlockSpec((SEQ_LEN, PAIR), lambda i, _: (0, i)),
                pl.BlockSpec((1, 2, SEQ_LEN), lambda i, _: (i, 0, 0)),
                whole((SEQ_LEN, WIDTH)),
                whole((first, WIDTH)),
                whole((second, WIDTH)),
            ],
            scratch_shapes=[
                pltpu.VMEM((SEQ_LEN, WIDTH), bf16),
                pltpu.VMEM((SEQ_LEN, 3 * WIDTH), bf16),
                pltpu.VMEM((SEQ_LEN, WIDTH), bf16),
                pltpu.VMEM((SEQ_LEN, PAIR), bf16),
                pltpu.VMEM((SEQ_LEN, PAIR), bf16),
                pltpu.VMEM((PAIR, SEQ_LEN), f32),
                pltpu.VMEM((WIDTH, 3 * WIDTH), bf16),
                pltpu.VMEM((WIDTH, WIDTH), bf16),
                pltpu.VMEM((WIDTH, PAIR), bf16),
                pltpu.VMEM((8, WIDTH), f32),
            ],
        ),
        out_shape=[
            jax.ShapeDtypeStruct((SEQ_LEN, 3 * WIDTH), bf16),
            jax.ShapeDtypeStruct((SEQ_LEN, WIDTH), bf16),
            jax.ShapeDtypeStruct((pairs, 2, SEQ_LEN), f32),
            jax.ShapeDtypeStruct((SEQ_LEN, WIDTH), f32),
            jax.ShapeDtypeStruct((first, WIDTH), bf16),
            jax.ShapeDtypeStruct((second, WIDTH), bf16),
        ],
        compiler_params=params(),
        cost_estimate=cost(30),
        name="attention_forward",
    )(scalars, inputs, *weight_arrays(weights), segment_col, slot_row, after)


def pick_piece(step, refs, counts):
    ends = starts_of(counts)[1:]
    weight = refs[-1][...]
    for ref, end in reversed(list(zip(refs[:-1], ends[:-1]))):
        weight = jnp.where(step < end, ref[...], weight)
    return weight


def starts_of(counts):
    starts = [0]
    for count in counts:
        starts.append(starts[-1] + count)
    return starts


def piece_specs(shape, dim, counts):
    def at(block):
        return tuple(block if d == dim else 0 for d in range(len(shape)))

    def spec(start, count):
        return pl.BlockSpec(shape, lambda i: at(jnp.clip(i - start, 0, count - 1)))

    return [spec(start, count) for start, count in zip(starts_of(counts), counts)]


UNITS = 512


ANY = pl.BlockSpec(memory_space=pl.ANY)


def grad_hidden_kernel(counts, grad_ref, *refs):
    weight = pick_piece(pl.program_id(0), refs[:-2], counts)
    refs[-1][...] = dot_nt(grad_ref[...], weight).astype(bf16)


def grad_hidden(arrived, pieces, after):
    rows = arrived.shape[0]
    counts = [piece.shape[0] // UNITS for piece in pieces]
    return pl.pallas_call(
        functools.partial(grad_hidden_kernel, counts),
        grid=(sum(counts),),
        in_specs=[whole((rows, WIDTH))] + piece_specs((UNITS, WIDTH), 0, counts) + [ANY],
        out_specs=pl.BlockSpec((rows, UNITS), lambda i: (0, i)),
        out_shape=jax.ShapeDtypeStruct((rows, sum(counts) * UNITS), bf16),
        compiler_params=params(),
        cost_estimate=cost(15),
        name="grad_hidden",
    )(arrived, *pieces, after)


def expert_kernel(resumed, counts, rows_ref, grad_ref, *refs):
    weight_refs, refs = refs[: len(counts)], refs[len(counts) :]
    hidden_ref, pre_ref, back_ref, total = refs[1:] if resumed else refs
    step = pl.program_id(0)
    weight = pick_piece(step, weight_refs, counts)
    root = 0.7978845608028654
    cube = 0.044715

    @pl.when(step == 0)
    def _():
        total[...] = refs[0][...] if resumed else jnp.zeros_like(total)

    rows = rows_ref.shape[0]
    before = dot(rows_ref[...], weight)
    upstream = grad_ref[...].reshape(rows, EXPERT_UNITS).astype(f32)
    square = before * before
    inner = root + (root * cube) * square
    tanh = jnp.tanh(before * inner)
    hidden = before * (0.5 + 0.5 * tanh)
    hidden_ref[...] = hidden.astype(bf16)
    slope = 0.5 + 0.5 * tanh + (hidden - hidden * tanh) * (3.0 * inner - 2.0 * root)
    grad_pre = (upstream * slope).astype(bf16)
    pre_ref[...] = grad_pre
    total[...] += dot_nt(grad_pre, weight)

    @pl.when(step == pl.num_programs(0) - 1)
    def _():
        back_ref[...] = total[...].astype(back_ref.dtype)


EXPERT_UNITS = 768


def expert_part(arrived, grads, pieces, chunk, side, partial=None, last=True):
    rows = arrived.shape[0]
    experts, capacity, _ = grads.shape
    shares = shares_of(capacity)
    share = shares[chunk]
    place = sum(shares[:chunk]) // share
    counts = [piece.shape[1] // EXPERT_UNITS for piece in pieces]
    units = sum(piece.shape[1] for piece in pieces)
    start = side * counts[0]
    wide = pl.BlockSpec((rows, EXPERT_UNITS), lambda i: (0, i))
    resumed = partial is not None
    full = pl.BlockSpec((rows, WIDTH), lambda i: (0, 0), **ONCE)
    return pl.pallas_call(
        functools.partial(expert_kernel, resumed, counts),
        grid=(sum(counts),),
        in_specs=[
            full,
            pl.BlockSpec((experts, share, EXPERT_UNITS), lambda i: (0, place, i + start)),
        ]
        + piece_specs((WIDTH, EXPERT_UNITS), 1, counts)
        + ([full] if resumed else []),
        out_specs=[wide, wide, full],
        out_shape=[
            jax.ShapeDtypeStruct((rows, units), bf16),
            jax.ShapeDtypeStruct((rows, units), bf16),
            jax.ShapeDtypeStruct((rows, WIDTH), bf16 if last else f32),
        ],
        scratch_shapes=[pltpu.VMEM((rows, WIDTH), f32)],
        compiler_params=params(),
        cost_estimate=cost(10 * len(pieces)),
        name="expert",
    )(arrived, grads, *pieces, *([partial] if resumed else []))


def expert(arrived, grads, own, other, chunk):
    if chunk:
        hidden, pre, back = expert_part(arrived, grads, [own, other], chunk, 0)
        return ((hidden, 0), (hidden, 1)), ((pre, 0), (pre, 1)), back
    hidden_own, pre_own, partial = expert_part(arrived, grads, [own], chunk, 0, None, False)
    hidden_other, pre_other, back = expert_part(arrived, grads, [other], chunk, 1, partial)
    return ((hidden_own, 0), (hidden_other, 0)), ((pre_own, 0), (pre_other, 0)), back


def expert_out_kernel(first_ref, first_other_ref, second_ref, second_other_ref, own_ref, other_ref, _, out_ref):
    experts = out_ref.shape[0]
    place = 0
    for hidden_ref, other in ((first_ref, first_other_ref), (second_ref, second_other_ref)):
        share = hidden_ref.shape[0] // experts
        total = dot(hidden_ref[...], own_ref[...]) + dot(other[...], other_ref[...])
        out_ref[:, place : place + share] = total.astype(bf16).reshape(experts, share, WIDTH)
        place += share


def expert_result(hidden, own, other, after, experts):
    steps = 4
    units = own.shape[0]
    parts = [part for chunk in hidden for part in chunk]
    tiles = [pl.BlockSpec((a.shape[0] // steps, units), lambda i, column=column: (i, column)) for a, column in parts]
    capacity = sum(chunk[0][0].shape[0] for chunk in hidden) // experts
    weight = pl.BlockSpec(own.shape, lambda i: (0, 0), **ONCE)
    return pl.pallas_call(
        expert_out_kernel,
        grid=(steps,),
        in_specs=[*tiles, weight, weight, ANY],
        out_specs=pl.BlockSpec((experts // steps, capacity, WIDTH), lambda i: (i, 0, 0)),
        out_shape=jax.ShapeDtypeStruct((experts, capacity, WIDTH), bf16),
        compiler_params=params(),
        cost_estimate=cost(15),
        name="expert_result",
    )(*[a for a, _ in parts], own, other, after)


def expert_grads_kernel(count, keep, *refs):
    arrived = refs[:count]
    grads = refs[count : 2 * count]
    hidden = refs[2 * count : 3 * count]
    pre = refs[3 * count : 4 * count]
    arrived_t = refs[-1]
    starts = starts_of([ref.shape[0] for ref in arrived])

    @pl.when(pl.program_id(0) == 0)
    def _():
        for chunk in range(count):
            arrived_t[:, starts[chunk] : starts[chunk + 1]] = arrived[chunk][...].T

    total_in, total_out = None, None
    for chunk in range(count):
        part_in = dot(arrived_t[:, starts[chunk] : starts[chunk + 1]], pre[chunk][...])
        part_out = dot_tn(hidden[chunk][...], grads[chunk][...].reshape(-1, WIDTH))
        total_in = part_in if total_in is None else total_in + part_in
        total_out = part_out if total_out is None else total_out + part_out
    if keep:
        peer_ref, in_ref, out_ref = refs[4 * count : -1]
        in_ref[...] = total_in + peer_ref[0, 0].astype(f32)
        out_ref[...] = total_out + peer_ref[0, 1].astype(f32)
    else:
        out_ref = refs[4 * count]
        out_ref[0, 0] = total_in.astype(bf16)
        out_ref[0, 1] = total_out.astype(bf16)


def expert_grads(arrived, grads, hidden, pre, units, peer=None):
    count = len(arrived)
    experts, capacity, _ = grads.shape
    shares = shares_of(capacity)
    keep = peer is not None

    def part(chunk):
        place = sum(shares[:chunk]) // shares[chunk]
        return pl.BlockSpec((experts, shares[chunk], WIDTH), lambda i: (0, place, 0), **ONCE)

    steps = units // WIDTH
    wide = [
        pl.BlockSpec((a.shape[0], WIDTH), lambda i, shift=column * steps: (0, i + shift)) for a, column in hidden
    ]
    full = [pl.BlockSpec(a.shape, lambda i: (0, 0), **ONCE) for a in arrived]
    square = pl.BlockSpec((1, 2, WIDTH, WIDTH), lambda i: (i, 0, 0, 0))
    if keep:
        out_specs = [
            pl.BlockSpec((WIDTH, WIDTH), lambda i: (0, i)),
            pl.BlockSpec((WIDTH, WIDTH), lambda i: (i, 0)),
        ]
        out_shape = [
            jax.ShapeDtypeStruct((WIDTH, units), f32),
            jax.ShapeDtypeStruct((units, WIDTH), f32),
        ]
    else:
        out_specs = square
        out_shape = jax.ShapeDtypeStruct((steps, 2, WIDTH, WIDTH), bf16)
    return pl.pallas_call(
        functools.partial(expert_grads_kernel, count, keep),
        grid=(steps,),
        in_specs=[*full, *[part(c) for c in range(count)], *wide, *wide] + ([square] if keep else []),
        out_specs=out_specs,
        out_shape=out_shape,
        scratch_shapes=[pltpu.VMEM((WIDTH, experts * capacity), bf16)],
        compiler_params=params(),
        cost_estimate=cost(1 if keep else 17),
        name="expert_grads_kept" if keep else "expert_grads_sent",
    )(*arrived, *[grads] * count, *[a for a, _ in hidden], *[a for a, _ in pre], *([peer] if keep else []))


def backward_kernel(
    experts,
    capacity,
    scalars,
    x_ref,
    cot_ref,
    middle_ref,
    first_ref,
    second_ref,
    slot_ref,
    segment_ref,
    *refs,
):
    weight_refs = refs[:10]
    packed_ref, context_ref, logsum_ref, _ = refs[10:14]
    kept_refs, sent_refs, grad_input_ref = refs[14:16], refs[16:18], refs[18]
    (
        grad_middle,
        grad_branch,
        turned,
        arranged,
        grad_context,
        query_seg,
        key_seg,
        sums,
        all_probs,
        all_scores,
        queries_pair,
        keys_pair,
        upstream_pair,
        grad_packed,
        mixing,
        output,
        norm_tall,
        norms,
    ) = refs[19:]
    step = pl.program_id(0)
    base = scalars[1]
    kept_rows = HALF

    @pl.when(step == 0)
    def _():
        load_norms(base, weight_refs[8:], norm_tall, norms)
        load_pairs(base, weight_refs[4:8], output)
        query_seg[...], key_seg[...] = segment_terms(segment_ref[...])
        slots = chunked(slot_ref[...], capacity, experts)
        gain_sum = jnp.zeros((1, WIDTH), f32)
        shift_sum = jnp.zeros((1, WIDTH), f32)
        for start in range(0, SEQ_LEN, BLOCK):
            stop = start + BLOCK
            upstream = combine(slots, (first_ref, second_ref), start, BLOCK)
            scaled, inverse = normalize(middle_ref[start:stop])
            result = cot_ref[0, start:stop].astype(f32) + norm_backward(upstream, scaled, inverse, norms[1:2])
            grad_middle[start:stop] = result
            grad_branch[start:stop] = result.astype(bf16)
            turned[:, start:stop] = result.T.astype(bf16)
            gain_sum += jnp.sum(upstream * scaled, axis=0, keepdims=True)
            shift_sum += jnp.sum(upstream, axis=0, keepdims=True)
        sums[1:2] = gain_sum
        sums[3:4] = shift_sum
        grad_context[...] = dot(grad_branch[...], output[...]).astype(bf16)
        rearrange(base, turned, arranged)
        grads = dot(arranged[...], context_ref[...]).astype(bf16)
        for side in range(2):
            part = grads[:, side * HALF : (side + 1) * HALF]
            kept_refs[side][:, TRIPLE : 4 * HALF] = part[:kept_rows]
            sent_refs[side][:, TRIPLE : 4 * HALF] = part[kept_rows:]

    columns = pl.ds(pl.multiple_of(step * PAIR, PAIR), PAIR)
    pair_grad = grad_context[:, columns]
    inner = pair_grad.astype(f32) * context_ref[:, columns].astype(f32)
    query = packed_ref[:, :PAIR]
    keys = packed_ref[:, PAIR : 2 * PAIR]
    keys_wide = jnp.concatenate([keys, key_seg[...]], axis=1)
    lane = iota((SEQ_LEN, PAIR), 1)
    ones = ((lane >= SEGMENTS) & (lane < SEGMENTS + 3)).astype(f32).astype(bf16)
    values_wide = jnp.concatenate([packed_ref[:, 2 * PAIR :], ones], axis=1)
    logs = jnp.concatenate([logsum_ref[0], jnp.zeros((6, SEQ_LEN), f32)], axis=0).T
    for head in range(2):
        first_row = head * SEQ_LEN
        mask = head_mask(head)
        own = query * (mask * HEAD_DIM**-0.5).astype(bf16)
        upstream = pair_grad * mask.astype(bf16)
        queries_pair[first_row : first_row + SEQ_LEN] = own
        upstream_pair[first_row : first_row + SEQ_LEN] = upstream
        keys_pair[first_row : first_row + SEQ_LEN] = keys * mask.astype(bf16)
        delta = jnp.sum(inner * mask, axis=1, keepdims=True)
        own_wide = jnp.concatenate([own, minus(lane, logs[:, head : head + 1], query_seg[...])], axis=1)
        upstream_wide = jnp.concatenate([upstream, minus(lane, delta, jnp.zeros((SEQ_LEN, PAIR), f32))], axis=1)
        for start in range(0, SEQ_LEN, BLOCK):
            stop = start + BLOCK
            column = first_row + start
            for first, last in [(start, stop)] + ([(0, start)] if start else []):
                probs = jnp.exp(dot_nt(keys_wide[first:last], own_wide[start:stop]))
                if first == start:
                    probs = jnp.where(iota(probs.shape, 0) <= iota(probs.shape, 1), probs, 0.0)
                grad_probs = dot_nt(values_wide[first:last], upstream_wide[start:stop])
                all_probs[first:last, column : column + BLOCK] = probs.astype(bf16)
                all_scores[first:last, column : column + BLOCK] = (probs * grad_probs).astype(bf16)
    for start in range(0, SEQ_LEN, BLOCK):
        stop = start + BLOCK
        grad_query, grad_key, grad_value = None, None, None
        for head in range(2):
            first_row = head * SEQ_LEN
            later = slice(first_row + start, first_row + SEQ_LEN)
            column = first_row + start
            part_value = dot(all_probs[start:stop, later], upstream_pair[later])
            part_key = dot(all_scores[start:stop, later], queries_pair[later])
            part_query = dot_tn(all_scores[:stop, column : column + BLOCK], keys_pair[first_row : first_row + stop])
            grad_value = part_value if grad_value is None else grad_value + part_value
            grad_key = part_key if grad_key is None else grad_key + part_key
            grad_query = part_query if grad_query is None else grad_query + part_query
        grad_packed[start:stop, pair_columns(step, 0)] = (grad_query * (HEAD_DIM**-0.5)).astype(bf16)
        grad_packed[start:stop, pair_columns(step, 1)] = grad_key.astype(bf16)
        grad_packed[start:stop, pair_columns(step, 2)] = grad_value.astype(bf16)

    @pl.when(step == pl.num_programs(0) - 1)
    def _():
        load_pairs(base, weight_refs[:4], mixing)
        gain_sum = jnp.zeros((1, WIDTH), f32)
        shift_sum = jnp.zeros((1, WIDTH), f32)
        for start in range(0, SEQ_LEN, BLOCK):
            stop = start + BLOCK
            upstream = dot_nt(grad_packed[start:stop], mixing[...])
            scaled, inverse = normalize(x_ref[0, start:stop].astype(f32))
            result = grad_middle[start:stop] + norm_backward(upstream, scaled, inverse, norms[0:1])
            grad_input_ref[start:stop] = result.astype(bf16)
            normed = scaled * norms[0:1] + norms[2:3]
            turned[:, start:stop] = normed.T.astype(bf16)
            gain_sum += jnp.sum(upstream * scaled, axis=0, keepdims=True)
            shift_sum += jnp.sum(upstream, axis=0, keepdims=True)
        rearrange(base, turned, arranged)
        for side in range(2):
            part = dot(arranged[...], grad_packed[:, side * TRIPLE : (side + 1) * TRIPLE]).astype(bf16)
            kept_refs[side][:, :TRIPLE] = part[:kept_rows]
            sent_refs[side][:, :TRIPLE] = part[kept_rows:]
        sums[0:1] = gain_sum
        sums[2:3] = shift_sum
        sums[4:8] = jnp.zeros((4, WIDTH), f32)
        tall = jnp.concatenate([sums[...], jnp.zeros((PAIR - 8, WIDTH), f32)], axis=0)
        turned[:, :PAIR] = tall.T.astype(bf16)
        rearrange(base, turned.at[:, :PAIR], arranged.at[:, :PAIR])
        kept_refs[0][:, 4 * HALF :] = arranged[:kept_rows, :PAIR]
        sent_refs[0][:, 4 * HALF :] = arranged[kept_rows:, :PAIR]


def backward(scalars, inputs, cotangent, middle, back, slot_col, segment_col, weights, packed, context, logsums, after, experts, capacity):
    pairs = WIDTH // PAIR
    rows = back[0].shape[0]
    one = lambda i, place: (place[0], 0, 0)
    full = whole((SEQ_LEN, WIDTH))
    once = pl.BlockSpec((SEQ_LEN, WIDTH), lambda i, _: (0, 0), **ONCE)
    columns = [4 * HALF + PAIR, 4 * HALF] * 2
    return pl.pallas_call(
        functools.partial(backward_kernel, experts, capacity),
        grid_spec=pltpu.PrefetchScalarGridSpec(
            num_scalar_prefetch=1,
            grid=(pairs,),
            in_specs=[
                pl.BlockSpec((1, SEQ_LEN, WIDTH), one, **ONCE),
                pl.BlockSpec((1, SEQ_LEN, WIDTH), one, **ONCE),
                once,
                *[pl.BlockSpec(b.shape, lambda i, _: (0, 0), **ONCE) for b in back],
                whole((SEQ_LEN, 1)),
                whole((SEQ_LEN, 1)),
                *weight_specs(),
                pl.BlockSpec((SEQ_LEN, 3 * PAIR), lambda i, _: (0, i)),
                once,
                pl.BlockSpec((1, 2, SEQ_LEN), lambda i, _: (i, 0, 0)),
                ANY,
            ],
            out_specs=[
                *[pl.BlockSpec((HALF, c), lambda i, _: (0, 0), **ONCE) for c in columns],
                pl.BlockSpec((SEQ_LEN, WIDTH), lambda i, _: (0, 0), **ONCE),
            ],
            scratch_shapes=[
                pltpu.VMEM((SEQ_LEN, WIDTH), f32),
                pltpu.VMEM((SEQ_LEN, WIDTH), bf16),
                pltpu.VMEM((WIDTH, SEQ_LEN), bf16),
                pltpu.VMEM((WIDTH, SEQ_LEN), bf16),
                pltpu.VMEM((SEQ_LEN, WIDTH), bf16),
                pltpu.VMEM((SEQ_LEN, PAIR), bf16),
                pltpu.VMEM((SEQ_LEN, PAIR), bf16),
                pltpu.VMEM((8, WIDTH), f32),
                pltpu.VMEM((SEQ_LEN, 2 * SEQ_LEN), bf16),
                pltpu.VMEM((SEQ_LEN, 2 * SEQ_LEN), bf16),
                pltpu.VMEM((2 * SEQ_LEN, PAIR), bf16),
                pltpu.VMEM((2 * SEQ_LEN, PAIR), bf16),
                pltpu.VMEM((2 * SEQ_LEN, PAIR), bf16),
                pltpu.VMEM((SEQ_LEN, 3 * WIDTH), bf16),
                pltpu.VMEM((WIDTH, 3 * WIDTH), bf16),
                pltpu.VMEM((WIDTH, WIDTH), bf16),
                pltpu.VMEM((WIDTH, PAIR), bf16),
                pltpu.VMEM((8, WIDTH), f32),
            ],
        ),
        out_shape=[
            *[jax.ShapeDtypeStruct((HALF, c), bf16) for c in columns],
            jax.ShapeDtypeStruct((SEQ_LEN, WIDTH), bf16),
        ],
        compiler_params=params(),
        cost_estimate=cost(50),
        name="attention_backward",
    )(
        scalars,
        inputs,
        cotangent,
        middle,
        *back,
        slot_col,
        segment_col,
        *weight_arrays(weights),
        packed,
        context,
        logsums,
        after,
    )


def result_kernel(middle_ref, slot_ref, back_ref, out_ref):
    routed = combine(slot_ref[...], (back_ref,), 0, BLOCK)
    out_ref[...] = (middle_ref[...] + routed).astype(bf16)


def result(middle, slot_col, back):
    rows = back.shape[0]
    tile = pl.BlockSpec((BLOCK, WIDTH), lambda i: (i, 0))
    return pl.pallas_call(
        result_kernel,
        grid=(SEQ_LEN // BLOCK,),
        in_specs=[
            tile,
            pl.BlockSpec((BLOCK, 1), lambda i: (i, 0)),
            whole((rows, WIDTH)),
        ],
        out_specs=tile,
        out_shape=jax.ShapeDtypeStruct((SEQ_LEN, WIDTH), bf16),
        compiler_params=params(),
        cost_estimate=cost(8),
        name="result",
    )(middle, slot_col, back)


def swap(values):
    return lax.ppermute(values, "tensor", [(0, 1), (1, 0)])


def exchange(values, experts):
    shape = values.shape
    parts = values.reshape(experts, shape[0] // experts, shape[1])
    return lax.all_to_all(parts, "dp", split_axis=0, concat_axis=0, tiled=True).reshape(shape)


def both(place, values, other):
    first = place == 0
    return jnp.stack([jnp.where(first, values, other), jnp.where(first, other, values)])


def flip(values, bit):
    size = lax.axis_size("dp")
    return lax.ppermute(values, "dp", [(i, i ^ bit) for i in range(size)])


def after(values, *others):
    return lax.optimization_barrier((values, *others))[0]


def rows_of(parts):
    return jnp.concatenate(parts, axis=0)


def fetch_by_halves(shard):
    own = shard
    for bit in (8, 4):
        own = rows_of([own, flip(own, bit)])
    middle = own.shape[0] // 2
    first, second = own[:middle], own[middle:]
    first_peer, second_next = swap(first), flip(second, 2)
    first_next = flip(rows_of([first, first_peer]), 2)
    second_peer = swap(rows_of([second, second_next]))
    near = rows_of([first, first_next[:middle], second, second_next])
    near_peer = rows_of([first_peer, first_next[middle:], second_peer])
    return near, flip(near, 1), near_peer, flip(near_peer, 1)


def fetch_whole(shard):
    own = lax.all_gather(rows_of([shard, swap(shard)]), "dp", axis=0, tiled=True)
    own = own.reshape(-1, 2, shard.shape[0], shard.shape[1]).transpose(1, 0, 2, 3).reshape(2, -1, SLAB, shard.shape[1])
    return tuple(rows_of([own[side, o ^ far] for o in OFFSETS]) for side in (0, 1) for far in (0, 1))


def pool_by_halves(kept, sent, peer, output, grad_peer):
    size = lax.axis_size("dp")
    groups = [[high * 4 + low for high in range(size // 4)] for low in range(4)]
    totals = [None, None]
    for side in (1, 0):
        near = (kept[side].astype(f32) + after(flip(sent[side], 1), peer).astype(f32)).astype(bf16)
        middle = near.shape[0] // 2
        near = (near[:middle].astype(f32) + after(flip(near[middle:], 2), *([] if side else [grad_peer])).astype(f32)).astype(bf16)
        parts = after(near, output).reshape(size // 4, SLAB, -1)
        parts = lax.all_to_all(parts, "dp", split_axis=0, concat_axis=0, tiled=True, axis_index_groups=groups)
        totals[side] = jnp.sum(parts.astype(f32), axis=0)
    return totals


def pool_whole(kept, sent):
    totals = []
    for side in range(2):
        full = jnp.concatenate([kept[side], sent[side]], axis=0)
        full = full.reshape(2, 2, 4, SLAB, -1).transpose(2, 1, 0, 3, 4).reshape(WIDTH, -1)
        totals.append(lax.psum_scatter(full, "dp", scatter_dimension=0, tiled=True).astype(f32))
    return totals


def body(
    inputs,
    qkv_weight,
    out_weight,
    norm_gains,
    norm_shifts,
    expert_in,
    expert_out,
    token_ids,
    hash_table,
    segment_ids,
    cotangent,
):
    place = lax.axis_index("tensor")
    experts = lax.axis_size("dp")
    by_halves = experts * SLAB == WIDTH
    base = lax.axis_index("dp") if by_halves else jnp.zeros((), jnp.int32)
    places = jnp.stack([place, base]).astype(jnp.int32)
    capacity = 2 * SEQ_LEN // experts
    depth = qkv_weight.shape[0]
    half = qkv_weight.shape[2]

    norms = jnp.concatenate([norm_gains, norm_shifts], axis=0).T
    norms = jnp.pad(norms, ((0, 0), (0, PAIR - norms.shape[1])))
    shard = jnp.concatenate([qkv_weight.reshape(depth, 3 * half), out_weight, norms], axis=1)
    weights = fetch_by_halves(shard) if by_halves else fetch_whole(shard)

    in_own, out_own = expert_in[0], expert_out[0]
    out_other = swap(after(out_own, weights[2]))
    in_other = swap(after(in_own, weights[2]))

    ids = lax.dynamic_index_in_dim(token_ids, place, 0, keepdims=False)
    chosen = jnp.take(hash_table, ids, axis=0)
    segment_col = lax.dynamic_index_in_dim(segment_ids, place, 0, keepdims=False).reshape(SEQ_LEN, 1)
    sent, slot_row, slot_col = route(places, chosen, cotangent, experts, capacity)
    grads = exchange(sent, experts)

    packed, context, logsums, middle, first, second = forward(
        places, inputs, weights, segment_col, slot_row, slot_col, experts, capacity
    )
    upstream = grad_hidden(grads, [out_own, out_other], first)
    second, upstream = lax.optimization_barrier((second, upstream))
    arrived = [exchange(first, experts), exchange(second, experts)]
    upstream = upstream.reshape(experts, capacity, -1)
    grads = grads.reshape(experts, capacity, WIDTH)
    done = [expert(a, upstream, in_own, in_other, c) for c, a in enumerate(arrived)]
    hidden = [d[0] for d in done]
    pre = [d[1] for d in done]
    sent = expert_grads(arrived, grads, [h[1] for h in hidden], [p[1] for p in pre], in_own.shape[1])
    back = [exchange(done[0][2], experts), exchange(after(done[1][2], sent), experts)]
    peer = swap(sent)
    routed_send = expert_result(hidden, out_own, out_other, sent, experts)
    routed = exchange(routed_send.reshape(experts * capacity, WIDTH), experts)

    kept_own, kept_other, sent_own, sent_other, grad_own = backward(
        places, inputs, cotangent, middle, back, slot_col, segment_col, weights, packed, context, logsums,
        routed_send, experts, capacity
    )
    kept, sent_rows = (kept_own, kept_other), (sent_own, sent_other)
    output = result(middle, slot_col, routed)
    grad_peer, output_peer = swap(grad_own), swap(output)
    if by_halves:
        pooled, pooled_peer = pool_by_halves(kept, sent_rows, peer, output, grad_peer)
    else:
        pooled, pooled_peer = pool_whole(kept, sent_rows)
    shared = jnp.concatenate([pooled_peer, pooled[:, 4 * half :]], axis=1).astype(bf16)
    owned = pooled + swap(after(shared, output_peer)).astype(f32)
    grad_qkv = owned[:, : 3 * half].reshape(depth, 3, half)
    grad_out = owned[:, 3 * half : 4 * half]
    grad_norm = owned[:, 4 * half : 4 * half + 4].T
    grad_expert_in, grad_expert_out = expert_grads(
        arrived, grads, [h[0] for h in hidden], [p[0] for p in pre], in_own.shape[1], peer
    )

    return (
        both(place, output, output_peer),
        both(place, grad_own, grad_peer),
        grad_qkv,
        grad_out,
        grad_norm[:2],
        grad_norm[2:],
        grad_expert_in[None],
        grad_expert_out[None],
    )


def solution(mesh):
    return jax.shard_map(
        body,
        mesh=mesh,
        in_specs=(
            P("dp", None, None),
            P("dp", None, "tensor"),
            P("dp", "tensor"),
            P(None, "dp"),
            P(None, "dp"),
            P("dp", None, "tensor"),
            P("dp", "tensor", None),
            P("dp", None),
            P(),
            P("dp", None),
            P("dp", None, None),
        ),
        out_specs=(
            P("dp", None, None),
            P("dp", None, None),
            P("dp", None, "tensor"),
            P("dp", "tensor"),
            P(None, "dp"),
            P(None, "dp"),
            P("dp", None, "tensor"),
            P("dp", "tensor", None),
        ),
        check_vma=False,
    )
```

```python
import functools

import jax
import jax.numpy as jnp
from jax import lax
from jax.experimental import pallas as pl
from jax.experimental.pallas import tpu as pltpu
from jax.sharding import PartitionSpec as P

HEAD_DIM = 64
SEQ_LEN = 1024
WIDTH = 768
PAIR = 128
BLOCK = 256
EPSILON = 1e-05
MASKED = -1e30
SEGMENTS = 4
SLAB = 48
OFFSETS = (0, 8, 2, 10, 4, 12, 6, 14)
VMEM = 60 * 1024 * 1024

f32 = jnp.float32
bf16 = jnp.bfloat16


def dot(a, b):
    return jnp.dot(a, b, preferred_element_type=f32)


def dot_nt(a, b):
    return lax.dot_general(a, b, (((1,), (1,)), ((), ())), preferred_element_type=f32)


def dot_tn(a, b):
    return lax.dot_general(a, b, (((0,), (0,)), ((), ())), preferred_element_type=f32)


def iota(shape, dim):
    return lax.broadcasted_iota(jnp.int32, shape, dim)


def params(axes=1):
    return pltpu.CompilerParams(
        dimension_semantics=("arbitrary",) * axes, vmem_limit_bytes=VMEM
    )


def cost(microseconds):
    return pl.CostEstimate(flops=int(microseconds * 1.1e9), bytes_accessed=1 << 20, transcendentals=0)


def whole(shape):
    zeros = (0,) * len(shape)
    return pl.BlockSpec(shape, lambda *_: zeros)


def normalize(values):
    centred = values - jnp.mean(values, axis=-1, keepdims=True)
    variance = jnp.mean(centred * centred, axis=-1, keepdims=True)
    inverse = lax.rsqrt(variance + EPSILON)
    return centred * inverse, inverse


def norm_backward(upstream, scaled, inverse, gain):
    weighted = upstream * gain
    inner = jnp.mean(weighted * scaled, axis=-1, keepdims=True)
    centred = weighted - jnp.mean(weighted, axis=-1, keepdims=True)
    return inverse * (centred - scaled * inner)


def slab(number):
    return pl.ds(pl.multiple_of(number * SLAB, SLAB), SLAB)


def assemble(base, near_ref, far_ref, out_ref):
    for ref, flip in ((near_ref, 0), (far_ref, 1)):
        for j, offset in enumerate(OFFSETS):
            out_ref[slab(base ^ offset ^ flip), :] = ref[j * SLAB : (j + 1) * SLAB, :]


def load_pairs(base, refs, out_ref):
    width = out_ref.shape[1] // 2
    for side in range(2):
        assemble(base, refs[2 * side], refs[2 * side + 1], out_ref.at[:, side * width : (side + 1) * width])


def load_norms(base, refs, tall_ref, out_ref):
    assemble(base, *refs, tall_ref)
    out_ref[...] = tall_ref[...].astype(f32).T[:8]


ONCE = dict(pipeline_mode=pl.Buffered(1))
HALF = WIDTH // 2
TRIPLE = 3 * HALF


def weight_specs():
    mixing = pl.BlockSpec((HALF, TRIPLE), lambda *_: (0, 0), **ONCE)
    output = pl.BlockSpec((HALF, HALF), lambda *_: (0, 3), **ONCE)
    norm = pl.BlockSpec((HALF, PAIR), lambda *_: (0, 4 * HALF // PAIR), **ONCE)
    return [mixing] * 4 + [output] * 4 + [norm] * 2


def weight_arrays(parts):
    return [*parts, *parts, parts[0], parts[1]]


def pair_columns(step, kind):
    pairs = HALF // PAIR
    return pl.ds(pl.multiple_of((step // pairs) * TRIPLE + kind * HALF + (step % pairs) * PAIR, PAIR), PAIR)


def rearrange(base, from_ref, out_ref):
    place = 0
    for low in range(2):
        for next_low in range(2):
            for high in range(4):
                number = (high << 2) | ((base ^ (next_low << 1) ^ low) & 3)
                out_ref[place : place + SLAB] = from_ref[slab(number), :]
                place += SLAB


def dispatch(slot_row, values, out_refs):
    base = 0
    for out_ref in out_refs:
        rows = out_ref.shape[0]
        for start in range(0, rows, BLOCK):
            pick = (iota((BLOCK, SEQ_LEN), 0) + (base + start) == slot_row).astype(f32).astype(bf16)
            out_ref[start : start + BLOCK] = dot(pick, values).astype(bf16)
        base += rows


def shares_of(capacity):
    return capacity // 2, capacity // 2


def chunked(slot, capacity, experts):
    first, second = shares_of(capacity)
    expert = slot // capacity
    rank = slot - expert * capacity
    late = experts * first + expert * second + rank - first
    return jnp.where(rank < first, expert * first + rank, late)


def combine(slot_col, back_refs, start, size):
    total, base = None, 0
    for back_ref in back_refs:
        rows = back_ref.shape[0]
        pick = (iota((size, rows), 1) + base == slot_col[start : start + size]).astype(f32)
        part = dot(pick.astype(bf16), back_ref[...])
        total = part if total is None else total + part
        base += rows
    return total


def route_kernel(experts, capacity, _, row_ref, col_ref, cot_ref, out_ref, slot_row_ref, slot_col_ref):
    row = row_ref[...]
    hot = (iota((experts, SEQ_LEN), 0) == row).astype(f32)
    order = (iota((SEQ_LEN, SEQ_LEN), 0) <= iota((SEQ_LEN, SEQ_LEN), 1)).astype(f32).astype(bf16)
    seen = dot(hot.astype(bf16), order)
    rank = jnp.sum(seen * hot, axis=0, keepdims=True).astype(jnp.int32) - 1
    slot_row = row * capacity + rank
    slot_row_ref[...] = slot_row
    col = col_ref[...]
    hot_col = (iota((SEQ_LEN, experts), 1) == col).astype(f32)
    seen_col = dot_tn(order, hot_col.astype(bf16))
    rank_col = jnp.sum(seen_col * hot_col, axis=1, keepdims=True).astype(jnp.int32) - 1
    slot_col_ref[...] = col * capacity + rank_col
    dispatch(slot_row, cot_ref[0], (out_ref,))


def route(tensor_place, chosen, cotangent, experts, capacity):
    rows = experts * capacity
    one = lambda i, place: (place[0], 0, 0)
    return pl.pallas_call(
        functools.partial(route_kernel, experts, capacity),
        grid_spec=pltpu.PrefetchScalarGridSpec(
            num_scalar_prefetch=1,
            grid=(1,),
            in_specs=[
                whole((1, SEQ_LEN)),
                whole((SEQ_LEN, 1)),
                pl.BlockSpec((1, SEQ_LEN, WIDTH), one),
            ],
            out_specs=[
                whole((rows, WIDTH)),
                whole((1, SEQ_LEN)),
                whole((SEQ_LEN, 1)),
            ],
        ),
        out_shape=[
            jax.ShapeDtypeStruct((rows, WIDTH), bf16),
            jax.ShapeDtypeStruct((1, SEQ_LEN), jnp.int32),
            jax.ShapeDtypeStruct((SEQ_LEN, 1), jnp.int32),
        ],
        compiler_params=params(),
        cost_estimate=cost(7),
        name="route",
    )(tensor_place, chosen.reshape(1, SEQ_LEN), chosen.reshape(SEQ_LEN, 1), cotangent)


def segment_terms(segment_col):
    lane = iota((SEQ_LEN, PAIR), 1)
    query = jnp.where((lane != segment_col) & (lane < SEGMENTS), MASKED, 0.0).astype(bf16)
    key = (lane == segment_col) | ((lane >= SEGMENTS) & (lane < SEGMENTS + 3))
    return query, key.astype(f32).astype(bf16)


def minus(lane, column, others):
    result = others.astype(f32)
    for place in range(SEGMENTS, SEGMENTS + 3):
        part = column.astype(bf16).astype(f32)
        result = jnp.where(lane == place, -part, result)
        column = column - part
    return result.astype(bf16)


def causal(block):
    return jnp.where(iota(block.shape, 0) <= iota(block.shape, 1), block, MASKED)


def head_mask(head):
    lane = iota((1, PAIR), 1)
    mine = (lane >= head * HEAD_DIM) & (lane < (head + 1) * HEAD_DIM)
    return mine.astype(f32)


def forward_kernel(
    experts,
    capacity,
    scalars,
    x_ref,
    *refs,
):
    weight_refs = refs[:10]
    segment_ref, slot_ref, _, packed_ref, context_ref, logsum_ref, middle_ref, first_ref, second_ref = refs[10:19]
    normed, all_packed, all_context, query_seg, key_seg, context_t, mixing, output, norm_tall, norms = refs[19:]
    step = pl.program_id(0)
    base = scalars[1]

    @pl.when(step == 0)
    def _():
        load_norms(base, weight_refs[8:], norm_tall, norms)
        load_pairs(base, weight_refs[:4], mixing)
        for start in range(0, SEQ_LEN, BLOCK):
            scaled, _ = normalize(x_ref[0, start : start + BLOCK].astype(f32))
            normed[start : start + BLOCK] = (scaled * norms[0:1] + norms[2:3]).astype(bf16)
        for side in range(2):
            columns = slice(side * TRIPLE, (side + 1) * TRIPLE)
            all_packed[:, columns] = dot(normed[...], mixing[:, columns]).astype(bf16)
        query_seg[...], key_seg[...] = segment_terms(segment_ref[...])

    query, key, value = [all_packed[:, pair_columns(step, kind)] for kind in range(3)]
    packed_ref[:, :PAIR] = query
    packed_ref[:, PAIR : 2 * PAIR] = key
    packed_ref[:, 2 * PAIR :] = value
    keys = jnp.concatenate([key, key_seg[...]], axis=1)
    values_t = value.T
    for head in range(2):
        low, high = head * HEAD_DIM, (head + 1) * HEAD_DIM
        own = query * (head_mask(head) * HEAD_DIM**-0.5).astype(bf16)
        own = jnp.concatenate([own, query_seg[...]], axis=1)
        for start in range(0, SEQ_LEN, BLOCK):
            stop = start + BLOCK
            block = own[start:stop]
            near = causal(dot_nt(keys[start:stop], block))
            highest = jnp.max(near, axis=0, keepdims=True)
            if start:
                far = dot_nt(keys[:start], block)
                highest = jnp.maximum(highest, jnp.max(far, axis=0, keepdims=True))
            near = jnp.exp(near - highest)
            total = jnp.sum(near, axis=0, keepdims=True)
            result = dot(values_t[low:high, start:stop], near.astype(bf16))
            if start:
                far = jnp.exp(far - highest)
                total = total + jnp.sum(far, axis=0, keepdims=True)
                result = result + dot(values_t[low:high, :start], far.astype(bf16))
            context_t[low:high, start:stop] = result * (1.0 / total)
            logsum_ref[0, head : head + 1, start:stop] = highest + jnp.log(total)
    context = context_t[...].T.astype(bf16)
    context_ref[...] = context
    all_context[:, pl.ds(pl.multiple_of(step * PAIR, PAIR), PAIR)] = context

    @pl.when(step == pl.num_programs(0) - 1)
    def _():
        load_pairs(base, weight_refs[4:8], output)
        slots = chunked(slot_ref[...], capacity, experts)
        for start in range(0, SEQ_LEN, BLOCK):
            stop = start + BLOCK
            middle = x_ref[0, start:stop].astype(f32) + dot_nt(all_context[start:stop], output[...])
            middle_ref[start:stop] = middle
            scaled, _ = normalize(middle)
            normed[start:stop] = (scaled * norms[1:2] + norms[3:4]).astype(bf16)
        dispatch(slots, normed[...], (first_ref, second_ref))


def forward(scalars, inputs, weights, segment_col, slot_row, after, experts, capacity):
    first, second = [experts * share for share in shares_of(capacity)]
    pairs = WIDTH // PAIR
    one = lambda i, place: (place[0], 0, 0)
    return pl.pallas_call(
        functools.partial(forward_kernel, experts, capacity),
        grid_spec=pltpu.PrefetchScalarGridSpec(
            num_scalar_prefetch=1,
            grid=(pairs,),
            in_specs=[
                pl.BlockSpec((1, SEQ_LEN, WIDTH), one, **ONCE),
                *weight_specs(),
                whole((SEQ_LEN, 1)),
                whole((1, SEQ_LEN)),
                pl.BlockSpec(memory_space=pl.ANY),
            ],
            out_specs=[
                pl.BlockSpec((SEQ_LEN, 3 * PAIR), lambda i, _: (0, i)),
                pl.BlockSpec((SEQ_LEN, PAIR), lambda i, _: (0, i)),
                pl.BlockSpec((1, 2, SEQ_LEN), lambda i, _: (i, 0, 0)),
                whole((SEQ_LEN, WIDTH)),
                whole((first, WIDTH)),
                whole((second, WIDTH)),
            ],
            scratch_shapes=[
                pltpu.VMEM((SEQ_LEN, WIDTH), bf16),
                pltpu.VMEM((SEQ_LEN, 3 * WIDTH), bf16),
                pltpu.VMEM((SEQ_LEN, WIDTH), bf16),
                pltpu.VMEM((SEQ_LEN, PAIR), bf16),
                pltpu.VMEM((SEQ_LEN, PAIR), bf16),
                pltpu.VMEM((PAIR, SEQ_LEN), f32),
                pltpu.VMEM((WIDTH, 3 * WIDTH), bf16),
                pltpu.VMEM((WIDTH, WIDTH), bf16),
                pltpu.VMEM((WIDTH, PAIR), bf16),
                pltpu.VMEM((8, WIDTH), f32),
            ],
        ),
        out_shape=[
            jax.ShapeDtypeStruct((SEQ_LEN, 3 * WIDTH), bf16),
            jax.ShapeDtypeStruct((SEQ_LEN, WIDTH), bf16),
            jax.ShapeDtypeStruct((pairs, 2, SEQ_LEN), f32),
            jax.ShapeDtypeStruct((SEQ_LEN, WIDTH), f32),
            jax.ShapeDtypeStruct((first, WIDTH), bf16),
            jax.ShapeDtypeStruct((second, WIDTH), bf16),
        ],
        compiler_params=params(),
        cost_estimate=cost(30),
        name="attention_forward",
    )(scalars, inputs, *weight_arrays(weights), segment_col, slot_row, after)


def pick_piece(step, refs, counts):
    ends = starts_of(counts)[1:]
    weight = refs[-1][...]
    for ref, end in reversed(list(zip(refs[:-1], ends[:-1]))):
        weight = jnp.where(step < end, ref[...], weight)
    return weight


def starts_of(counts):
    starts = [0]
    for count in counts:
        starts.append(starts[-1] + count)
    return starts


def piece_specs(shape, dim, counts):
    def at(block):
        return tuple(block if d == dim else 0 for d in range(len(shape)))

    def spec(start, count):
        return pl.BlockSpec(shape, lambda i: at(jnp.clip(i - start, 0, count - 1)))

    return [spec(start, count) for start, count in zip(starts_of(counts), counts)]


UNITS = 512


ANY = pl.BlockSpec(memory_space=pl.ANY)


def grad_hidden_kernel(counts, grad_ref, *refs):
    weight = pick_piece(pl.program_id(0), refs[:-2], counts)
    refs[-1][...] = dot_nt(grad_ref[...], weight).astype(bf16)


def grad_hidden(arrived, pieces, after):
    rows = arrived.shape[0]
    counts = [piece.shape[0] // UNITS for piece in pieces]
    return pl.pallas_call(
        functools.partial(grad_hidden_kernel, counts),
        grid=(sum(counts),),
        in_specs=[whole((rows, WIDTH))] + piece_specs((UNITS, WIDTH), 0, counts) + [ANY],
        out_specs=pl.BlockSpec((rows, UNITS), lambda i: (0, i)),
        out_shape=jax.ShapeDtypeStruct((rows, sum(counts) * UNITS), bf16),
        compiler_params=params(),
        cost_estimate=cost(15),
        name="grad_hidden",
    )(arrived, *pieces, after)


def expert_kernel(resumed, counts, rows_ref, grad_ref, *refs):
    weight_refs, refs = refs[: len(counts)], refs[len(counts) :]
    hidden_ref, pre_ref, back_ref, total = refs[1:] if resumed else refs
    step = pl.program_id(0)
    weight = pick_piece(step, weight_refs, counts)
    root = 0.7978845608028654
    cube = 0.044715

    @pl.when(step == 0)
    def _():
        total[...] = refs[0][...] if resumed else jnp.zeros_like(total)

    rows = rows_ref.shape[0]
    before = dot(rows_ref[...], weight)
    upstream = grad_ref[...].reshape(rows, EXPERT_UNITS).astype(f32)
    square = before * before
    inner = root + (root * cube) * square
    tanh = jnp.tanh(before * inner)
    hidden = before * (0.5 + 0.5 * tanh)
    hidden_ref[...] = hidden.astype(bf16)
    slope = 0.5 + 0.5 * tanh + (hidden - hidden * tanh) * (3.0 * inner - 2.0 * root)
    grad_pre = (upstream * slope).astype(bf16)
    pre_ref[...] = grad_pre
    total[...] += dot_nt(grad_pre, weight)

    @pl.when(step == pl.num_programs(0) - 1)
    def _():
        back_ref[...] = total[...].astype(back_ref.dtype)


EXPERT_UNITS = 768


def expert_part(arrived, grads, pieces, chunk, side, partial=None, last=True):
    rows = arrived.shape[0]
    experts, capacity, _ = grads.shape
    shares = shares_of(capacity)
    share = shares[chunk]
    place = sum(shares[:chunk]) // share
    counts = [piece.shape[1] // EXPERT_UNITS for piece in pieces]
    units = sum(piece.shape[1] for piece in pieces)
    start = side * counts[0]
    wide = pl.BlockSpec((rows, EXPERT_UNITS), lambda i: (0, i))
    resumed = partial is not None
    full = pl.BlockSpec((rows, WIDTH), lambda i: (0, 0), **ONCE)
    return pl.pallas_call(
        functools.partial(expert_kernel, resumed, counts),
        grid=(sum(counts),),
        in_specs=[
            full,
            pl.BlockSpec((experts, share, EXPERT_UNITS), lambda i: (0, place, i + start)),
        ]
        + piece_specs((WIDTH, EXPERT_UNITS), 1, counts)
        + ([full] if resumed else []),
        out_specs=[wide, wide, full],
        out_shape=[
            jax.ShapeDtypeStruct((rows, units), bf16),
            jax.ShapeDtypeStruct((rows, units), bf16),
            jax.ShapeDtypeStruct((rows, WIDTH), bf16 if last else f32),
        ],
        scratch_shapes=[pltpu.VMEM((rows, WIDTH), f32)],
        compiler_params=params(),
        cost_estimate=cost(10 * len(pieces)),
        name="expert",
    )(arrived, grads, *pieces, *([partial] if resumed else []))


def expert(arrived, grads, own, other, chunk):
    if chunk:
        hidden, pre, back = expert_part(arrived, grads, [own, other], chunk, 0)
        return ((hidden, 0), (hidden, 1)), ((pre, 0), (pre, 1)), back
    hidden_own, pre_own, partial = expert_part(arrived, grads, [own], chunk, 0, None, False)
    hidden_other, pre_other, back = expert_part(arrived, grads, [other], chunk, 1, partial)
    return ((hidden_own, 0), (hidden_other, 0)), ((pre_own, 0), (pre_other, 0)), back


def expert_out_kernel(first_ref, first_other_ref, second_ref, second_other_ref, own_ref, other_ref, _, out_ref):
    experts = out_ref.shape[0]
    place = 0
    for hidden_ref, other in ((first_ref, first_other_ref), (second_ref, second_other_ref)):
        share = hidden_ref.shape[0] // experts
        total = dot(hidden_ref[...], own_ref[...]) + dot(other[...], other_ref[...])
        out_ref[:, place : place + share] = total.astype(bf16).reshape(experts, share, WIDTH)
        place += share


def expert_result(hidden, own, other, after, experts):
    steps = 4
    units = own.shape[0]
    parts = [part for chunk in hidden for part in chunk]
    tiles = [pl.BlockSpec((a.shape[0] // steps, units), lambda i, column=column: (i, column)) for a, column in parts]
    capacity = sum(chunk[0][0].shape[0] for chunk in hidden) // experts
    weight = pl.BlockSpec(own.shape, lambda i: (0, 0), **ONCE)
    return pl.pallas_call(
        expert_out_kernel,
        grid=(steps,),
        in_specs=[*tiles, weight, weight, ANY],
        out_specs=pl.BlockSpec((experts // steps, capacity, WIDTH), lambda i: (i, 0, 0)),
        out_shape=jax.ShapeDtypeStruct((experts, capacity, WIDTH), bf16),
        compiler_params=params(),
        cost_estimate=cost(15),
        name="expert_result",
    )(*[a for a, _ in parts], own, other, after)


def expert_grads_kernel(count, keep, *refs):
    arrived = refs[:count]
    grads = refs[count : 2 * count]
    hidden = refs[2 * count : 3 * count]
    pre = refs[3 * count : 4 * count]
    arrived_t = refs[-1]
    starts = starts_of([ref.shape[0] for ref in arrived])

    @pl.when(pl.program_id(0) == 0)
    def _():
        for chunk in range(count):
            arrived_t[:, starts[chunk] : starts[chunk + 1]] = arrived[chunk][...].T

    total_in, total_out = None, None
    for chunk in range(count):
        part_in = dot(arrived_t[:, starts[chunk] : starts[chunk + 1]], pre[chunk][...])
        part_out = dot_tn(hidden[chunk][...], grads[chunk][...].reshape(-1, WIDTH))
        total_in = part_in if total_in is None else total_in + part_in
        total_out = part_out if total_out is None else total_out + part_out
    if keep:
        peer_ref, in_ref, out_ref = refs[4 * count : -1]
        in_ref[...] = total_in + peer_ref[0, 0].astype(f32)
        out_ref[...] = total_out + peer_ref[0, 1].astype(f32)
    else:
        out_ref = refs[4 * count]
        out_ref[0, 0] = total_in.astype(bf16)
        out_ref[0, 1] = total_out.astype(bf16)


def expert_grads(arrived, grads, hidden, pre, units, peer=None):
    count = len(arrived)
    experts, capacity, _ = grads.shape
    shares = shares_of(capacity)
    keep = peer is not None

    def part(chunk):
        place = sum(shares[:chunk]) // shares[chunk]
        return pl.BlockSpec((experts, shares[chunk], WIDTH), lambda i: (0, place, 0), **ONCE)

    steps = units // WIDTH
    wide = [
        pl.BlockSpec((a.shape[0], WIDTH), lambda i, shift=column * steps: (0, i + shift)) for a, column in hidden
    ]
    full = [pl.BlockSpec(a.shape, lambda i: (0, 0), **ONCE) for a in arrived]
    square = pl.BlockSpec((1, 2, WIDTH, WIDTH), lambda i: (i, 0, 0, 0))
    if keep:
        out_specs = [
            pl.BlockSpec((WIDTH, WIDTH), lambda i: (0, i)),
            pl.BlockSpec((WIDTH, WIDTH), lambda i: (i, 0)),
        ]
        out_shape = [
            jax.ShapeDtypeStruct((WIDTH, units), f32),
            jax.ShapeDtypeStruct((units, WIDTH), f32),
        ]
    else:
        out_specs = square
        out_shape = jax.ShapeDtypeStruct((steps, 2, WIDTH, WIDTH), bf16)
    return pl.pallas_call(
        functools.partial(expert_grads_kernel, count, keep),
        grid=(steps,),
        in_specs=[*full, *[part(c) for c in range(count)], *wide, *wide] + ([square] if keep else []),
        out_specs=out_specs,
        out_shape=out_shape,
        scratch_shapes=[pltpu.VMEM((WIDTH, experts * capacity), bf16)],
        compiler_params=params(),
        cost_estimate=cost(1 if keep else 17),
        name="expert_grads_kept" if keep else "expert_grads_sent",
    )(*arrived, *[grads] * count, *[a for a, _ in hidden], *[a for a, _ in pre], *([peer] if keep else []))


def backward_kernel(
    experts,
    capacity,
    scalars,
    x_ref,
    cot_ref,
    middle_ref,
    first_ref,
    second_ref,
    slot_ref,
    segment_ref,
    *refs,
):
    weight_refs = refs[:10]
    packed_ref, context_ref, logsum_ref, _ = refs[10:14]
    kept_refs, sent_refs, grad_input_ref = refs[14:16], refs[16:18], refs[18]
    (
        grad_middle,
        grad_branch,
        turned,
        arranged,
        grad_context,
        query_seg,
        key_seg,
        sums,
        all_probs,
        all_scores,
        queries_pair,
        keys_pair,
        upstream_pair,
        grad_packed,
        mixing,
        output,
        norm_tall,
        norms,
    ) = refs[19:]
    step = pl.program_id(0)
    base = scalars[1]
    kept_rows = HALF

    @pl.when(step == 0)
    def _():
        load_norms(base, weight_refs[8:], norm_tall, norms)
        load_pairs(base, weight_refs[4:8], output)
        query_seg[...], key_seg[...] = segment_terms(segment_ref[...])
        slots = chunked(slot_ref[...], capacity, experts)
        gain_sum = jnp.zeros((1, WIDTH), f32)
        shift_sum = jnp.zeros((1, WIDTH), f32)
        for start in range(0, SEQ_LEN, BLOCK):
            stop = start + BLOCK
            upstream = combine(slots, (first_ref, second_ref), start, BLOCK)
            scaled, inverse = normalize(middle_ref[start:stop])
            result = cot_ref[0, start:stop].astype(f32) + norm_backward(upstream, scaled, inverse, norms[1:2])
            grad_middle[start:stop] = result
            grad_branch[start:stop] = result.astype(bf16)
            turned[:, start:stop] = result.T.astype(bf16)
            gain_sum += jnp.sum(upstream * scaled, axis=0, keepdims=True)
            shift_sum += jnp.sum(upstream, axis=0, keepdims=True)
        sums[1:2] = gain_sum
        sums[3:4] = shift_sum
        grad_context[...] = dot(grad_branch[...], output[...]).astype(bf16)
        rearrange(base, turned, arranged)
        grads = dot(arranged[...], context_ref[...]).astype(bf16)
        for side in range(2):
            part = grads[:, side * HALF : (side + 1) * HALF]
            kept_refs[side][:, TRIPLE : 4 * HALF] = part[:kept_rows]
            sent_refs[side][:, TRIPLE : 4 * HALF] = part[kept_rows:]

    columns = pl.ds(pl.multiple_of(step * PAIR, PAIR), PAIR)
    pair_grad = grad_context[:, columns]
    inner = pair_grad.astype(f32) * context_ref[:, columns].astype(f32)
    query = packed_ref[:, :PAIR]
    keys = packed_ref[:, PAIR : 2 * PAIR]
    keys_wide = jnp.concatenate([keys, key_seg[...]], axis=1)
    lane = iota((SEQ_LEN, PAIR), 1)
    ones = ((lane >= SEGMENTS) & (lane < SEGMENTS + 3)).astype(f32).astype(bf16)
    values_wide = jnp.concatenate([packed_ref[:, 2 * PAIR :], ones], axis=1)
    logs = jnp.concatenate([logsum_ref[0], jnp.zeros((6, SEQ_LEN), f32)], axis=0).T
    for head in range(2):
        first_row = head * SEQ_LEN
        mask = head_mask(head)
        own = query * (mask * HEAD_DIM**-0.5).astype(bf16)
        upstream = pair_grad * mask.astype(bf16)
        queries_pair[first_row : first_row + SEQ_LEN] = own
        upstream_pair[first_row : first_row + SEQ_LEN] = upstream
        keys_pair[first_row : first_row + SEQ_LEN] = keys * mask.astype(bf16)
        delta = jnp.sum(inner * mask, axis=1, keepdims=True)
        own_wide = jnp.concatenate([own, minus(lane, logs[:, head : head + 1], query_seg[...])], axis=1)
        upstream_wide = jnp.concatenate([upstream, minus(lane, delta, jnp.zeros((SEQ_LEN, PAIR), f32))], axis=1)
        for start in range(0, SEQ_LEN, BLOCK):
            stop = start + BLOCK
            column = first_row + start
            for first, last in [(start, stop)] + ([(0, start)] if start else []):
                probs = jnp.exp(dot_nt(keys_wide[first:last], own_wide[start:stop]))
                if first == start:
                    probs = jnp.where(iota(probs.shape, 0) <= iota(probs.shape, 1), probs, 0.0)
                grad_probs = dot_nt(values_wide[first:last], upstream_wide[start:stop])
                all_probs[first:last, column : column + BLOCK] = probs.astype(bf16)
                all_scores[first:last, column : column + BLOCK] = (probs * grad_probs).astype(bf16)
    for start in range(0, SEQ_LEN, BLOCK):
        stop = start + BLOCK
        grad_query, grad_key, grad_value = None, None, None
        for head in range(2):
            first_row = head * SEQ_LEN
            later = slice(first_row + start, first_row + SEQ_LEN)
            column = first_row + start
            part_value = dot(all_probs[start:stop, later], upstream_pair[later])
            part_key = dot(all_scores[start:stop, later], queries_pair[later])
            part_query = dot_tn(all_scores[:stop, column : column + BLOCK], keys_pair[first_row : first_row + stop])
            grad_value = part_value if grad_value is None else grad_value + part_value
            grad_key = part_key if grad_key is None else grad_key + part_key
            grad_query = part_query if grad_query is None else grad_query + part_query
        grad_packed[start:stop, pair_columns(step, 0)] = (grad_query * (HEAD_DIM**-0.5)).astype(bf16)
        grad_packed[start:stop, pair_columns(step, 1)] = grad_key.astype(bf16)
        grad_packed[start:stop, pair_columns(step, 2)] = grad_value.astype(bf16)

    @pl.when(step == pl.num_programs(0) - 1)
    def _():
        load_pairs(base, weight_refs[:4], mixing)
        gain_sum = jnp.zeros((1, WIDTH), f32)
        shift_sum = jnp.zeros((1, WIDTH), f32)
        for start in range(0, SEQ_LEN, BLOCK):
            stop = start + BLOCK
            upstream = dot_nt(grad_packed[start:stop], mixing[...])
            scaled, inverse = normalize(x_ref[0, start:stop].astype(f32))
            result = grad_middle[start:stop] + norm_backward(upstream, scaled, inverse, norms[0:1])
            grad_input_ref[start:stop] = result.astype(bf16)
            normed = scaled * norms[0:1] + norms[2:3]
            turned[:, start:stop] = normed.T.astype(bf16)
            gain_sum += jnp.sum(upstream * scaled, axis=0, keepdims=True)
            shift_sum += jnp.sum(upstream, axis=0, keepdims=True)
        rearrange(base, turned, arranged)
        for side in range(2):
            part = dot(arranged[...], grad_packed[:, side * TRIPLE : (side + 1) * TRIPLE]).astype(bf16)
            kept_refs[side][:, :TRIPLE] = part[:kept_rows]
            sent_refs[side][:, :TRIPLE] = part[kept_rows:]
        sums[0:1] = gain_sum
        sums[2:3] = shift_sum
        sums[4:8] = jnp.zeros((4, WIDTH), f32)
        tall = jnp.concatenate([sums[...], jnp.zeros((PAIR - 8, WIDTH), f32)], axis=0)
        turned[:, :PAIR] = tall.T.astype(bf16)
        rearrange(base, turned.at[:, :PAIR], arranged.at[:, :PAIR])
        kept_refs[0][:, 4 * HALF :] = arranged[:kept_rows, :PAIR]
        sent_refs[0][:, 4 * HALF :] = arranged[kept_rows:, :PAIR]


def backward(scalars, inputs, cotangent, middle, back, slot_col, segment_col, weights, packed, context, logsums, after, experts, capacity):
    pairs = WIDTH // PAIR
    rows = back[0].shape[0]
    one = lambda i, place: (place[0], 0, 0)
    full = whole((SEQ_LEN, WIDTH))
    once = pl.BlockSpec((SEQ_LEN, WIDTH), lambda i, _: (0, 0), **ONCE)
    columns = [4 * HALF + PAIR, 4 * HALF] * 2
    return pl.pallas_call(
        functools.partial(backward_kernel, experts, capacity),
        grid_spec=pltpu.PrefetchScalarGridSpec(
            num_scalar_prefetch=1,
            grid=(pairs,),
            in_specs=[
                pl.BlockSpec((1, SEQ_LEN, WIDTH), one, **ONCE),
                pl.BlockSpec((1, SEQ_LEN, WIDTH), one, **ONCE),
                once,
                *[pl.BlockSpec(b.shape, lambda i, _: (0, 0), **ONCE) for b in back],
                whole((SEQ_LEN, 1)),
                whole((SEQ_LEN, 1)),
                *weight_specs(),
                pl.BlockSpec((SEQ_LEN, 3 * PAIR), lambda i, _: (0, i)),
                once,
                pl.BlockSpec((1, 2, SEQ_LEN), lambda i, _: (i, 0, 0)),
                ANY,
            ],
            out_specs=[
                *[pl.BlockSpec((HALF, c), lambda i, _: (0, 0), **ONCE) for c in columns],
                pl.BlockSpec((SEQ_LEN, WIDTH), lambda i, _: (0, 0), **ONCE),
            ],
            scratch_shapes=[
                pltpu.VMEM((SEQ_LEN, WIDTH), f32),
                pltpu.VMEM((SEQ_LEN, WIDTH), bf16),
                pltpu.VMEM((WIDTH, SEQ_LEN), bf16),
                pltpu.VMEM((WIDTH, SEQ_LEN), bf16),
                pltpu.VMEM((SEQ_LEN, WIDTH), bf16),
                pltpu.VMEM((SEQ_LEN, PAIR), bf16),
                pltpu.VMEM((SEQ_LEN, PAIR), bf16),
                pltpu.VMEM((8, WIDTH), f32),
                pltpu.VMEM((SEQ_LEN, 2 * SEQ_LEN), bf16),
                pltpu.VMEM((SEQ_LEN, 2 * SEQ_LEN), bf16),
                pltpu.VMEM((2 * SEQ_LEN, PAIR), bf16),
                pltpu.VMEM((2 * SEQ_LEN, PAIR), bf16),
                pltpu.VMEM((2 * SEQ_LEN, PAIR), bf16),
                pltpu.VMEM((SEQ_LEN, 3 * WIDTH), bf16),
                pltpu.VMEM((WIDTH, 3 * WIDTH), bf16),
                pltpu.VMEM((WIDTH, WIDTH), bf16),
                pltpu.VMEM((WIDTH, PAIR), bf16),
                pltpu.VMEM((8, WIDTH), f32),
            ],
        ),
        out_shape=[
            *[jax.ShapeDtypeStruct((HALF, c), bf16) for c in columns],
            jax.ShapeDtypeStruct((SEQ_LEN, WIDTH), bf16),
        ],
        compiler_params=params(),
        cost_estimate=cost(50),
        name="attention_backward",
    )(
        scalars,
        inputs,
        cotangent,
        middle,
        *back,
        slot_col,
        segment_col,
        *weight_arrays(weights),
        packed,
        context,
        logsums,
        after,
    )


def result_kernel(middle_ref, slot_ref, back_ref, out_ref):
    routed = combine(slot_ref[...], (back_ref,), 0, BLOCK)
    out_ref[...] = (middle_ref[...] + routed).astype(bf16)


def result(middle, slot_col, back):
    rows = back.shape[0]
    tile = pl.BlockSpec((BLOCK, WIDTH), lambda i: (i, 0))
    return pl.pallas_call(
        result_kernel,
        grid=(SEQ_LEN // BLOCK,),
        in_specs=[
            tile,
            pl.BlockSpec((BLOCK, 1), lambda i: (i, 0)),
            whole((rows, WIDTH)),
        ],
        out_specs=tile,
        out_shape=jax.ShapeDtypeStruct((SEQ_LEN, WIDTH), bf16),
        compiler_params=params(),
        cost_estimate=cost(8),
        name="result",
    )(middle, slot_col, back)


def swap(values):
    return lax.ppermute(values, "tensor", [(0, 1), (1, 0)])


def exchange(values, experts):
    shape = values.shape
    parts = values.reshape(experts, shape[0] // experts, shape[1])
    return lax.all_to_all(parts, "dp", split_axis=0, concat_axis=0, tiled=True).reshape(shape)


def both(place, values, other):
    first = place == 0
    return jnp.stack([jnp.where(first, values, other), jnp.where(first, other, values)])


def both_at_once(place, values, other):
    mine = lax.broadcasted_iota(jnp.int32, (2, 1, 1), 0) == place
    return jnp.where(mine, values[None], other[None])


def flip(values, bit):
    size = lax.axis_size("dp")
    return lax.ppermute(values, "dp", [(i, i ^ bit) for i in range(size)])


def after(values, *others):
    return lax.optimization_barrier((values, *others))[0]


def rows_of(parts):
    return jnp.concatenate(parts, axis=0)


def fetch_by_halves(shard):
    own = shard
    for bit in (8, 4):
        own = rows_of([own, flip(own, bit)])
    middle = own.shape[0] // 2
    first, second = own[:middle], own[middle:]
    first_peer, second_next = swap(first), flip(second, 2)
    first_next = flip(rows_of([first, first_peer]), 2)
    second_peer = swap(rows_of([second, second_next]))
    near = rows_of([first, first_next[:middle], second, second_next])
    near_peer = rows_of([first_peer, first_next[middle:], second_peer])
    return near, flip(near, 1), near_peer, flip(near_peer, 1)


def fetch_whole(shard):
    own = lax.all_gather(rows_of([shard, swap(shard)]), "dp", axis=0, tiled=True)
    own = own.reshape(-1, 2, shard.shape[0], shard.shape[1]).transpose(1, 0, 2, 3).reshape(2, -1, SLAB, shard.shape[1])
    return tuple(rows_of([own[side, o ^ far] for o in OFFSETS]) for side in (0, 1) for far in (0, 1))


def pool_by_halves(kept, sent, peer, output, grad_peer):
    size = lax.axis_size("dp")
    groups = [[high * 4 + low for high in range(size // 4)] for low in range(4)]
    totals = [None, None]
    for side in (1, 0):
        near = (kept[side].astype(f32) + after(flip(sent[side], 1), peer).astype(f32)).astype(bf16)
        middle = near.shape[0] // 2
        near = (near[:middle].astype(f32) + after(flip(near[middle:], 2), *([] if side else [grad_peer])).astype(f32)).astype(bf16)
        parts = after(near, output).reshape(size // 4, SLAB, -1)
        parts = lax.all_to_all(parts, "dp", split_axis=0, concat_axis=0, tiled=True, axis_index_groups=groups)
        totals[side] = jnp.sum(parts.astype(f32), axis=0)
    return totals


def pool_whole(kept, sent):
    totals = []
    for side in range(2):
        full = jnp.concatenate([kept[side], sent[side]], axis=0)
        full = full.reshape(2, 2, 4, SLAB, -1).transpose(2, 1, 0, 3, 4).reshape(WIDTH, -1)
        totals.append(lax.psum_scatter(full, "dp", scatter_dimension=0, tiled=True).astype(f32))
    return totals


def body(
    inputs,
    qkv_weight,
    out_weight,
    norm_gains,
    norm_shifts,
    expert_in,
    expert_out,
    token_ids,
    hash_table,
    segment_ids,
    cotangent,
):
    place = lax.axis_index("tensor")
    experts = lax.axis_size("dp")
    by_halves = experts * SLAB == WIDTH
    base = lax.axis_index("dp") if by_halves else jnp.zeros((), jnp.int32)
    places = jnp.stack([place, base]).astype(jnp.int32)
    capacity = 2 * SEQ_LEN // experts
    depth = qkv_weight.shape[0]
    half = qkv_weight.shape[2]

    norms = jnp.concatenate([norm_gains, norm_shifts], axis=0).T
    norms = jnp.pad(norms, ((0, 0), (0, PAIR - norms.shape[1])))
    shard = jnp.concatenate([qkv_weight.reshape(depth, 3 * half), out_weight, norms], axis=1)
    weights = fetch_by_halves(shard) if by_halves else fetch_whole(shard)

    in_own, out_own = expert_in[0], expert_out[0]
    out_other = swap(after(out_own, weights[2]))
    in_other = swap(after(in_own, weights[2]))

    ids = lax.dynamic_index_in_dim(token_ids, place, 0, keepdims=False)
    chosen = jnp.take(hash_table, ids, axis=0)
    segment_col = lax.dynamic_index_in_dim(segment_ids, place, 0, keepdims=False).reshape(SEQ_LEN, 1)
    sent, slot_row, slot_col = route(places, chosen, cotangent, experts, capacity)
    grads = exchange(sent, experts)

    packed, context, logsums, middle, first, second = forward(
        places, inputs, weights, segment_col, slot_row, slot_col, experts, capacity
    )
    upstream = grad_hidden(grads, [out_own, out_other], first)
    second, upstream = lax.optimization_barrier((second, upstream))
    arrived = [exchange(first, experts), exchange(second, experts)]
    upstream = upstream.reshape(experts, capacity, -1)
    grads = grads.reshape(experts, capacity, WIDTH)
    done = [expert(a, upstream, in_own, in_other, c) for c, a in enumerate(arrived)]
    hidden = [d[0] for d in done]
    pre = [d[1] for d in done]
    sent = expert_grads(arrived, grads, [h[1] for h in hidden], [p[1] for p in pre], in_own.shape[1])
    back = [exchange(done[0][2], experts), exchange(after(done[1][2], sent), experts)]
    peer = swap(sent)
    routed_send = expert_result(hidden, out_own, out_other, sent, experts)
    routed = exchange(routed_send.reshape(experts * capacity, WIDTH), experts)

    kept_own, kept_other, sent_own, sent_other, grad_own = backward(
        places, inputs, cotangent, middle, back, slot_col, segment_col, weights, packed, context, logsums,
        routed_send, experts, capacity
    )
    kept, sent_rows = (kept_own, kept_other), (sent_own, sent_other)
    output = result(middle, slot_col, routed)
    grad_peer, output_peer = swap(grad_own), swap(output)
    if by_halves:
        pooled, pooled_peer = pool_by_halves(kept, sent_rows, peer, output, grad_peer)
    else:
        pooled, pooled_peer = pool_whole(kept, sent_rows)
    shared = jnp.concatenate([pooled_peer, pooled[:, 4 * half :]], axis=1).astype(bf16)
    owned = pooled + swap(after(shared, output_peer)).astype(f32)
    grad_qkv = owned[:, : 3 * half].reshape(depth, 3, half)
    grad_out = owned[:, 3 * half : 4 * half]
    grad_norm = owned[:, 4 * half : 4 * half + 4].T
    grad_expert_in, grad_expert_out = expert_grads(
        arrived, grads, [h[0] for h in hidden], [p[0] for p in pre], in_own.shape[1], peer
    )

    return (
        both_at_once(place, output, output_peer),
        both(place, grad_own, grad_peer),
        grad_qkv,
        grad_out,
        grad_norm[:2],
        grad_norm[2:],
        grad_expert_in[None],
        grad_expert_out[None],
    )


def solution(mesh):
    return jax.shard_map(
        body,
        mesh=mesh,
        in_specs=(
            P("dp", None, None),
            P("dp", None, "tensor"),
            P("dp", "tensor"),
            P(None, "dp"),
            P(None, "dp"),
            P("dp", None, "tensor"),
            P("dp", "tensor", None),
            P("dp", None),
            P(),
            P("dp", None),
            P("dp", None, None),
        ),
        out_specs=(
            P("dp", None, None),
            P("dp", None, None),
            P("dp", None, "tensor"),
            P("dp", "tensor"),
            P(None, "dp"),
            P(None, "dp"),
            P("dp", None, "tensor"),
            P("dp", "tensor", None),
        ),
        check_vma=False,
    )
```
